32 devices in a mesh: tile: 8 (over z, y), slab: 4 (over x, core).
Axes of the slice: x: 2, y: 2, z: 4, core: 2. Of those that a mesh axis runs over, the one named last changes fastest.
Arguments:
- voxel_cell: int32 [12288, 128], P(('tile', 'slab')), may hold values from 0 to 255
- offsets: float32 [12288, 2, 128], P(('tile', 'slab')), may hold values from 0 to 1
- line_center: float32 [12288, 128], P(('tile', 'slab')), may hold values from 0 to 128
- line_width: float32 [12288, 128], P(('tile', 'slab')), may hold values from 1 to 12
- luminosity: float32 [12288, 128], P(('tile', 'slab')), may hold values from 0.3 to 8
- block_rows: int32 [12288], P(('tile', 'slab')), may hold values from 1 to 128, as said below
- block_chan: int32 [12288], P(('tile', 'slab')), may hold values from 0 to 31, as said below
- slot_table: int32 [32, 768], P(('tile', 'slab')), may hold values from -1 to 383, as said below
- beam_width: float32 [4096], P('slab'), may hold values from 0.6 to 3
- spectral_taps: float32 [31], replicated, may hold values from -3 to 3
Outputs:
- sky_cube: float32 [8, 256, 4096], P('tile', None, 'slab')
The draws below stay inside these ranges and needn't reach their ends.
Inputs may be any that keep to these rules, and one draw needn't show every extreme that they name: `slot_table`: row i lists the blocks of device i: entry j belongs to destination device j // 24, that is field j // 24 // 4 and slab j // 24 % 4, and holds a local block index or -1 for an empty slot. Every local block stands in exactly one entry of its row. In every draw some destination receives 24 blocks from every device. `block_chan`: A block listed for a destination of slab s has its channel block in s * 8 .. (s + 1) * 8 - 1. Rows 0 .. block_rows - 1 of a block are emitters, the others padding.
All inputs are finite; a program needn't handle non-finite values.
Results may differ from the reference program's by a relative error of at most 0.0045.
Values sent between devices are 32-bit elements; how exact they have to be, the bound alone decides.
No kernel may reach another device: no remote copies, remote signals or barrier semaphores. Data moves between devices by JAX's collectives and lax.ppermute only.
A program may use at most 64 MiB of HBM per device.

```python
import math
import jax
import jax.numpy as jnp
from jax import lax

SIDE = 16
CH = 4096
CB = 128
ROWS = 128
TAPS = 31
BLK_DEV = 384
HALF = 15
NCB = 32
BLOCKS = 12288
CAP = 24
N_TILE = 8
N_SLAB = 4


def routing_tables(key):
    device_count = N_TILE * N_SLAB
    slot_count = device_count * CAP
    blocks_share = NCB // N_SLAB
    level_key, hot_key = jax.random.split(key)
    levels = jax.random.randint(level_key, (device_count,), 0, 3)
    hot_dest = jax.random.randint(hot_key, (), 0, device_count)
    levels = jnp.where(jnp.arange(device_count) == hot_dest, 8, levels)
    slot_level = jnp.repeat(levels, CAP)
    slot_ids = jnp.arange(slot_count)

    def one_source(source):
        source_key = jax.random.fold_in(key, source + 1000)
        jitter_key, order_key, chan_key = jax.random.split(source_key, 3)
        jitter = jax.random.randint(jitter_key, (slot_count,), 0, 1024)
        scores = ((slot_level * 1024 + jitter) * slot_count + slot_ids).astype(jnp.int32)
        chosen = lax.top_k(scores, BLK_DEV)[1]
        block_order = jax.random.permutation(order_key, BLK_DEV).astype(jnp.int32)
        slot_row = jnp.full((slot_count,), -1, jnp.int32).at[chosen].set(block_order)
        dest_slab = chosen // CAP % N_SLAB
        chan_vals = dest_slab * blocks_share + jax.random.randint(chan_key, (BLK_DEV,), 0, blocks_share)
        chan_row = jnp.zeros((BLK_DEV,), jnp.int32).at[block_order].set(chan_vals.astype(jnp.int32))
        return (slot_row, chan_row)
    tables, chan_rows = jax.vmap(one_source)(jnp.arange(device_count))
    return (tables, chan_rows.reshape(-1))


def draw_slot_table(key, part):
    return routing_tables(jax.random.fold_in(key, 17))[0]


def draw_block_chan(key, part):
    return routing_tables(jax.random.fold_in(key, 17))[1]


def draw_block_rows(key, part):
    first_key, second_key = jax.random.split(jax.random.fold_in(key, 29))
    counts = jax.random.randint(first_key, (BLOCKS,), 1, ROWS + 1)
    full_block = jax.random.randint(second_key, (), 0, BLOCKS)
    return jnp.where(jnp.arange(BLOCKS) == full_block, ROWS, counts).astype(jnp.int32)


def with_ends(values, own_key, smallest, largest):
    longest = values.shape.index(max(values.shape))
    spots = []
    for shift in (0, 1):
        where = [jax.random.randint(jax.random.fold_in(own_key, axis), (), 0, length) for axis, length in enumerate(values.shape)]
        where[longest] = (where[longest] + shift) % values.shape[longest]
        spots.append(tuple(where))
    return values.at[spots[0]].set(smallest).at[spots[1]].set(largest)


def block_levels(stream_key, extent, shards, least, high):
    gain, own = 1.0, jax.random.fold_in(stream_key, 6)
    for position, shards_of in shards:
        heights = jnp.exp(jax.random.uniform(jax.random.fold_in(own, position), (shards_of,), jnp.float32, least / len(shards), high / len(shards)))
        gain = gain * jnp.repeat(heights, extent[position] // shards_of).reshape([-1 if axis == position else 1 for axis in range(len(extent))])
    return gain


def normal_values(own_key, dims, spread, most, dtype=jnp.bfloat16):
    return jnp.clip(spread * jax.random.normal(own_key, dims, jnp.float32), -most, most).astype(dtype)


def setup_inputs(seed: int = 0) -> dict:
    splits = jax.random.split(jax.random.key(seed), 11)
    return {
        "voxel_cell": with_ends(jax.random.randint(splits[0], (BLOCKS, ROWS), 0, SIDE * SIDE), jax.random.fold_in(splits[0], 1), 0, (SIDE * SIDE) - 1).astype(jnp.int32),
        "offsets": jnp.clip(1.0 * jax.random.uniform(splits[1], (BLOCKS, 2, ROWS), jnp.float32) ** block_levels(splits[1], (BLOCKS, 2, ROWS), ((0, 32),), -0.2, 0.2), 0.0, 1.0),
        "line_center": jnp.clip(128.0 * jax.random.uniform(splits[2], (BLOCKS, ROWS), jnp.float32) ** block_levels(splits[2], (BLOCKS, ROWS), ((0, 32),), -0.2, 0.2), 0.0, 128.0),
        "line_width": jnp.clip(jnp.exp(math.log(12.0) - 2.4849066 * jax.random.uniform(splits[3], (BLOCKS, ROWS), jnp.float32) ** block_levels(splits[3], (BLOCKS, ROWS), ((0, 32),), -0.2, 0.2)), 1.0, 12.0),
        "luminosity": jnp.clip(jnp.exp(math.log(8.0) - 3.2834143 * jax.random.uniform(splits[4], (BLOCKS, ROWS), jnp.float32) ** block_levels(splits[4], (BLOCKS, ROWS), ((0, 32),), -0.2, 0.2)), 0.3, 8.0),
        "block_rows": draw_block_rows(jax.random.fold_in(splits[10], 71), 0),
        "block_chan": draw_block_chan(jax.random.fold_in(splits[10], 71), 0),
        "slot_table": draw_slot_table(jax.random.fold_in(splits[10], 71), 0),
        "beam_width": jnp.clip(jnp.exp(math.log(3.0) - 1.60943787 * jax.random.uniform(splits[8], (CH,), jnp.float32) ** block_levels(splits[8], (CH,), ((0, 4),), -0.2, 0.2)), 0.6, 3.0),
        "spectral_taps": normal_values(splits[9], (TAPS,), 0.35, 3.0, jnp.float32),
    }


def line_weights(centers, widths, bright):
    channel_pos = lax.broadcasted_iota(jnp.float32, (1, 1, CB), 2) + 0.5
    profile = jnp.exp(-jnp.square(channel_pos - centers[:, :, None]) / (2.0 * jnp.square(widths[:, :, None])))
    totals = jnp.sum(profile, axis=2, keepdims=True)
    return (bright[:, :, None] * profile / totals).astype(jnp.bfloat16)


def beam_kernel(widths):
    places = lax.broadcasted_iota(jnp.float32, (SIDE, SIDE, 1), 0)
    others = lax.broadcasted_iota(jnp.float32, (SIDE, SIDE, 1), 1)
    kernel = jnp.exp(-jnp.square(places - others) / (2.0 * jnp.square(widths)[None, None, :]))
    return kernel / jnp.sum(kernel, axis=1, keepdims=True)


def reference(voxel_cell, offsets, line_center, line_width, luminosity, block_rows, block_chan, slot_table, beam_width, spectral_taps):
    device_count = N_TILE * N_SLAB
    block_total = voxel_cell.shape[0]
    per_device = block_total // device_count
    slot_total = slot_table.shape[1]
    per_dest = slot_total // device_count
    sources = lax.broadcasted_iota(jnp.int32, slot_table.shape, 0)
    slot_pos = lax.broadcasted_iota(jnp.int32, slot_table.shape, 1)
    global_block = jnp.where(slot_table >= 0, sources * per_device + slot_table, block_total).astype(jnp.int32)
    dest_values = (slot_pos // per_dest // N_SLAB).astype(jnp.int32)
    dest_tile = jnp.zeros((block_total + 1,), jnp.int32).at[global_block.reshape(-1)].set(dest_values.reshape(-1))[:block_total]
    segments = N_TILE * SIDE * SIDE * NCB
    span_size = math.gcd(block_total, 512)
    turn_count = block_total // span_size
    stacked = (voxel_cell.reshape(turn_count, span_size, ROWS), offsets.reshape(turn_count, span_size, 2, ROWS), line_center.reshape(turn_count, span_size, ROWS), line_width.reshape(turn_count, span_size, ROWS), luminosity.reshape(turn_count, span_size, ROWS), block_rows.reshape(turn_count, span_size), block_chan.reshape(turn_count, span_size), dest_tile.reshape(turn_count, span_size))

    def add_span(cube_sum, pieces):
        cell_ids, offset_rows, centers, widths, lumens, counts, chan_ids, tile_ids = pieces
        live_rows = lax.broadcasted_iota(jnp.int32, cell_ids.shape, 1) < counts[:, None]
        rounded = lax.optimization_barrier(lumens.astype(jnp.bfloat16)).astype(jnp.float32)
        bright = jnp.where(live_rows, rounded, jnp.float32(0.0))
        line_rows = line_weights(centers, widths, bright).astype(jnp.float32).reshape(-1, CB)
        cell_x = cell_ids // SIDE
        cell_y = cell_ids % SIDE
        frac_x = offset_rows[:, 0]
        frac_y = offset_rows[:, 1]
        for step_x in (0, 1):
            for step_y in (0, 1):
                weight_x = frac_x if step_x else 1.0 - frac_x
                weight_y = frac_y if step_y else 1.0 - frac_y
                weight = lax.optimization_barrier((weight_x * weight_y).astype(jnp.bfloat16)).astype(jnp.float32)
                target_x = cell_x + step_x
                target_y = cell_y + step_y
                inside = (target_x < SIDE) & (target_y < SIDE)
                target_ids = jnp.where(inside, (tile_ids[:, None] * (SIDE * SIDE) + target_x * SIDE + target_y) * NCB + chan_ids[:, None], segments).astype(jnp.int32)
                cube_sum = cube_sum.at[target_ids.reshape(-1)].add(weight.reshape(-1, 1) * line_rows)
        return cube_sum, None

    cube_sum = lax.scan(add_span, jnp.zeros((segments + 1, CB), jnp.float32), stacked)[0]
    binned = cube_sum[:segments].reshape(N_TILE, SIDE, SIDE, CH)
    kernel = beam_kernel(beam_width)
    along_x = jnp.einsum("xac,tayc->txyc", kernel, binned, precision=lax.Precision.HIGHEST)
    beamed = jnp.einsum("ybc,txbc->txyc", kernel, along_x, precision=lax.Precision.HIGHEST)
    padded = jnp.pad(beamed, ((0, 0), (0, 0), (0, 0), (HALF, HALF)))
    result = jnp.zeros_like(beamed)
    for tap_index in range(TAPS):
        result = result + spectral_taps[tap_index] * padded[:, :, :, tap_index:tap_index + CH]
    return result.reshape(N_TILE, SIDE * SIDE, CH)
```

```python
import functools
import math

import jax
import jax.numpy as jnp
from jax import lax
from jax.experimental import pallas as pl
from jax.experimental.pallas import tpu as pltpu
from jax.sharding import PartitionSpec as P

SIDE = 16
PIX = SIDE * SIDE
CB = 128
ROWS = 128
TAPS = 31
HALF = 15
EDGE = 16
NCB = 32
FIELDS = 6
LOG2E = math.log2(math.e)


def chunk_sizes(per_dest):
    count = 3 if per_dest % 3 == 0 else 1
    return [per_dest // count] * count


def padded_rows(rows):
    return -(-rows // 8) * 8


def pack_kernel(sizes, slab_count, share, slot_ref, count_ref, chan_ref, cell_ref, offset_ref, center_ref,
                width_ref, lum_ref, *refs):
    outs, (cell_f, decay, rounded) = refs[: len(sizes)], refs[len(sizes) :]
    dest_count = outs[0].shape[0]
    per_dest = sum(sizes)
    cell_f[...] = cell_ref[...].astype(jnp.float32)
    decay[...] = (-0.5 * LOG2E) / jnp.square(width_ref[...])
    rounded[...] = lum_ref[...].astype(jnp.bfloat16).astype(jnp.float32)
    lane = lax.broadcasted_iota(jnp.int32, (1, ROWS), 1)

    def one_dest(dest, carry):
        first_chan = lax.rem(dest, slab_count) * share
        chan_row = jnp.zeros((1, ROWS), jnp.int32)
        count_row = jnp.zeros((1, ROWS), jnp.int32)
        slot = 0
        for out, size in zip(outs, sizes):
            for place in range(size):
                block = slot_ref[0, dest * per_dest + slot]
                filled = block >= 0
                block = jnp.maximum(block, 0)
                live = jnp.where(filled, count_ref[block], 0)
                chan = jnp.where(filled, chan_ref[block] - first_chan, 0)
                chan_row = jnp.where(lane == slot, chan, chan_row)
                count_row = jnp.where(lane == slot, live, count_row)
                row = place * FIELDS
                here = pl.ds(block, 1)
                out[dest, row : row + 1, :] = cell_f[here, :]
                out[dest, row + 1 : row + 3, :] = offset_ref[pl.ds(2 * block, 2), :]
                out[dest, row + 3 : row + 4, :] = center_ref[here, :]
                out[dest, row + 4 : row + 5, :] = decay[here, :]
                out[dest, row + 5 : row + 6, :] = jnp.where(lane < live, rounded[here, :], 0.0)
                slot += 1
        meta = sizes[0] * FIELDS
        outs[0][dest, meta : meta + 1, :] = chan_row.astype(jnp.float32)
        outs[0][dest, meta + 1 : meta + 2, :] = count_row.astype(jnp.float32)
        return carry

    lax.fori_loop(0, dest_count, one_dest, 0)


def pack(sizes, dest_count, slab_count, share, slot_list, counts, chans, cells, offsets, centers, widths, lums):
    rows = [size * FIELDS for size in sizes]
    rows[0] += 2
    block_total = cells.shape[0]
    smem = pl.BlockSpec(memory_space=pltpu.SMEM)
    vmem = pl.BlockSpec(memory_space=pltpu.VMEM)
    return pl.pallas_call(
        functools.partial(pack_kernel, sizes, slab_count, share),
        out_shape=[jax.ShapeDtypeStruct((dest_count, padded_rows(r), ROWS), jnp.float32) for r in rows],
        in_specs=[smem] * 3 + [vmem] * 5,
        out_specs=[vmem] * len(sizes),
        scratch_shapes=[pltpu.VMEM((block_total, ROWS), jnp.float32)] * 3,
        name="pack",
    )(slot_list, counts, chans, cells, offsets.reshape(block_total * 2, ROWS), centers, widths, lums)


def deposit_kernel(size, first, chan_ref, got_ref, *refs):
    acc = refs[-1]
    if first == 0:
        acc[...] = jnp.zeros_like(acc)
    else:
        acc[...] = refs[0][...]
    source_count = got_ref.shape[0]
    place16 = lax.broadcasted_iota(jnp.int32, (SIDE, ROWS), 0).astype(jnp.float32)
    chan_pos = lax.broadcasted_iota(jnp.int32, (CB, ROWS), 0).astype(jnp.float32) + 0.5

    def hat(cell, frac):
        apart = place16 - cell
        return jnp.where(apart == 0.0, 1.0 - frac, jnp.where(apart == 1.0, frac, 0.0))

    def one_source(source, carry):
        for place in range(size):
            row = place * FIELDS
            cell, frac_x, frac_y, center, decay, bright = (
                got_ref[source, row + field : row + field + 1, :] for field in range(FIELDS)
            )
            cell_x = jnp.floor(cell * (1.0 / SIDE))
            weight_x = hat(cell_x, frac_x)
            weight_y = hat(cell - SIDE * cell_x, frac_y)
            spread = jnp.concatenate(
                [(weight_x[x : x + 1, :] * weight_y).astype(jnp.bfloat16) for x in range(SIDE)], axis=0
            )
            profile = jnp.exp2(jnp.square(chan_pos - center) * decay)
            scale = bright / jnp.sum(profile, axis=0, keepdims=True)
            line = (profile * scale).astype(jnp.bfloat16)
            part = lax.dot_general(
                spread, line, (((1,), (1,)), ((), ())), preferred_element_type=jnp.float32
            )
            chan = chan_ref[source, first + place]
            acc[chan] += part
        return carry

    lax.fori_loop(0, source_count, one_source, 0)


def deposit(size, first, share, chans, got, *held):
    smem = pl.BlockSpec(memory_space=pltpu.SMEM)
    vmem = pl.BlockSpec(memory_space=pltpu.VMEM)
    work = got.shape[0] * size
    return pl.pallas_call(
        functools.partial(deposit_kernel, size, first),
        out_shape=jax.ShapeDtypeStruct((share, PIX, CB), jnp.float32),
        in_specs=[smem, vmem] + [vmem] * len(held),
        out_specs=vmem,
        input_output_aliases={2: 0} if held else {},
        cost_estimate=pl.CostEstimate(
            flops=work * 2 * PIX * CB * ROWS, transcendentals=work * CB * ROWS, bytes_accessed=got.size * 4
        ),
        name="deposit",
    )(chans, got, *held)


def smooth_kernel(acc_ref, width_ref, out_ref):
    decay = (-0.5 * LOG2E) / jnp.square(width_ref[...])
    places = lax.broadcasted_iota(jnp.int32, (SIDE, CB), 0).astype(jnp.float32)
    beam = [jnp.exp2(jnp.square(places - float(v)) * decay) for v in range(SIDE)]
    norm = beam[0]
    for v in range(1, SIDE):
        norm = norm + beam[v]
    inverse = 1.0 / norm
    beam = [b * inverse for b in beam]
    along_x = [None] * SIDE
    for v in range(SIDE):
        plane = acc_ref[0, v * SIDE : (v + 1) * SIDE, :]
        for x in range(SIDE):
            term = beam[v][x : x + 1, :] * plane
            along_x[x] = term if v == 0 else along_x[x] + term
    for x in range(SIDE):
        total = None
        for v in range(SIDE):
            term = beam[v] * along_x[x][v : v + 1, :]
            total = term if v == 0 else total + term
        out_ref[x * SIDE : (x + 1) * SIDE, :] = total


def smooth(acc, widths):
    share = acc.shape[0]
    return pl.pallas_call(
        smooth_kernel,
        out_shape=jax.ShapeDtypeStruct((PIX, share * CB), jnp.float32),
        grid=(share,),
        in_specs=[
            pl.BlockSpec((1, PIX, CB), lambda i: (i, 0, 0)),
            pl.BlockSpec((1, CB), lambda i: (0, i)),
        ],
        out_specs=pl.BlockSpec((PIX, CB), lambda i: (0, i)),
        name="smooth",
    )(acc, widths.reshape(1, -1))


def taps_kernel(taps_ref, cube_ref, before_ref, after_ref, out_ref):
    span = 3 * CB
    apart = lax.broadcasted_iota(jnp.int32, (span, CB), 0) - lax.broadcasted_iota(jnp.int32, (span, CB), 1)
    band = jnp.zeros((span, CB), jnp.float32)
    for k in range(TAPS):
        band = jnp.where(apart == CB - HALF + k, taps_ref[k], band)
    count = cube_ref.shape[1] // CB

    def times(left, right):
        return jnp.dot(left, right, precision=lax.Precision.HIGHEST, preferred_element_type=jnp.float32)

    for i in range(count):
        low, high = max(i - 1, 0), min(i + 2, count)
        total = times(cube_ref[:, low * CB : high * CB], band[(low - i + 1) * CB : (high - i + 1) * CB])
        if i == 0:
            total = total + times(before_ref[...], band[CB - EDGE : CB])
        if i == count - 1:
            total = total + times(after_ref[...], band[2 * CB : 2 * CB + EDGE])
        out_ref[:, i * CB : (i + 1) * CB] = total


def sum_taps(taps, cube, before, after):
    smem = pl.BlockSpec(memory_space=pltpu.SMEM)
    vmem = pl.BlockSpec(memory_space=pltpu.VMEM)
    return pl.pallas_call(
        taps_kernel,
        out_shape=jax.ShapeDtypeStruct(cube.shape, jnp.float32),
        in_specs=[smem, vmem, vmem, vmem],
        out_specs=vmem,
        name="taps",
    )(taps, cube, before, after)


def body(
    voxel_cell,
    offsets,
    line_center,
    line_width,
    luminosity,
    block_rows,
    block_chan,
    slot_table,
    beam_width,
    spectral_taps,
):
    slab_count = lax.axis_size("slab")
    dest_count = lax.axis_size("tile") * slab_count
    per_dest = slot_table.shape[1] // dest_count
    share = NCB // slab_count
    sizes = chunk_sizes(per_dest)
    sent = pack(
        sizes, dest_count, slab_count, share, slot_table, block_rows, block_chan,
        voxel_cell, offsets, line_center, line_width, luminosity,
    )
    got = [
        lax.all_to_all(piece, ("tile", "slab"), split_axis=0, concat_axis=0, tiled=True) for piece in sent
    ]
    chans = got[0][:, sizes[0] * FIELDS, :per_dest].astype(jnp.int32)
    held = ()
    first = 0
    for size, piece in zip(sizes, got):
        held = (deposit(size, first, share, chans, piece, *held),)
        first += size
    cube = smooth(held[0], beam_width)
    ends = slab_count - 1
    before = lax.ppermute(cube[:, -EDGE:], "slab", [(i, i + 1) for i in range(ends)])
    after = lax.ppermute(cube[:, :EDGE], "slab", [(i + 1, i) for i in range(ends)])
    return sum_taps(spectral_taps, cube, before, after)[None]


def solution(mesh):
    placed = (
        P(("tile", "slab"), None),
        P(("tile", "slab"), None, None),
        P(("tile", "slab"), None),
        P(("tile", "slab"), None),
        P(("tile", "slab"), None),
        P(("tile", "slab")),
        P(("tile", "slab")),
        P(("tile", "slab"), None),
        P("slab"),
        P(),
    )
    return jax.shard_map(
        body, mesh=mesh, in_specs=placed, out_specs=P("tile", None, "slab"), check_vma=False
    )
```

```python
import functools
import math

import jax
import jax.numpy as jnp
from jax import lax
from jax.experimental import pallas as pl
from jax.experimental.pallas import tpu as pltpu
from jax.sharding import PartitionSpec as P

SIDE = 16
PIX = SIDE * SIDE
CB = 128
ROWS = 128
TAPS = 31
HALF = 15
EDGE = 16
NCB = 32
FIELDS = 6
UNROLL = 6
LOG2E = math.log2(math.e)


def chunk_sizes(per_dest):
    late = per_dest // 3
    return [per_dest - late, late]


def padded_rows(rows):
    return -(-rows // 8) * 8


def pack_kernel(sizes, slab_count, share, slot_ref, count_ref, chan_ref, cell_ref, offset_ref, center_ref,
                width_ref, lum_ref, *refs):
    outs, (cell_f, decay, rounded) = refs[: len(sizes)], refs[len(sizes) :]
    dest_count = outs[0].shape[0]
    per_dest = sum(sizes)
    cell_f[...] = cell_ref[...].astype(jnp.float32)
    decay[...] = (-0.5 * LOG2E) / jnp.square(width_ref[...])
    rounded[...] = lum_ref[...].astype(jnp.bfloat16).astype(jnp.float32)
    lane = lax.broadcasted_iota(jnp.int32, (1, ROWS), 1)

    def one_dest(dest, carry):
        first_chan = lax.rem(dest, slab_count) * share
        chan_row = jnp.zeros((1, ROWS), jnp.int32)
        count_row = jnp.zeros((1, ROWS), jnp.int32)
        slot = 0
        for out, size in zip(outs, sizes):
            for place in range(size):
                block = slot_ref[0, dest * per_dest + slot]
                filled = block >= 0
                block = jnp.maximum(block, 0)
                live = jnp.where(filled, count_ref[block], 0)
                chan = jnp.where(filled, chan_ref[block] - first_chan, 0)
                chan_row = jnp.where(lane == slot, chan, chan_row)
                count_row = jnp.where(lane == slot, live, count_row)
                row = place * FIELDS
                here = pl.ds(block, 1)
                out[dest, row : row + 1, :] = cell_f[here, :]
                out[dest, row + 1 : row + 3, :] = offset_ref[pl.ds(2 * block, 2), :]
                out[dest, row + 3 : row + 4, :] = center_ref[here, :]
                out[dest, row + 4 : row + 5, :] = decay[here, :]
                out[dest, row + 5 : row + 6, :] = jnp.where(lane < live, rounded[here, :], 0.0)
                slot += 1
        meta = sizes[0] * FIELDS
        outs[0][dest, meta : meta + 1, :] = chan_row.astype(jnp.float32)
        outs[0][dest, meta + 1 : meta + 2, :] = count_row.astype(jnp.float32)
        return carry

    lax.fori_loop(0, dest_count, one_dest, 0)


def pack(sizes, dest_count, slab_count, share, slot_list, counts, chans, cells, offsets, centers, widths, lums):
    rows = [size * FIELDS for size in sizes]
    rows[0] += 2
    block_total = cells.shape[0]
    smem = pl.BlockSpec(memory_space=pltpu.SMEM)
    vmem = pl.BlockSpec(memory_space=pltpu.VMEM)
    return pl.pallas_call(
        functools.partial(pack_kernel, sizes, slab_count, share),
        out_shape=[jax.ShapeDtypeStruct((dest_count, padded_rows(r), ROWS), jnp.float32) for r in rows],
        in_specs=[smem] * 3 + [vmem] * 5,
        out_specs=[vmem] * len(sizes),
        scratch_shapes=[pltpu.VMEM((block_total, ROWS), jnp.float32)] * 3,
        name="pack",
    )(slot_list, counts, chans, cells, offsets.reshape(block_total * 2, ROWS), centers, widths, lums)


def add_emitters(size, first, meta_ref, got_ref, acc, streams, fill, todo):
    source_count = got_ref.shape[0]
    share = acc.shape[0]
    stride = streams.shape[0] // share
    lane = lax.broadcasted_iota(jnp.int32, (FIELDS, ROWS), 1)
    for c in range(share):
        fill[c] = 0

    def append(source, carry):
        for place in range(size):
            row = place * FIELDS
            chan = meta_ref[source, 0, first + place]
            start = fill[chan]
            shift = start & (ROWS - 1)
            group = chan * stride + (start >> 7)
            turned = pltpu.roll(got_ref[source, row : row + FIELDS, :], shift, 1)
            pltpu.store(streams.at[group, 0:FIELDS, :], turned, mask=lane >= shift)
            streams[group + 1, 0:FIELDS, :] = turned
            fill[chan] = start + meta_ref[source, 1, first + place]
        return carry

    lax.fori_loop(0, source_count, append, 0)

    def list_chan(chan, count):
        total = fill[chan]

        def list_pair(pair, at):
            todo[0, at] = chan
            todo[1, at] = chan * stride + 2 * pair
            todo[2, at] = total - 2 * ROWS * pair
            return at + 1

        return lax.fori_loop(0, (total + 2 * ROWS - 1) >> 8, list_pair, count)

    pair_count = lax.fori_loop(0, share, list_chan, 0)
    for extra in range(UNROLL - 1):
        todo[0, pair_count + extra] = 0
        todo[1, pair_count + extra] = 0
        todo[2, pair_count + extra] = 0

    place16 = lax.broadcasted_iota(jnp.int32, (SIDE, ROWS), 0).astype(jnp.float32)
    place8 = lax.broadcasted_iota(jnp.int32, (8, ROWS), 0).astype(jnp.float32) + 0.5

    def hat(cell, frac):
        apart = place16 - cell
        return jnp.where(apart == 0.0, 1.0 - frac, jnp.where(apart == 1.0, frac, 0.0))

    def factors(group, left):
        props = jnp.where(lane < left, streams[group, 0:FIELDS, :], 0.0)
        cell, frac_x, frac_y, center, decay, bright = (props[f : f + 1, :] for f in range(FIELDS))
        cell_x = jnp.floor(cell * (1.0 / SIDE))
        weight_x = hat(cell_x, frac_x)
        weight_y = hat(cell - SIDE * cell_x, frac_y)
        spread = jnp.concatenate(
            [(weight_x[x : x + 1, :] * weight_y).astype(jnp.bfloat16) for x in range(SIDE)], axis=0
        )
        apart = place8 - center
        profile = [jnp.exp2(jnp.square(apart + 8.0 * i) * decay) for i in range(CB // 8)]
        total = profile[0]
        for part in profile[1:]:
            total = total + part
        scale = bright / jnp.sum(total, axis=0, keepdims=True)
        line = jnp.concatenate(profile, axis=0) * scale
        return spread, line.astype(jnp.bfloat16)

    def some_pairs(turn, carry):
        for step in range(UNROLL):
            at = turn * UNROLL + step
            chan, group, left = todo[0, at], todo[1, at], todo[2, at]
            spread_0, line_0 = factors(group, left)
            spread_1, line_1 = factors(group + 1, left - ROWS)
            acc[chan] += lax.dot_general(
                jnp.concatenate([spread_0, spread_1], axis=1),
                jnp.concatenate([line_0, line_1], axis=1),
                (((1,), (1,)), ((), ())),
                preferred_element_type=jnp.float32,
            )
        return carry

    lax.fori_loop(0, (pair_count + UNROLL - 1) // UNROLL, some_pairs, 0)


def first_kernel(size, meta_ref, got_ref, acc, streams, fill, todo):
    acc[...] = jnp.zeros_like(acc)
    add_emitters(size, 0, meta_ref, got_ref, acc, streams, fill, todo)


def last_kernel(size, first, meta_ref, got_ref, held_ref, width_ref, cube_ref, head_ref, tail_ref, acc, streams, fill, todo):
    acc[...] = held_ref[...]
    add_emitters(size, first, meta_ref, got_ref, acc, streams, fill, todo)
    share = acc.shape[0]

    def one_chan(chan, carry):
        columns = pl.ds(pl.multiple_of(chan * CB, CB), CB)
        smooth(acc.at[chan], width_ref[:, columns], cube_ref, columns)
        return carry

    lax.fori_loop(0, share, one_chan, 0)
    head_ref[...] = cube_ref[:, :CB].T[:EDGE]
    tail_ref[...] = cube_ref[:, (share - 1) * CB :].T[CB - EDGE :]


def smooth(plane_ref, widths, cube_ref, columns):
    decay = (-0.5 * LOG2E) / jnp.square(widths)
    places = lax.broadcasted_iota(jnp.int32, (SIDE, CB), 0).astype(jnp.float32)
    beam = [jnp.exp2(jnp.square(places - float(v)) * decay) for v in range(SIDE)]
    norm = beam[0]
    for v in range(1, SIDE):
        norm = norm + beam[v]
    inverse = 1.0 / norm
    beam = [b * inverse for b in beam]
    half = SIDE // 2
    even, odd = [None] * half, [None] * half
    for v in range(half):
        low = plane_ref[v * SIDE : (v + 1) * SIDE, :]
        high = plane_ref[(SIDE - 1 - v) * SIDE : (SIDE - v) * SIDE, :]
        both, apart = low + high, low - high
        near, far = beam[v][:half], beam[SIDE - 1 - v][:half]
        mean, rest = 0.5 * (near + far), 0.5 * (near - far)
        for x in range(half):
            term_even, term_odd = mean[x : x + 1, :] * both, rest[x : x + 1, :] * apart
            even[x] = term_even if v == 0 else even[x] + term_even
            odd[x] = term_odd if v == 0 else odd[x] + term_odd
    for x in range(SIDE):
        along_x = even[x] + odd[x] if x < half else even[SIDE - 1 - x] - odd[SIDE - 1 - x]
        total = None
        for v in range(SIDE):
            term = beam[v] * along_x[v : v + 1, :]
            total = term if v == 0 else total + term
        cube_ref[x * SIDE : (x + 1) * SIDE, columns] = total


SMEM = pl.BlockSpec(memory_space=pltpu.SMEM)
VMEM = pl.BlockSpec(memory_space=pltpu.VMEM)


def emitter_scratch(work, share):
    return [
        pltpu.VMEM((share * (work + 2), 8, ROWS), jnp.float32),
        pltpu.SMEM((share,), jnp.int32),
        pltpu.SMEM((3, work // 2 + share + UNROLL), jnp.int32),
    ]


def emitter_cost(work, got):
    return pl.CostEstimate(
        flops=work * 2 * PIX * CB * ROWS, transcendentals=work * CB * ROWS, bytes_accessed=got.size * 4
    )


def deposit_first(size, share, meta, got):
    work = got.shape[0] * size
    return pl.pallas_call(
        functools.partial(first_kernel, size),
        out_shape=jax.ShapeDtypeStruct((share, PIX, CB), jnp.float32),
        in_specs=[SMEM, VMEM],
        out_specs=VMEM,
        scratch_shapes=emitter_scratch(work, share),
        cost_estimate=emitter_cost(work, got),
        name="deposit_first",
    )(meta, got)


def deposit_last(size, first, share, meta, got, held, widths):
    work = got.shape[0] * size
    edge = jax.ShapeDtypeStruct((EDGE, PIX), jnp.float32)
    return pl.pallas_call(
        functools.partial(last_kernel, size, first),
        out_shape=[jax.ShapeDtypeStruct((PIX, share * CB), jnp.float32), edge, edge],
        in_specs=[SMEM, VMEM, VMEM, VMEM],
        out_specs=[VMEM] * 3,
        scratch_shapes=[pltpu.VMEM((share, PIX, CB), jnp.float32)] + emitter_scratch(work, share),
        cost_estimate=emitter_cost(work, got),
        name="deposit_last",
    )(meta, got, held, widths.reshape(1, -1))


def split(values):
    high = values.astype(jnp.bfloat16)
    return high, (values - high.astype(jnp.float32)).astype(jnp.bfloat16)


def times(left, right, dims):
    (left_high, left_low), (right_high, right_low) = left, right

    def dot(a, b):
        return lax.dot_general(a, b, (dims, ((), ())), preferred_element_type=jnp.float32)

    return dot(left_high, right_high) + (dot(left_high, right_low) + dot(left_low, right_high))


def band_kernel(taps_ref, high_ref, low_ref):
    rows, columns = high_ref.shape
    apart = lax.broadcasted_iota(jnp.int32, (3 * CB, CB), 0) - lax.broadcasted_iota(jnp.int32, (3 * CB, CB), 1)
    band = jnp.zeros((3 * CB, CB), jnp.float32)
    for k in range(TAPS):
        band = jnp.where(apart == CB - HALF + k, taps_ref[k], band)
    high, low = split(band)
    high_ref[...] = jnp.zeros_like(high_ref)
    low_ref[...] = jnp.zeros_like(low_ref)
    for i in range(columns // CB):
        high_ref[i * CB : (i + 3) * CB, i * CB : (i + 1) * CB] = high
        low_ref[i * CB : (i + 3) * CB, i * CB : (i + 1) * CB] = low


def bands(taps, wide):
    return pl.pallas_call(
        band_kernel,
        out_shape=[jax.ShapeDtypeStruct((wide + 2 * CB, wide), jnp.bfloat16)] * 2,
        in_specs=[SMEM],
        out_specs=[VMEM] * 2,
        name="bands",
    )(taps)


def taps_kernel(high_ref, low_ref, cube_ref, out_ref):
    wide = high_ref.shape[1]
    end = cube_ref.shape[1]
    for start in range(0, end, wide):
        low, high = max(start - CB, 0), min(start + wide + CB, end)
        rows = slice(low - start + CB, high - start + CB)
        out_ref[:, start : start + wide] = times(
            split(cube_ref[:, low:high]), (high_ref[rows], low_ref[rows]), ((1,), (0,))
        )


def sum_taps(band, cube):
    return pl.pallas_call(
        taps_kernel,
        out_shape=jax.ShapeDtypeStruct(cube.shape, jnp.float32),
        in_specs=[VMEM] * 3,
        out_specs=VMEM,
        cost_estimate=pl.CostEstimate(
            flops=6 * cube.size * band[0].shape[0], transcendentals=0, bytes_accessed=cube.size * 8
        ),
        name="taps",
    )(*band, cube)


def edge_kernel(high_ref, low_ref, before_ref, after_ref, part_ref, out_ref):
    wide = high_ref.shape[1]
    side = pl.program_id(0)

    @pl.when(side == 0)
    def _():
        rows, columns = slice(CB - EDGE, CB), slice(0, CB)
        out_ref[...] = part_ref[...] + times(
            split(before_ref[...]), (high_ref[rows, columns], low_ref[rows, columns]), ((0,), (0,))
        )

    @pl.when(side == 1)
    def _():
        rows, columns = slice(wide + CB, wide + CB + EDGE), slice(wide - CB, wide)
        out_ref[...] = part_ref[...] + times(
            split(after_ref[...]), (high_ref[rows, columns], low_ref[rows, columns]), ((0,), (0,))
        )


def add_edges(band, before, after, part):
    last = part.shape[1] // CB - 1
    whole = [pl.BlockSpec(a.shape, lambda i: (0, 0)) for a in (*band, before, after)]
    block = pl.BlockSpec((PIX, CB), lambda i: (0, i * last))
    return pl.pallas_call(
        edge_kernel,
        out_shape=jax.ShapeDtypeStruct(part.shape, jnp.float32),
        grid=(2,),
        in_specs=whole + [block],
        out_specs=block,
        input_output_aliases={4: 0},
        name="edges",
    )(*band, before, after, part)


def body(
    voxel_cell,
    offsets,
    line_center,
    line_width,
    luminosity,
    block_rows,
    block_chan,
    slot_table,
    beam_width,
    spectral_taps,
):
    slab_count = lax.axis_size("slab")
    dest_count = lax.axis_size("tile") * slab_count
    per_dest = slot_table.shape[1] // dest_count
    share = NCB // slab_count
    sizes = chunk_sizes(per_dest)
    sent = pack(
        sizes, dest_count, slab_count, share, slot_table, block_rows, block_chan,
        voxel_cell, offsets, line_center, line_width, luminosity,
    )
    got = []
    for piece in sent:
        if got:
            piece, got[-1] = lax.optimization_barrier((piece, got[-1]))
        got.append(lax.all_to_all(piece, ("tile", "slab"), split_axis=0, concat_axis=0, tiled=True))
    meta = got[0][:, sizes[0] * FIELDS : sizes[0] * FIELDS + 2, :per_dest].astype(jnp.int32)
    band = bands(spectral_taps, 2 * CB if share % 2 == 0 else CB)
    held = deposit_first(sizes[0], share, meta, got[0])
    cube, head, tail = deposit_last(sizes[1], sizes[0], share, meta, got[1], held, beam_width)
    ends = slab_count - 1
    before = lax.ppermute(tail, "slab", [(i, i + 1) for i in range(ends)])
    after = lax.ppermute(head, "slab", [(i + 1, i) for i in range(ends)])
    return add_edges(band, before, after, sum_taps(band, cube))[None]


def solution(mesh):
    placed = (
        P(("tile", "slab"), None),
        P(("tile", "slab"), None, None),
        P(("tile", "slab"), None),
        P(("tile", "slab"), None),
        P(("tile", "slab"), None),
        P(("tile", "slab")),
        P(("tile", "slab")),
        P(("tile", "slab"), None),
        P("slab"),
        P(),
    )
    return jax.shard_map(
        body, mesh=mesh, in_specs=placed, out_specs=P("tile", None, "slab"), check_vma=False
    )
```

```python
import functools
import math

import jax
import jax.numpy as jnp
from jax import lax
from jax.experimental import pallas as pl
from jax.experimental.pallas import tpu as pltpu
from jax.sharding import PartitionSpec as P

SIDE = 16
PIX = SIDE * SIDE
CB = 128
ROWS = 128
TAPS = 31
HALF = 15
EDGE = 16
NCB = 32
FIELDS = 6
UNROLL = 6
LOG2E = math.log2(math.e)
SMEM = pl.BlockSpec(memory_space=pltpu.SMEM)
VMEM = pl.BlockSpec(memory_space=pltpu.VMEM)
ANY = pl.BlockSpec(memory_space=pl.ANY)


def chunk_sizes(per_dest):
    part = max(per_dest * 3 // 8, 1)
    sizes = [part, part, per_dest - 2 * part]
    return [size for size in sizes if size > 0]


def padded_rows(rows):
    return -(-rows // 8) * 8


def pack_kernel(sizes, slab_count, share, slot_ref, count_ref, chan_ref, cell_ref, offset_ref, center_ref,
                width_ref, lum_ref, *refs):
    outs, (props, stream) = refs[: len(sizes)], refs[len(sizes) :]
    dest_count = outs[0].shape[0]
    per_dest = sum(sizes)
    lane = lax.broadcasted_iota(jnp.int32, (8, ROWS), 1)
    row_lane = lax.broadcasted_iota(jnp.int32, (1, ROWS), 1)

    def gather_fields(tile, carry):
        first = pl.multiple_of(tile * 8, 8)
        here = pl.ds(first, 8)
        fields = (
            cell_ref[here, :].astype(jnp.float32),
            offset_ref[pl.ds(2 * first, 8, stride=2), :],
            offset_ref[pl.ds(2 * first + 1, 8, stride=2), :],
            center_ref[here, :],
            (-0.5 * LOG2E) / jnp.square(width_ref[here, :]),
            lum_ref[here, :].astype(jnp.bfloat16).astype(jnp.float32),
        )
        for field, values in enumerate(fields):
            props[pl.ds(8 * first + field, 8, stride=8), :] = values
        return carry

    lax.fori_loop(0, cell_ref.shape[0] // 8, gather_fields, 0, unroll=2)

    def one_dest(dest, longest):
        first_chan = lax.rem(dest, slab_count) * share
        chan_row = jnp.zeros((1, ROWS), jnp.int32)
        end_row = jnp.zeros((1, ROWS), jnp.int32)
        start = jnp.int32(0)
        for slot in range(per_dest):
            block = slot_ref[0, dest * per_dest + slot]
            filled = block >= 0
            block = jnp.maximum(block, 0)
            live = jnp.where(filled, count_ref[block], 0)
            chan_row = jnp.where(row_lane == slot, chan_ref[block], chan_row)
            shift = start & (ROWS - 1)
            group = start >> 7
            turned = pltpu.roll(props[pl.ds(pl.multiple_of(block * 8, 8), 8), :], shift, 1)
            pltpu.store(stream.at[group], turned, mask=lane >= shift)
            stream[group + 1] = turned
            start = start + live
            end_row = jnp.where(row_lane == slot, start, end_row)
        group = 0
        for out, size in zip(outs, sizes):
            for place in range(size):
                out[dest, place * FIELDS : (place + 1) * FIELDS, :] = stream[group, 0:FIELDS, :]
                group += 1
        meta = sizes[0] * FIELDS
        outs[0][dest, meta : meta + 1, :] = (chan_row - first_chan).astype(jnp.float32)
        outs[0][dest, meta + 1 : meta + 2, :] = end_row.astype(jnp.float32)
        return jnp.maximum(longest, start)

    longest = lax.fori_loop(0, dest_count, one_dest, jnp.int32(0))
    meta = sizes[0] * FIELDS

    def tell(dest, carry):
        row = outs[0][dest, meta : meta + 1, :]
        outs[0][dest, meta : meta + 1, :] = jnp.where(row_lane == ROWS - 1, longest.astype(jnp.float32), row)
        return carry

    lax.fori_loop(0, dest_count, tell, 0)


def pack(sizes, dest_count, slab_count, share, slot_list, counts, chans, cells, offsets, centers, widths, lums):
    rows = [size * FIELDS for size in sizes]
    rows[0] += 2
    block_total = cells.shape[0]
    return pl.pallas_call(
        functools.partial(pack_kernel, sizes, slab_count, share),
        out_shape=[jax.ShapeDtypeStruct((dest_count, padded_rows(r), ROWS), jnp.float32) for r in rows],
        in_specs=[SMEM] * 3 + [VMEM] * 5,
        out_specs=[VMEM] * len(sizes),
        scratch_shapes=[
            pltpu.VMEM((block_total * 8, ROWS), jnp.float32),
            pltpu.VMEM((sum(sizes) + 2, 8, ROWS), jnp.float32),
        ],
        name="pack",
    )(slot_list, counts, chans, cells, offsets.reshape(block_total * 2, ROWS), centers, widths, lums)


def exclusive(size):
    before = lax.broadcasted_iota(jnp.int32, (size, size), 0)
    return (before < lax.broadcasted_iota(jnp.int32, (size, size), 1)).astype(jnp.bfloat16)


def plan_moves(size, first, per_dest, share, stride, rows, chan, end, plan):
    sources = chan.shape[0]
    lane = lax.broadcasted_iota(jnp.int32, chan.shape, 1)
    low, high = float(first * ROWS), float((first + size) * ROWS)
    start = jnp.where(lane == 0, 0.0, pltpu.roll(end, 1, 1))
    begin = jnp.clip(start, low, high) - low
    count = jnp.where(lane < per_dest, jnp.clip(end, low, high) - low - begin, 0.0)
    chan = jnp.where(count > 0.0, chan, 0.0)
    across = exclusive(ROWS)
    down = exclusive(sources)
    filled = jnp.zeros(chan.shape, jnp.float32)
    totals = jnp.zeros(chan.shape, jnp.float32)
    for c in range(share):
        own = jnp.where(chan == float(c), count, 0.0)
        moved = own.astype(jnp.bfloat16)
        here = jnp.dot(moved, across, preferred_element_type=jnp.float32)
        above = lax.dot_general(down, moved, (((0,), (0,)), ((), ())), preferred_element_type=jnp.float32)
        above = jnp.sum(above, axis=1, keepdims=True) + float(c * stride * ROWS)
        filled = filled + jnp.where(chan == float(c), here + above, 0.0)
        total = jnp.sum(jnp.sum(own, axis=0, keepdims=True), axis=1, keepdims=True)
        totals = totals + jnp.where(lane == c, total, 0.0)
    filled = filled.astype(jnp.int32)
    begin = begin.astype(jnp.int32)
    base = lax.broadcasted_iota(jnp.int32, chan.shape, 0) * rows
    group = jnp.minimum(begin >> 7, size - 1)
    table = totals.astype(jnp.int32)
    for values in ((filled >> 7) * 8, (filled - begin) & (ROWS - 1), begin & (ROWS - 1), base + group * FIELDS):
        table = jnp.where(lane < per_dest, values, pltpu.roll(table, per_dest, 1))
    plan[...] = table


def add_emitters(size, first, per_dest, chan, end, got, acc, streams, todo, plan, moves, sem):
    source_count = chan.shape[0]
    share = acc.shape[0]
    stride = streams.shape[0] // (8 * share)
    lane = lax.broadcasted_iota(jnp.int32, (FIELDS, ROWS), 1)
    plan_moves(size, first, per_dest, share, stride, (got.shape[0] - 8) // source_count, chan, end, plan)
    copy = pltpu.make_async_copy(plan, moves, sem)
    copy.start()
    copy.wait()

    def append(source, carry):
        for place in range(per_dest):
            row, begin, turn, target = (moves[source, k * per_dest + place] for k in range(4))
            target = pl.multiple_of(target, 8)
            here = got[pl.ds(row, FIELDS), :]
            there = got[pl.ds(row + FIELDS, FIELDS), :]
            filled = (jnp.full(lane.shape, begin, jnp.int32) + turn) & (ROWS - 1)
            whole = pltpu.roll(jnp.where(lane >= begin, here, there), turn, 1)
            pltpu.store(streams.at[pl.ds(target, FIELDS), :], whole, mask=lane >= filled)
            streams[pl.ds(target + 8, FIELDS), :] = whole
        return carry

    lax.fori_loop(0, source_count, append, 0)

    def list_chan(chan, count):
        total = moves[0, 4 * per_dest + chan]

        def list_pair(pair, at):
            todo[0, at] = chan
            todo[1, at] = chan * stride + 2 * pair
            todo[2, at] = total - 2 * ROWS * pair
            return at + 1

        return lax.fori_loop(0, (total + 2 * ROWS - 1) >> 8, list_pair, count)

    pair_count = lax.fori_loop(0, share, list_chan, 0)
    for extra in range(UNROLL - 1):
        todo[0, pair_count + extra] = 0
        todo[1, pair_count + extra] = 0
        todo[2, pair_count + extra] = 0

    place16 = lax.broadcasted_iota(jnp.int32, (SIDE, ROWS), 0).astype(jnp.float32)
    place8 = lax.broadcasted_iota(jnp.int32, (8, ROWS), 0).astype(jnp.float32) + 0.5

    def hat(cell, frac):
        apart = place16 - cell
        return jnp.where(apart == 0.0, 1.0 - frac, jnp.where(apart == 1.0, frac, 0.0))

    def factors(group, left):
        props = jnp.where(lane < left, streams[pl.ds(pl.multiple_of(group * 8, 8), FIELDS), :], 0.0)
        cell, frac_x, frac_y, center, decay, bright = (props[f : f + 1, :] for f in range(FIELDS))
        cell_x = jnp.floor(cell * (1.0 / SIDE))
        weight_x = hat(cell_x, frac_x)
        weight_y = hat(cell - SIDE * cell_x, frac_y)
        spread = jnp.concatenate(
            [(weight_x[x : x + 1, :] * weight_y).astype(jnp.bfloat16) for x in range(SIDE)], axis=0
        )
        apart = place8 - center
        profile = [jnp.exp2(jnp.square(apart + 8.0 * i) * decay) for i in range(CB // 8)]
        total = profile[0]
        for part in profile[1:]:
            total = total + part
        scale = bright / jnp.sum(total, axis=0, keepdims=True)
        line = jnp.concatenate(profile, axis=0) * scale
        return spread, line.astype(jnp.bfloat16)

    def some_pairs(turn, carry):
        for step in range(UNROLL):
            at = turn * UNROLL + step
            chan, group, left = todo[0, at], todo[1, at], todo[2, at]
            spread_0, line_0 = factors(group, left)
            spread_1, line_1 = factors(group + 1, left - ROWS)
            acc[chan] += lax.dot_general(
                jnp.concatenate([spread_0, spread_1], axis=1),
                jnp.concatenate([line_0, line_1], axis=1),
                (((1,), (1,)), ((), ())),
                preferred_element_type=jnp.float32,
            )
        return carry

    lax.fori_loop(0, (pair_count + UNROLL - 1) // UNROLL, some_pairs, 0)


def fetch(got_ref, got, sem):
    copy = pltpu.make_async_copy(got_ref, got.at[pl.ds(0, got_ref.shape[0])], sem)
    copy.start()
    return copy


def first_kernel(size, per_dest, share, got_ref, acc, got, got_sem, *scratch):
    copy = fetch(got_ref, got, got_sem)
    acc[...] = jnp.zeros_like(acc)
    sources = scratch[-2].shape[0]
    rows = got_ref.shape[0] // sources
    copy.wait()
    chan = got[pl.ds(size * FIELDS, sources, stride=rows), :]
    end = got[pl.ds(size * FIELDS + 1, sources, stride=rows), :]
    add_emitters(size, 0, per_dest, chan, end, got, acc, *scratch)


def more_kernel(size, first, per_dest, chan_ref, end_ref, got_ref, held_ref, acc, got, got_sem, *scratch):
    copy = fetch(got_ref, got, got_sem)
    acc[...] = held_ref[...]
    copy.wait()
    add_emitters(size, first, per_dest, chan_ref[...], end_ref[...], got, acc, *scratch)


def last_kernel(size, first, per_dest, chan_ref, end_ref, got_ref, held_ref, width_ref, cube_ref, head_ref, tail_ref,
                acc, got, got_sem, *scratch):
    copy = fetch(got_ref, got, got_sem)
    acc[...] = held_ref[...]
    copy.wait()
    add_emitters(size, first, per_dest, chan_ref[...], end_ref[...], got, acc, *scratch)
    share = acc.shape[0]

    def one_chan(chan, carry):
        columns = pl.ds(pl.multiple_of(chan * CB, CB), CB)
        smooth(acc.at[chan], width_ref[:, columns], cube_ref, columns)
        return carry

    lax.fori_loop(0, share, one_chan, 0)
    head_ref[...] = cube_ref[:, :CB].T[:EDGE]
    tail_ref[...] = cube_ref[:, (share - 1) * CB :].T[CB - EDGE :]


def smooth(plane_ref, widths, cube_ref, columns):
    decay = (-0.5 * LOG2E) / jnp.square(widths)
    places = lax.broadcasted_iota(jnp.int32, (SIDE, CB), 0).astype(jnp.float32)
    beam = [jnp.exp2(jnp.square(places - float(v)) * decay) for v in range(SIDE)]
    norm = beam[0]
    for v in range(1, SIDE):
        norm = norm + beam[v]
    inverse = 1.0 / norm
    beam = [b * inverse for b in beam]
    half = SIDE // 2
    even, odd = [None] * half, [None] * half
    for v in range(half):
        low = plane_ref[v * SIDE : (v + 1) * SIDE, :]
        high = plane_ref[(SIDE - 1 - v) * SIDE : (SIDE - v) * SIDE, :]
        both, apart = low + high, low - high
        near, far = beam[v][:half], beam[SIDE - 1 - v][:half]
        mean, rest = 0.5 * (near + far), 0.5 * (near - far)
        for x in range(half):
            term_even, term_odd = mean[x : x + 1, :] * both, rest[x : x + 1, :] * apart
            even[x] = term_even if v == 0 else even[x] + term_even
            odd[x] = term_odd if v == 0 else odd[x] + term_odd
    for x in range(SIDE):
        along_x = even[x] + odd[x] if x < half else even[SIDE - 1 - x] - odd[SIDE - 1 - x]
        total = None
        for v in range(SIDE):
            term = beam[v] * along_x[v : v + 1, :]
            total = term if v == 0 else total + term
        cube_ref[x * SIDE : (x + 1) * SIDE, columns] = total


def emitter_scratch(size, got, share):
    sources, rows = got.shape[:2]
    work = size * sources
    return [
        pltpu.VMEM((sources * rows + 8, ROWS), jnp.float32),
        pltpu.SemaphoreType.DMA,
        pltpu.VMEM((share * (work + 2) * 8, ROWS), jnp.float32),
        pltpu.SMEM((3, work // 2 + share + UNROLL), jnp.int32),
        pltpu.VMEM((sources, ROWS), jnp.int32),
        pltpu.SMEM((sources, ROWS), jnp.int32),
        pltpu.SemaphoreType.DMA,
    ]


def flat(got):
    return got.reshape(-1, ROWS)


def emitter_cost(size, got):
    work = size * got.shape[0]
    return pl.CostEstimate(
        flops=work * 2 * PIX * CB * ROWS, transcendentals=work * CB * ROWS, bytes_accessed=got.size * 4
    )


def deposit_first(size, per_dest, share, got):
    return pl.pallas_call(
        functools.partial(first_kernel, size, per_dest, share),
        out_shape=jax.ShapeDtypeStruct((share, PIX, CB), jnp.float32),
        in_specs=[ANY],
        out_specs=VMEM,
        scratch_shapes=emitter_scratch(size, got, share),
        cost_estimate=emitter_cost(size, got),
        name="deposit_first",
    )(flat(got))


def deposit_more(size, first, per_dest, share, chan, end, got, held):
    return pl.pallas_call(
        functools.partial(more_kernel, size, first, per_dest),
        out_shape=jax.ShapeDtypeStruct((share, PIX, CB), jnp.float32),
        in_specs=[VMEM, VMEM, ANY, VMEM],
        out_specs=VMEM,
        scratch_shapes=emitter_scratch(size, got, share),
        input_output_aliases={3: 0},
        name="deposit_more",
    )(chan, end, flat(got), held)


def deposit_last(size, first, per_dest, share, chan, end, got, held, widths):
    edge = jax.ShapeDtypeStruct((EDGE, PIX), jnp.float32)
    return pl.pallas_call(
        functools.partial(last_kernel, size, first, per_dest),
        out_shape=[jax.ShapeDtypeStruct((PIX, share * CB), jnp.float32), edge, edge],
        in_specs=[VMEM, VMEM, ANY, VMEM, VMEM],
        out_specs=[VMEM] * 3,
        scratch_shapes=[pltpu.VMEM((share, PIX, CB), jnp.float32)] + emitter_scratch(size, got, share),
        cost_estimate=emitter_cost(size, got),
        name="deposit_last",
    )(chan, end, flat(got), held, widths.reshape(1, -1))


def split(values):
    high = values.astype(jnp.bfloat16)
    return high, (values - high.astype(jnp.float32)).astype(jnp.bfloat16)


def times(left, right, dims):
    (left_high, left_low), (right_high, right_low) = left, right

    def dot(a, b):
        return lax.dot_general(a, b, (dims, ((), ())), preferred_element_type=jnp.float32)

    return dot(left_high, right_high) + (dot(left_high, right_low) + dot(left_low, right_high))


def band_kernel(taps_ref, high_ref, low_ref):
    rows, columns = high_ref.shape
    apart = lax.broadcasted_iota(jnp.int32, (3 * CB, CB), 0) - lax.broadcasted_iota(jnp.int32, (3 * CB, CB), 1)
    band = jnp.zeros((3 * CB, CB), jnp.float32)
    for k in range(TAPS):
        band = jnp.where(apart == CB - HALF + k, taps_ref[k], band)
    high, low = split(band)
    high_ref[...] = jnp.zeros_like(high_ref)
    low_ref[...] = jnp.zeros_like(low_ref)
    for i in range(columns // CB):
        high_ref[i * CB : (i + 3) * CB, i * CB : (i + 1) * CB] = high
        low_ref[i * CB : (i + 3) * CB, i * CB : (i + 1) * CB] = low


def bands(taps, wide):
    return pl.pallas_call(
        band_kernel,
        out_shape=[jax.ShapeDtypeStruct((wide + 2 * CB, wide), jnp.bfloat16)] * 2,
        in_specs=[SMEM],
        out_specs=[VMEM] * 2,
        name="bands",
    )(taps)


def taps_kernel(high_ref, low_ref, cube_ref, out_ref):
    wide = high_ref.shape[1]
    end = cube_ref.shape[1]
    for start in range(0, end, wide):
        low, high = max(start - CB, 0), min(start + wide + CB, end)
        rows = slice(low - start + CB, high - start + CB)
        out_ref[:, start : start + wide] = times(
            split(cube_ref[:, low:high]), (high_ref[rows], low_ref[rows]), ((1,), (0,))
        )


def sum_taps(band, cube):
    return pl.pallas_call(
        taps_kernel,
        out_shape=jax.ShapeDtypeStruct(cube.shape, jnp.float32),
        in_specs=[VMEM] * 3,
        out_specs=VMEM,
        cost_estimate=pl.CostEstimate(
            flops=6 * cube.size * band[0].shape[0], transcendentals=0, bytes_accessed=cube.size * 8
        ),
        name="taps",
    )(*band, cube)


def edge_kernel(high_ref, low_ref, before_ref, after_ref, part_ref, out_ref):
    side = pl.program_id(0)
    edge = jnp.where(side == 0, before_ref[...], after_ref[...])
    out_ref[...] = part_ref[...] + times(split(edge), (high_ref[...], low_ref[...]), ((0,), (0,)))


def add_edges(band, before, after, part):
    last = part.shape[1] // CB - 1
    rows, columns = band[0].shape
    top, bottom = (CB - EDGE) // EDGE, (rows - CB) // EDGE
    corner = pl.BlockSpec((EDGE, CB), lambda i: (top + i * (bottom - top), i * (columns // CB - 1)))
    edge = pl.BlockSpec((EDGE, PIX), lambda i: (0, 0))
    block = pl.BlockSpec((PIX, CB), lambda i: (0, i * last))
    return pl.pallas_call(
        edge_kernel,
        out_shape=jax.ShapeDtypeStruct(part.shape, jnp.float32),
        grid=(2,),
        in_specs=[corner, corner, edge, edge, block],
        out_specs=block,
        input_output_aliases={4: 0},
        name="edges",
    )(*band, before, after, part)


def body(
    voxel_cell,
    offsets,
    line_center,
    line_width,
    luminosity,
    block_rows,
    block_chan,
    slot_table,
    beam_width,
    spectral_taps,
):
    slab_count = lax.axis_size("slab")
    dest_count = lax.axis_size("tile") * slab_count
    per_dest = slot_table.shape[1] // dest_count
    share = NCB // slab_count
    sizes = chunk_sizes(per_dest)
    sent = pack(
        sizes, dest_count, slab_count, share, slot_table, block_rows, block_chan,
        voxel_cell, offsets, line_center, line_width, luminosity,
    )
    def exchange(piece):
        return lax.all_to_all(piece, ("tile", "slab"), split_axis=0, concat_axis=0, tiled=True)

    got_first = exchange(sent[0])
    got_first, last_piece = lax.optimization_barrier((got_first, sent[1]))
    got_last = exchange(last_piece)
    chan = got_first[:, sizes[0] * FIELDS, :]
    end = got_first[:, sizes[0] * FIELDS + 1, :]
    band = bands(spectral_taps, 2 * CB if share % 2 == 0 else CB)
    held = deposit_first(sizes[0], per_dest, share, got_first)
    reach = sizes[0] + sizes[1]
    if len(sizes) > 2:
        longest = jnp.max(chan[:, ROWS - 1])
        held, got_last = lax.optimization_barrier((held, got_last))
        held = lax.cond(
            longest > float(reach * ROWS),
            lambda held: deposit_more(sizes[2], reach, per_dest, share, chan, end, exchange(sent[2]), held),
            lambda held: held,
            held,
        )
    cube, head, tail = deposit_last(sizes[1], sizes[0], per_dest, share, chan, end, got_last, held, beam_width)
    ends = slab_count - 1
    before = lax.ppermute(tail, "slab", [(i, i + 1) for i in range(ends)])
    after = lax.ppermute(head, "slab", [(i + 1, i) for i in range(ends)])
    return add_edges(band, before, after, sum_taps(band, cube))[None]


def solution(mesh):
    placed = (
        P(("tile", "slab"), None),
        P(("tile", "slab"), None, None),
        P(("tile", "slab"), None),
        P(("tile", "slab"), None),
        P(("tile", "slab"), None),
        P(("tile", "slab")),
        P(("tile", "slab")),
        P(("tile", "slab"), None),
        P("slab"),
        P(),
    )
    return jax.shard_map(
        body, mesh=mesh, in_specs=placed, out_specs=P("tile", None, "slab"), check_vma=False
    )
```

```python
import functools
import math

import jax
import jax.numpy as jnp
from jax import lax
from jax.experimental import pallas as pl
from jax.experimental.pallas import tpu as pltpu
from jax.sharding import PartitionSpec as P

SIDE = 16
PIX = SIDE * SIDE
CB = 128
ROWS = 128
TAPS = 31
HALF = 15
EDGE = 16
NCB = 32
FIELDS = 6
UNROLL = 6
SKIP = 4
LOG2E = math.log2(math.e)
SMEM = pl.BlockSpec(memory_space=pltpu.SMEM)
VMEM = pl.BlockSpec(memory_space=pltpu.VMEM)
ANY = pl.BlockSpec(memory_space=pl.ANY)


def chunk_sizes(per_dest):
    early = late = max(per_dest * 9 // 24, 1)
    sizes = [early, late, per_dest - early - late]
    return [size for size in sizes if size > 0]


def padded_rows(rows):
    return -(-rows // 8) * 8


def pack_kernel(sizes, wanted, slab_count, share, slot_ref, count_ref, chan_ref, cell_ref, offset_ref, center_ref,
                width_ref, lum_ref, *refs):
    outs = dict(zip(wanted, refs))
    props, stream, slots, counts, chans, plan, moves, sem = refs[len(wanted) :]
    dest_count = slots.shape[0]
    per_dest = sum(sizes)
    block_total = cell_ref.shape[0]
    lane = lax.broadcasted_iota(jnp.int32, (dest_count, ROWS), 1)

    slot_row = slot_ref[...]
    blocks = lax.broadcasted_iota(jnp.int32, (block_total, slot_row.shape[1]), 0)
    chosen = jnp.where(blocks == slot_row, 1.0, 0.0).astype(jnp.bfloat16)
    table = jnp.concatenate([count_ref[...].reshape(1, -1), chan_ref[...].reshape(1, -1)], axis=0).astype(jnp.float32).astype(jnp.bfloat16)
    looked = jnp.dot(table, chosen, preferred_element_type=jnp.float32)
    slots[...] = jnp.zeros_like(slots)
    counts[...] = jnp.zeros_like(counts)
    chans[...] = jnp.zeros_like(chans)
    for dest in range(dest_count):
        columns = slice(dest * per_dest, (dest + 1) * per_dest)
        slots[dest : dest + 1, :per_dest] = slot_row[:, columns]
        counts[dest : dest + 1, :per_dest] = looked[0:1, columns]
        chans[dest : dest + 1, :per_dest] = looked[1:2, columns]
    count = counts[...]
    until = jnp.dot(count.astype(jnp.bfloat16), exclusive(ROWS), preferred_element_type=jnp.float32)
    end = until + count
    start = until.astype(jnp.int32)
    orders = jnp.zeros(lane.shape, jnp.int32)
    for values in ((start >> 7) * 8, start & (ROWS - 1), jnp.maximum(slots[...], 0) * 8):
        orders = jnp.where(lane < per_dest, values, pltpu.roll(orders, per_dest, 1))
    plan[...] = orders
    copy = pltpu.make_async_copy(plan, moves, sem)
    copy.start()

    if 0 in outs:
        rows = outs[0].shape[0] // dest_count
        dests = lax.broadcasted_iota(jnp.int32, lane.shape, 0)
        chan = chans[...] - (lax.rem(dests, slab_count) * share).astype(jnp.float32)
        longest = jnp.max(jnp.max(end, axis=0, keepdims=True), axis=1, keepdims=True)
        meta = sizes[0] * FIELDS
        outs[0][pl.ds(meta, dest_count, stride=rows), :] = jnp.where(lane == ROWS - 1, longest, chan)
        outs[0][pl.ds(meta + 1, dest_count, stride=rows), :] = end

    def gather_fields(tile, carry):
        first = pl.multiple_of(tile * 8, 8)
        here = pl.ds(first, 8)
        fields = (
            cell_ref[here, :].astype(jnp.float32),
            offset_ref[pl.ds(2 * first, 8, stride=2), :],
            offset_ref[pl.ds(2 * first + 1, 8, stride=2), :],
            center_ref[here, :],
            (-0.5 * LOG2E) / jnp.square(width_ref[here, :]),
            lum_ref[here, :].astype(jnp.bfloat16).astype(jnp.float32),
        )
        for field, values in enumerate(fields):
            props[pl.ds(8 * first + field, 8, stride=8), :] = values
        return carry

    lax.fori_loop(0, block_total // 8, gather_fields, 0, unroll=2)
    copy.wait()
    lanes = lax.broadcasted_iota(jnp.int32, (8, ROWS), 1)

    def one_dest(dest, carry):
        for slot in range(per_dest):
            row, shift, target = (moves[dest, k * per_dest + slot] for k in range(3))
            row, target = pl.multiple_of(row, 8), pl.multiple_of(target, 8)
            turned = pltpu.roll(props[pl.ds(row, 8), :], shift, 1)
            pltpu.store(stream.at[pl.ds(target, 8), :], turned, mask=lanes >= shift)
            stream[pl.ds(target + 8, 8), :] = turned
        group = 0
        for part, size in enumerate(sizes):
            if part in outs:
                out = outs[part]
                base = pl.multiple_of(dest * (out.shape[0] // dest_count), 8)
                for place in range(size):
                    out[pl.ds(base + place * FIELDS, FIELDS), :] = stream[8 * (group + place) : 8 * (group + place) + FIELDS, :]
            group += size
        return carry

    lax.fori_loop(0, dest_count, one_dest, 0)


def pack(sizes, wanted, dest_count, slab_count, share, slot_list, counts, chans, cells, offsets, centers, widths, lums):
    rows = [padded_rows(size * FIELDS + (2 if part == 0 else 0)) for part, size in enumerate(sizes)]
    block_total = cells.shape[0]
    sent = pl.pallas_call(
        functools.partial(pack_kernel, sizes, wanted, slab_count, share),
        out_shape=[jax.ShapeDtypeStruct((dest_count * rows[part], ROWS), jnp.float32) for part in wanted],
        in_specs=[VMEM] * 8,
        out_specs=[VMEM] * len(wanted),
        scratch_shapes=[
            pltpu.VMEM((block_total * 8, ROWS), jnp.float32),
            pltpu.VMEM(((sum(sizes) + 2) * 8, ROWS), jnp.float32),
            pltpu.VMEM((dest_count, ROWS), jnp.int32),
            pltpu.VMEM((dest_count, ROWS), jnp.float32),
            pltpu.VMEM((dest_count, ROWS), jnp.float32),
            pltpu.VMEM((dest_count, ROWS), jnp.int32),
            pltpu.SMEM((dest_count, ROWS), jnp.int32),
            pltpu.SemaphoreType.DMA,
        ],
        name="pack",
    )(
        slot_list, counts, chans, cells,
        offsets.reshape(block_total * 2, ROWS), centers, widths, lums,
    )
    return [piece.reshape(dest_count, rows[part], ROWS) for part, piece in zip(wanted, sent)]


def exclusive(size):
    before = lax.broadcasted_iota(jnp.int32, (size, size), 0)
    return (before < lax.broadcasted_iota(jnp.int32, (size, size), 1)).astype(jnp.bfloat16)


def plan_moves(size, first, per_dest, share, stride, rows, chan, end, plan):
    sources = chan.shape[0]
    lane = lax.broadcasted_iota(jnp.int32, chan.shape, 1)
    low, high = float(first * ROWS), float((first + size) * ROWS)
    start = jnp.where(lane == 0, 0.0, pltpu.roll(end, 1, 1))
    begin = jnp.clip(start, low, high) - low
    count = jnp.where(lane < per_dest, jnp.clip(end, low, high) - low - begin, 0.0)
    chan = jnp.where(count > 0.0, chan, 0.0)
    across = exclusive(ROWS)
    down = exclusive(sources)
    filled = jnp.zeros(chan.shape, jnp.float32)
    totals = jnp.zeros(chan.shape, jnp.float32)
    for c in range(share):
        own = jnp.where(chan == float(c), count, 0.0)
        moved = own.astype(jnp.bfloat16)
        here = jnp.dot(moved, across, preferred_element_type=jnp.float32)
        above = lax.dot_general(down, moved, (((0,), (0,)), ((), ())), preferred_element_type=jnp.float32)
        above = jnp.sum(above, axis=1, keepdims=True) + float(c * stride * ROWS)
        filled = filled + jnp.where(chan == float(c), here + above, 0.0)
        total = jnp.sum(jnp.sum(own, axis=0, keepdims=True), axis=1, keepdims=True)
        totals = totals + jnp.where(lane == c, total, 0.0)
    for start in range(0, per_dest, SKIP):
        inside = (lane >= start) & (lane < start + SKIP)
        total = jnp.sum(jnp.where(inside, count, 0.0), axis=1, keepdims=True)
        totals = totals + jnp.where(lane == share + start // SKIP, total, 0.0)
    filled = filled.astype(jnp.int32)
    begin = begin.astype(jnp.int32)
    base = lax.broadcasted_iota(jnp.int32, chan.shape, 0) * rows
    group = jnp.minimum(begin >> 7, size - 1)
    table = totals.astype(jnp.int32)
    for values in ((filled >> 7) * 8, (filled - begin) & (ROWS - 1), begin & (ROWS - 1), base + group * FIELDS):
        table = jnp.where(lane < per_dest, values, pltpu.roll(table, per_dest, 1))
    plan[...] = table


def add_emitters(size, first, per_dest, chan, end, got, acc, streams, todo, plan, moves, sem):
    source_count = chan.shape[0]
    share = acc.shape[0]
    stride = streams.shape[0] // (8 * share)
    lane = lax.broadcasted_iota(jnp.int32, (FIELDS, ROWS), 1)
    plan_moves(size, first, per_dest, share, stride, (got.shape[0] - 8) // source_count, chan, end, plan)
    copy = pltpu.make_async_copy(plan, moves, sem)
    copy.start()
    copy.wait()

    def move(source, places):
        for place in places:
            row, begin, turn, target = (moves[source, k * per_dest + place] for k in range(4))
            target = pl.multiple_of(target, 8)
            here = got[pl.ds(row, FIELDS), :]
            there = got[pl.ds(row + FIELDS, FIELDS), :]
            filled = (jnp.full(lane.shape, begin, jnp.int32) + turn) & (ROWS - 1)
            whole = pltpu.roll(jnp.where(lane >= begin, here, there), turn, 1)
            pltpu.store(streams.at[pl.ds(target, FIELDS), :], whole, mask=lane >= filled)
            streams[pl.ds(target + 8, FIELDS), :] = whole

    def append(source, carry):
        if first == 0:
            move(source, range(per_dest))
        for start in range(0, 0 if first == 0 else per_dest, SKIP):
            places = range(start, min(start + SKIP, per_dest))
            live = moves[source, 4 * per_dest + share + start // SKIP]
            pl.when(live > 0)(functools.partial(move, source, places))
        return carry

    lax.fori_loop(0, source_count, append, 0)

    def list_chan(chan, count):
        total = moves[0, 4 * per_dest + chan]

        def list_pair(pair, at):
            todo[0, at] = chan
            todo[1, at] = chan * stride + 2 * pair
            todo[2, at] = total - 2 * ROWS * pair
            return at + 1

        return lax.fori_loop(0, (total + 2 * ROWS - 1) >> 8, list_pair, count)

    pair_count = lax.fori_loop(0, share, list_chan, 0)
    for extra in range(UNROLL - 1):
        todo[0, pair_count + extra] = 0
        todo[1, pair_count + extra] = 0
        todo[2, pair_count + extra] = 0

    place16 = lax.broadcasted_iota(jnp.int32, (SIDE, ROWS), 0).astype(jnp.float32)
    place8 = lax.broadcasted_iota(jnp.int32, (8, ROWS), 0).astype(jnp.float32) + 0.5

    def hat(cell, frac):
        apart = place16 - cell
        return jnp.where(apart == 0.0, 1.0 - frac, jnp.where(apart == 1.0, frac, 0.0))

    def factors(group, left):
        props = jnp.where(lane < left, streams[pl.ds(pl.multiple_of(group * 8, 8), FIELDS), :], 0.0)
        cell, frac_x, frac_y, center, decay, bright = (props[f : f + 1, :] for f in range(FIELDS))
        cell_x = jnp.floor(cell * (1.0 / SIDE))
        weight_x = hat(cell_x, frac_x)
        weight_y = hat(cell - SIDE * cell_x, frac_y)
        spread = jnp.concatenate(
            [(weight_x[x : x + 1, :] * weight_y).astype(jnp.bfloat16) for x in range(SIDE)], axis=0
        )
        apart = place8 - center
        profile = [jnp.exp2(jnp.square(apart + 8.0 * i) * decay) for i in range(CB // 8)]
        total = profile[0]
        for part in profile[1:]:
            total = total + part
        scale = bright / jnp.sum(total, axis=0, keepdims=True)
        line = jnp.concatenate(profile, axis=0) * scale
        return spread, line.astype(jnp.bfloat16)

    def some_pairs(turn, carry):
        for step in range(UNROLL):
            at = turn * UNROLL + step
            chan, group, left = todo[0, at], todo[1, at], todo[2, at]
            spread_0, line_0 = factors(group, left)
            spread_1, line_1 = factors(group + 1, left - ROWS)
            acc[chan] += lax.dot_general(
                jnp.concatenate([spread_0, spread_1], axis=1),
                jnp.concatenate([line_0, line_1], axis=1),
                (((1,), (1,)), ((), ())),
                preferred_element_type=jnp.float32,
            )
        return carry

    lax.fori_loop(0, (pair_count + UNROLL - 1) // UNROLL, some_pairs, 0)


def fetch(got_ref, got, sem):
    copy = pltpu.make_async_copy(got_ref, got.at[pl.ds(0, got_ref.shape[0])], sem)
    copy.start()
    return copy


def first_kernel(size, per_dest, share, got_ref, acc, chan_ref, end_ref, got, got_sem, *scratch):
    copy = fetch(got_ref, got, got_sem)
    acc[...] = jnp.zeros_like(acc)
    sources = scratch[-2].shape[0]
    rows = got_ref.shape[0] // sources
    copy.wait()
    chan = got[pl.ds(size * FIELDS, sources, stride=rows), :]
    end = got[pl.ds(size * FIELDS + 1, sources, stride=rows), :]
    chan_ref[...] = chan
    end_ref[...] = end
    add_emitters(size, 0, per_dest, chan, end, got, acc, *scratch)


def more_kernel(size, first, per_dest, chan_ref, end_ref, got_ref, held_ref, acc, got, got_sem, *scratch):
    copy = fetch(got_ref, got, got_sem)
    acc[...] = held_ref[...]
    copy.wait()
    add_emitters(size, first, per_dest, chan_ref[...], end_ref[...], got, acc, *scratch)


def last_kernel(size, first, per_dest, chan_ref, end_ref, width_ref, got_ref, held_ref, cube, head_ref, tail_ref,
                acc, held_sem, got, got_sem, *scratch):
    held = pltpu.make_async_copy(held_ref, acc, held_sem)
    held.start()
    copy = fetch(got_ref, got, got_sem)
    copy.wait()
    held.wait()
    add_emitters(size, first, per_dest, chan_ref[...], end_ref[...], got, acc, *scratch)
    share = acc.shape[0]

    def one_chan(chan, carry):
        columns = pl.ds(pl.multiple_of(chan * CB, CB), CB)
        smooth(acc.at[chan], width_ref[:, columns], cube, columns)
        return carry

    lax.fori_loop(0, share, one_chan, 0)
    head_ref[...] = cube[:, :CB].T[:EDGE]
    tail_ref[...] = cube[:, (share - 1) * CB :].T[CB - EDGE :]


def smooth(plane_ref, widths, cube_ref, columns):
    decay = (-0.5 * LOG2E) / jnp.square(widths)
    places = lax.broadcasted_iota(jnp.int32, (SIDE, CB), 0).astype(jnp.float32)
    beam = [jnp.exp2(jnp.square(places - float(v)) * decay) for v in range(SIDE)]
    norm = beam[0]
    for v in range(1, SIDE):
        norm = norm + beam[v]
    inverse = 1.0 / norm
    beam = [b * inverse for b in beam]
    half = SIDE // 2
    even, odd = [None] * half, [None] * half
    for v in range(half):
        low = plane_ref[v * SIDE : (v + 1) * SIDE, :]
        high = plane_ref[(SIDE - 1 - v) * SIDE : (SIDE - v) * SIDE, :]
        both, apart = low + high, low - high
        near, far = beam[v][:half], beam[SIDE - 1 - v][:half]
        mean, rest = 0.5 * (near + far), 0.5 * (near - far)
        for x in range(half):
            term_even, term_odd = mean[x : x + 1, :] * both, rest[x : x + 1, :] * apart
            even[x] = term_even if v == 0 else even[x] + term_even
            odd[x] = term_odd if v == 0 else odd[x] + term_odd
    for x in range(SIDE):
        along_x = even[x] + odd[x] if x < half else even[SIDE - 1 - x] - odd[SIDE - 1 - x]
        total = None
        for v in range(SIDE):
            term = beam[v] * along_x[v : v + 1, :]
            total = term if v == 0 else total + term
        cube_ref[x * SIDE : (x + 1) * SIDE, columns] = total


def emitter_scratch(size, got, share):
    sources, rows = got.shape[:2]
    work = size * sources
    return [
        pltpu.VMEM((sources * rows + 8, ROWS), jnp.float32),
        pltpu.SemaphoreType.DMA,
        pltpu.VMEM((share * (work + 2) * 8, ROWS), jnp.float32),
        pltpu.SMEM((3, work // 2 + share + UNROLL), jnp.int32),
        pltpu.VMEM((sources, ROWS), jnp.int32),
        pltpu.SMEM((sources, ROWS), jnp.int32),
        pltpu.SemaphoreType.DMA,
    ]


def flat(got):
    return pltpu.with_memory_space_constraint(got.reshape(-1, ROWS), pltpu.VMEM)


def emitter_cost(size, got):
    work = size * got.shape[0]
    return pl.CostEstimate(
        flops=work * 2 * PIX * CB * ROWS, transcendentals=work * CB * ROWS, bytes_accessed=got.size * 4
    )


def deposit_first(size, per_dest, share, got):
    return pl.pallas_call(
        functools.partial(first_kernel, size, per_dest, share),
        out_shape=[jax.ShapeDtypeStruct((share, PIX, CB), jnp.float32)]
        + [jax.ShapeDtypeStruct((got.shape[0], ROWS), jnp.float32)] * 2,
        in_specs=[ANY],
        out_specs=[VMEM] * 3,
        scratch_shapes=emitter_scratch(size, got, share),
        cost_estimate=emitter_cost(size, got),
        name="deposit_first",
    )(flat(got))


def deposit_more(size, first, per_dest, share, chan, end, got, held):
    return pl.pallas_call(
        functools.partial(more_kernel, size, first, per_dest),
        out_shape=jax.ShapeDtypeStruct((share, PIX, CB), jnp.float32),
        in_specs=[VMEM, VMEM, ANY, VMEM],
        out_specs=VMEM,
        scratch_shapes=emitter_scratch(size, got, share),
        input_output_aliases={3: 0},
        name="deposit_more",
    )(chan, end, flat(got), held)


def deposit_last(size, first, per_dest, share, chan, end, got, held, widths):
    edge = jax.ShapeDtypeStruct((EDGE, PIX), jnp.float32)
    return pl.pallas_call(
        functools.partial(last_kernel, size, first, per_dest),
        out_shape=[jax.ShapeDtypeStruct((PIX, share * CB), jnp.float32), edge, edge],
        in_specs=[VMEM] * 3 + [ANY] * 2,
        out_specs=[VMEM] * 3,
        scratch_shapes=[
            pltpu.VMEM((share, PIX, CB), jnp.float32),
            pltpu.SemaphoreType.DMA,
        ]
        + emitter_scratch(size, got, share),
        cost_estimate=emitter_cost(size, got),
        name="deposit_last",
    )(chan, end, widths.reshape(1, -1), flat(got), held)


def split(values):
    high = values.astype(jnp.bfloat16)
    return high, (values - high.astype(jnp.float32)).astype(jnp.bfloat16)


def times(left, right, dims):
    (left_high, left_low), (right_high, right_low) = left, right

    def dot(a, b):
        return lax.dot_general(a, b, (dims, ((), ())), preferred_element_type=jnp.float32)

    return dot(left_high, right_high) + (dot(left_high, right_low) + dot(left_low, right_high))


def band_part(taps_ref, first, rows):
    shape = (rows, CB)
    apart = lax.broadcasted_iota(jnp.int32, shape, 0) - lax.broadcasted_iota(jnp.int32, shape, 1) + (first + HALF)
    band = jnp.zeros(shape, jnp.float32)
    for k in range(TAPS):
        band = jnp.where(apart == k, taps_ref[k], band)
    return split(band)


def taps_kernel(wide, taps_ref, cube_ref, out_ref, cube, high_ref, low_ref, sem):
    copy = pltpu.make_async_copy(cube_ref, cube, sem)
    copy.start()
    for ref, part in zip((high_ref, low_ref), band_part(taps_ref, -CB, 3 * CB)):
        ref[...] = jnp.zeros_like(ref)
        for i in range(0, wide, CB):
            ref[i : i + 3 * CB, i : i + CB] = part
    copy.wait()
    end = cube.shape[1]
    for start in range(0, end, wide):
        low, high = max(start - CB, 0), min(start + wide + CB, end)
        rows = slice(low - start + CB, high - start + CB)
        out_ref[:, start : start + wide] = times(
            split(cube[:, low:high]), (high_ref[rows], low_ref[rows]), ((1,), (0,))
        )


def sum_taps(taps, cube):
    wide = 2 * CB if cube.shape[1] % (2 * CB) == 0 else CB
    return pl.pallas_call(
        functools.partial(taps_kernel, wide),
        out_shape=jax.ShapeDtypeStruct(cube.shape, jnp.float32),
        in_specs=[SMEM, ANY],
        out_specs=VMEM,
        scratch_shapes=[pltpu.VMEM(cube.shape, jnp.float32)]
        + [pltpu.VMEM((wide + 2 * CB, wide), jnp.bfloat16)] * 2
        + [pltpu.SemaphoreType.DMA],
        cost_estimate=pl.CostEstimate(
            flops=6 * cube.size * (wide + 2 * CB), transcendentals=0, bytes_accessed=cube.size * 8
        ),
        name="taps",
    )(taps, cube)


def edge_kernel(taps_ref, before_ref, after_ref, part_ref, out_ref):
    side = pl.program_id(0)
    slab, last = lax.axis_index("slab"), lax.axis_size("slab") - 1

    @pl.when(side == 0)
    def _():
        edge = jnp.where(slab > 0, before_ref[...], 0.0)
        out_ref[...] = part_ref[...] + times(split(edge), band_part(taps_ref, -EDGE, EDGE), ((0,), (0,)))

    @pl.when(side == 1)
    def _():
        edge = jnp.where(slab < last, after_ref[...], 0.0)
        out_ref[...] = part_ref[...] + times(split(edge), band_part(taps_ref, CB, EDGE), ((0,), (0,)))


def add_edges(taps, before, after, part):
    last = part.shape[1] // CB - 1
    block = pl.BlockSpec((PIX, CB), lambda i: (0, i * last))
    before, after = (pltpu.with_memory_space_constraint(e, pltpu.VMEM) for e in (before, after))
    return pl.pallas_call(
        edge_kernel,
        out_shape=jax.ShapeDtypeStruct(part.shape, jnp.float32),
        grid=(2,),
        in_specs=[SMEM, VMEM, VMEM, block],
        out_specs=block,
        input_output_aliases={3: 0},
        name="edges",
    )(taps, before, after, part)


def body(
    voxel_cell,
    offsets,
    line_center,
    line_width,
    luminosity,
    block_rows,
    block_chan,
    slot_table,
    beam_width,
    spectral_taps,
):
    slab_count = lax.axis_size("slab")
    dest_count = lax.axis_size("tile") * slab_count
    per_dest = slot_table.shape[1] // dest_count
    share = NCB // slab_count
    sizes = chunk_sizes(per_dest)

    def packed(wanted):
        return pack(
            sizes, wanted, dest_count, slab_count, share, slot_table, block_rows, block_chan,
            voxel_cell, offsets, line_center, line_width, luminosity,
        )

    sent = packed((0, 1))
    def exchange(piece):
        return lax.all_to_all(piece, ("tile", "slab"), split_axis=0, concat_axis=0, tiled=True)

    got_first = exchange(sent[0])
    got_first, last_piece = lax.optimization_barrier((got_first, sent[1]))
    got_last = exchange(last_piece)
    held, chan, end = deposit_first(sizes[0], per_dest, share, got_first)
    reach = sizes[0] + sizes[1]
    if len(sizes) > 2:
        longest = jnp.max(chan[:, ROWS - 1])
        held, got_last = lax.optimization_barrier((held, got_last))
        held = lax.cond(
            longest > float(reach * ROWS),
            lambda held: deposit_more(sizes[2], reach, per_dest, share, chan, end, exchange(packed((2,))[0]), held),
            lambda held: held,
            held,
        )
    cube, head, tail = deposit_last(
        sizes[1], sizes[0], per_dest, share, chan, end, got_last, held, beam_width
    )
    before = lax.ppermute(tail, "slab", [(i, (i + 1) % slab_count) for i in range(slab_count)])
    after = lax.ppermute(head, "slab", [((i + 1) % slab_count, i) for i in range(slab_count)])
    return add_edges(spectral_taps, before, after, sum_taps(spectral_taps, cube))[None]


def solution(mesh):
    placed = (
        P(("tile", "slab"), None),
        P(("tile", "slab"), None, None),
        P(("tile", "slab"), None),
        P(("tile", "slab"), None),
        P(("tile", "slab"), None),
        P(("tile", "slab")),
        P(("tile", "slab")),
        P(("tile", "slab"), None),
        P("slab"),
        P(),
    )
    return jax.shard_map(
        body, mesh=mesh, in_specs=placed, out_specs=P("tile", None, "slab"), check_vma=False
    )
```

```python
import functools
import math

import jax
import jax.numpy as jnp
from jax import lax
from jax.experimental import pallas as pl
from jax.experimental.pallas import tpu as pltpu
from jax.sharding import PartitionSpec as P

SIDE = 16
PIX = SIDE * SIDE
CB = 128
ROWS = 128
TAPS = 31
HALF = 15
EDGE = 16
NCB = 32
FIELDS = 6
UNROLL = 6
SKIP = 8
LOG2E = math.log2(math.e)
SMEM = pl.BlockSpec(memory_space=pltpu.SMEM)
VMEM = pl.BlockSpec(memory_space=pltpu.VMEM)
ANY = pl.BlockSpec(memory_space=pl.ANY)


def chunk_sizes(per_dest):
    early = late = max(per_dest * 9 // 24, 1)
    sizes = [early, late, per_dest - early - late]
    return [size for size in sizes if size > 0]


def padded_rows(rows):
    return -(-rows // 8) * 8


def pack_kernel(sizes, wanted, slab_count, share, slot_ref, count_ref, chan_ref, cell_ref, offset_ref, center_ref,
                width_ref, lum_ref, *refs):
    outs = dict(zip(wanted, refs))
    props, stream, slots, counts, chans, plan, moves, sem = refs[len(wanted) :]
    dest_count = slots.shape[0]
    per_dest = sum(sizes)
    block_total = cell_ref.shape[0]
    lane = lax.broadcasted_iota(jnp.int32, (dest_count, ROWS), 1)

    slot_row = slot_ref[...]
    blocks = lax.broadcasted_iota(jnp.int32, (block_total, slot_row.shape[1]), 0)
    chosen = jnp.where(blocks == slot_row, 1.0, 0.0).astype(jnp.bfloat16)
    table = jnp.concatenate([count_ref[...].reshape(1, -1), chan_ref[...].reshape(1, -1)], axis=0).astype(jnp.float32).astype(jnp.bfloat16)
    looked = jnp.dot(table, chosen, preferred_element_type=jnp.float32)
    slots[...] = jnp.zeros_like(slots)
    counts[...] = jnp.zeros_like(counts)
    chans[...] = jnp.zeros_like(chans)
    for dest in range(dest_count):
        columns = slice(dest * per_dest, (dest + 1) * per_dest)
        slots[dest : dest + 1, :per_dest] = slot_row[:, columns]
        counts[dest : dest + 1, :per_dest] = looked[0:1, columns]
        chans[dest : dest + 1, :per_dest] = looked[1:2, columns]
    count = counts[...]
    until = jnp.dot(count.astype(jnp.bfloat16), exclusive(ROWS), preferred_element_type=jnp.float32)
    end = until + count
    start = until.astype(jnp.int32)
    orders = jnp.zeros(lane.shape, jnp.int32)
    for values in ((start >> 7) * 8, start & (ROWS - 1), jnp.maximum(slots[...], 0) * 8):
        orders = jnp.where(lane < per_dest, values, pltpu.roll(orders, per_dest, 1))
    plan[...] = orders
    copy = pltpu.make_async_copy(plan, moves, sem)
    copy.start()

    if 0 in outs:
        rows = outs[0].shape[0] // dest_count
        dests = lax.broadcasted_iota(jnp.int32, lane.shape, 0)
        chan = chans[...] - (lax.rem(dests, slab_count) * share).astype(jnp.float32)
        longest = jnp.max(jnp.max(end, axis=0, keepdims=True), axis=1, keepdims=True)
        meta = sizes[0] * FIELDS
        outs[0][pl.ds(meta, dest_count, stride=rows), :] = jnp.where(lane == ROWS - 1, longest, chan)
        outs[0][pl.ds(meta + 1, dest_count, stride=rows), :] = end

    def gather_fields(tile, carry):
        first = pl.multiple_of(tile * 8, 8)
        here = pl.ds(first, 8)
        fields = (
            cell_ref[here, :].astype(jnp.float32),
            offset_ref[pl.ds(2 * first, 8, stride=2), :],
            offset_ref[pl.ds(2 * first + 1, 8, stride=2), :],
            center_ref[here, :],
            (-0.5 * LOG2E) / jnp.square(width_ref[here, :]),
            lum_ref[here, :].astype(jnp.bfloat16).astype(jnp.float32),
        )
        for field, values in enumerate(fields):
            props[pl.ds(8 * first + field, 8, stride=8), :] = values
        return carry

    lax.fori_loop(0, block_total // 8, gather_fields, 0, unroll=2)
    copy.wait()
    lanes = lax.broadcasted_iota(jnp.int32, (8, ROWS), 1)

    def one_dest(dest, carry):
        for slot in range(per_dest):
            row, shift, target = (moves[dest, k * per_dest + slot] for k in range(3))
            row, target = pl.multiple_of(row, 8), pl.multiple_of(target, 8)
            turned = pltpu.roll(props[pl.ds(row, 8), :], shift, 1)
            pltpu.store(stream.at[pl.ds(target, 8), :], turned, mask=lanes >= shift)
            stream[pl.ds(target + 8, 8), :] = turned
        group = 0
        for part, size in enumerate(sizes):
            if part in outs:
                out = outs[part]
                base = pl.multiple_of(dest * (out.shape[0] // dest_count), 8)
                for place in range(size):
                    out[pl.ds(base + place * FIELDS, FIELDS), :] = stream[8 * (group + place) : 8 * (group + place) + FIELDS, :]
            group += size
        return carry

    lax.fori_loop(0, dest_count, one_dest, 0)


def pack(sizes, wanted, dest_count, slab_count, share, slot_list, counts, chans, cells, offsets, centers, widths, lums):
    rows = [padded_rows(size * FIELDS + (2 if part == 0 else 0)) for part, size in enumerate(sizes)]
    block_total = cells.shape[0]
    sent = pl.pallas_call(
        functools.partial(pack_kernel, sizes, wanted, slab_count, share),
        out_shape=[jax.ShapeDtypeStruct((dest_count * rows[part], ROWS), jnp.float32) for part in wanted],
        in_specs=[VMEM] * 8,
        out_specs=[VMEM] * len(wanted),
        scratch_shapes=[
            pltpu.VMEM((block_total * 8, ROWS), jnp.float32),
            pltpu.VMEM(((sum(sizes) + 2) * 8, ROWS), jnp.float32),
            pltpu.VMEM((dest_count, ROWS), jnp.int32),
            pltpu.VMEM((dest_count, ROWS), jnp.float32),
            pltpu.VMEM((dest_count, ROWS), jnp.float32),
            pltpu.VMEM((dest_count, ROWS), jnp.int32),
            pltpu.SMEM((dest_count, ROWS), jnp.int32),
            pltpu.SemaphoreType.DMA,
        ],
        name="pack",
    )(
        slot_list, counts, chans, cells,
        offsets.reshape(block_total * 2, ROWS), centers, widths, lums,
    )
    return [piece.reshape(dest_count, rows[part], ROWS) for part, piece in zip(wanted, sent)]


def exclusive(size):
    before = lax.broadcasted_iota(jnp.int32, (size, size), 0)
    return (before < lax.broadcasted_iota(jnp.int32, (size, size), 1)).astype(jnp.bfloat16)


def plan_moves(size, first, per_dest, share, stride, rows, chan, end, plan):
    sources = chan.shape[0]
    lane = lax.broadcasted_iota(jnp.int32, chan.shape, 1)
    low, high = float(first * ROWS), float((first + size) * ROWS)
    start = jnp.where(lane == 0, 0.0, pltpu.roll(end, 1, 1))
    begin = jnp.clip(start, low, high) - low
    count = jnp.where(lane < per_dest, jnp.clip(end, low, high) - low - begin, 0.0)
    chan = jnp.where(count > 0.0, chan, 0.0)
    across = exclusive(ROWS)
    down = exclusive(sources)
    filled = jnp.zeros(chan.shape, jnp.float32)
    totals = jnp.zeros(chan.shape, jnp.float32)
    for c in range(share):
        own = jnp.where(chan == float(c), count, 0.0)
        moved = own.astype(jnp.bfloat16)
        here = jnp.dot(moved, across, preferred_element_type=jnp.float32)
        above = lax.dot_general(down, moved, (((0,), (0,)), ((), ())), preferred_element_type=jnp.float32)
        above = jnp.sum(above, axis=1, keepdims=True) + float(c * stride * ROWS)
        filled = filled + jnp.where(chan == float(c), here + above, 0.0)
        total = jnp.sum(jnp.sum(own, axis=0, keepdims=True), axis=1, keepdims=True)
        totals = totals + jnp.where(lane == c, total, 0.0)
    for start in range(0, per_dest, SKIP):
        inside = (lane >= start) & (lane < start + SKIP)
        total = jnp.sum(jnp.where(inside, count, 0.0), axis=1, keepdims=True)
        totals = totals + jnp.where(lane == share + start // SKIP, total, 0.0)
    filled = filled.astype(jnp.int32)
    begin = begin.astype(jnp.int32)
    base = lax.broadcasted_iota(jnp.int32, chan.shape, 0) * rows
    group = jnp.minimum(begin >> 7, size - 1)
    table = totals.astype(jnp.int32)
    for values in ((filled >> 7) * 8, (filled - begin) & (ROWS - 1), begin & (ROWS - 1), base + group * FIELDS):
        table = jnp.where(lane < per_dest, values, pltpu.roll(table, per_dest, 1))
    plan[...] = table


def add_emitters(size, first, per_dest, chan, end, got, acc, streams, todo, plan, moves, sem, ready=()):
    source_count = chan.shape[0]
    share = acc.shape[0]
    stride = streams.shape[0] // (8 * share)
    lane = lax.broadcasted_iota(jnp.int32, (FIELDS, ROWS), 1)
    plan_moves(size, first, per_dest, share, stride, (got.shape[0] - 8) // source_count, chan, end, plan)
    copy = pltpu.make_async_copy(plan, moves, sem)
    copy.start()
    copy.wait()
    for other in ready:
        other.wait()

    def move(source, places):
        for place in places:
            row, begin, turn, target = (moves[source, k * per_dest + place] for k in range(4))
            target = pl.multiple_of(target, 8)
            here = got[pl.ds(row, FIELDS), :]
            there = got[pl.ds(row + FIELDS, FIELDS), :]
            filled = (jnp.full(lane.shape, begin, jnp.int32) + turn) & (ROWS - 1)
            whole = pltpu.roll(jnp.where(lane >= begin, here, there), turn, 1)
            pltpu.store(streams.at[pl.ds(target, FIELDS), :], whole, mask=lane >= filled)
            streams[pl.ds(target + 8, FIELDS), :] = whole

    def append(source, carry):
        if first == 0:
            move(source, range(per_dest))
        for start in range(0, 0 if first == 0 else per_dest, SKIP):
            places = range(start, min(start + SKIP, per_dest))
            live = moves[source, 4 * per_dest + share + start // SKIP]
            pl.when(live > 0)(functools.partial(move, source, places))
        return carry

    lax.fori_loop(0, source_count, append, 0)

    def list_chan(chan, count):
        total = moves[0, 4 * per_dest + chan]

        def list_pair(pair, at):
            todo[0, at] = chan
            todo[1, at] = chan * stride + 2 * pair
            todo[2, at] = total - 2 * ROWS * pair
            return at + 1

        return lax.fori_loop(0, (total + 2 * ROWS - 1) >> 8, list_pair, count)

    pair_count = lax.fori_loop(0, share, list_chan, 0)
    for extra in range(UNROLL - 1):
        todo[0, pair_count + extra] = 0
        todo[1, pair_count + extra] = 0
        todo[2, pair_count + extra] = 0

    place16 = lax.broadcasted_iota(jnp.int32, (SIDE, ROWS), 0).astype(jnp.float32)
    place8 = lax.broadcasted_iota(jnp.int32, (8, ROWS), 0).astype(jnp.float32) + 0.5

    def hat(cell, frac):
        apart = place16 - cell
        return jnp.where(apart == 0.0, 1.0 - frac, jnp.where(apart == 1.0, frac, 0.0))

    def factors(group, left):
        props = jnp.where(lane < left, streams[pl.ds(pl.multiple_of(group * 8, 8), FIELDS), :], 0.0)
        cell, frac_x, frac_y, center, decay, bright = (props[f : f + 1, :] for f in range(FIELDS))
        cell_x = jnp.floor(cell * (1.0 / SIDE))
        weight_x = hat(cell_x, frac_x)
        weight_y = hat(cell - SIDE * cell_x, frac_y)
        spread = jnp.concatenate(
            [(weight_x[x : x + 1, :] * weight_y).astype(jnp.bfloat16) for x in range(SIDE)], axis=0
        )
        apart = place8 - center
        profile = [jnp.exp2(jnp.square(apart + 8.0 * i) * decay) for i in range(CB // 8)]
        total = profile[0]
        for part in profile[1:]:
            total = total + part
        scale = bright / jnp.sum(total, axis=0, keepdims=True)
        line = jnp.concatenate(profile, axis=0) * scale
        return spread, line.astype(jnp.bfloat16)

    def some_pairs(turn, carry):
        for step in range(UNROLL):
            at = turn * UNROLL + step
            chan, group, left = todo[0, at], todo[1, at], todo[2, at]
            spread_0, line_0 = factors(group, left)
            spread_1, line_1 = factors(group + 1, left - ROWS)
            acc[chan] += lax.dot_general(
                jnp.concatenate([spread_0, spread_1], axis=1),
                jnp.concatenate([line_0, line_1], axis=1),
                (((1,), (1,)), ((), ())),
                preferred_element_type=jnp.float32,
            )
        return carry

    lax.fori_loop(0, (pair_count + UNROLL - 1) // UNROLL, some_pairs, 0)


def fetch(got_ref, got, sem):
    copy = pltpu.make_async_copy(got_ref, got.at[pl.ds(0, got_ref.shape[0])], sem)
    copy.start()
    return copy


def first_kernel(size, per_dest, share, got_ref, acc, chan_ref, end_ref, got, got_sem, *scratch):
    copy = fetch(got_ref, got, got_sem)
    acc[...] = jnp.zeros_like(acc)
    sources = scratch[-2].shape[0]
    rows = got_ref.shape[0] // sources
    copy.wait()
    chan = got[pl.ds(size * FIELDS, sources, stride=rows), :]
    end = got[pl.ds(size * FIELDS + 1, sources, stride=rows), :]
    chan_ref[...] = chan
    end_ref[...] = end
    add_emitters(size, 0, per_dest, chan, end, got, acc, *scratch)


def more_kernel(size, first, per_dest, chan_ref, end_ref, got_ref, held_ref, acc, got, got_sem, *scratch):
    copy = fetch(got_ref, got, got_sem)
    acc[...] = held_ref[...]
    copy.wait()
    add_emitters(size, first, per_dest, chan_ref[...], end_ref[...], got, acc, *scratch)


def last_kernel(size, first, per_dest, chan_ref, end_ref, width_ref, got_ref, held_ref, cube, near_ref, far_ref,
                acc, held_sem, got, got_sem, *scratch):
    held = pltpu.make_async_copy(held_ref, acc, held_sem)
    held.start()
    copy = fetch(got_ref, got, got_sem)
    add_emitters(size, first, per_dest, chan_ref[...], end_ref[...], got, acc, *scratch, ready=(copy, held))
    share = acc.shape[0]

    def one_chan(chan, carry):
        columns = pl.ds(pl.multiple_of(chan * CB, CB), CB)
        smooth(acc.at[chan], width_ref[:, columns], cube, columns)
        return carry

    lax.fori_loop(0, share, one_chan, 0)
    even = lax.rem(lax.axis_index("slab"), 2) == 0
    head = cube[:, :CB].T[:EDGE]
    tail = cube[:, (share - 1) * CB :].T[CB - EDGE :]
    near_ref[...] = jnp.where(even, tail, head)
    far_ref[...] = jnp.where(even, head, tail)


def smooth(plane_ref, widths, cube_ref, columns):
    decay = (-0.5 * LOG2E) / jnp.square(widths)
    places = lax.broadcasted_iota(jnp.int32, (SIDE, CB), 0).astype(jnp.float32)
    beam = [jnp.exp2(jnp.square(places - float(v)) * decay) for v in range(SIDE)]
    norm = beam[0]
    for v in range(1, SIDE):
        norm = norm + beam[v]
    inverse = 1.0 / norm
    beam = [b * inverse for b in beam]
    half = SIDE // 2
    even, odd = [None] * half, [None] * half
    for v in range(half):
        low = plane_ref[v * SIDE : (v + 1) * SIDE, :]
        high = plane_ref[(SIDE - 1 - v) * SIDE : (SIDE - v) * SIDE, :]
        both, apart = low + high, low - high
        near, far = beam[v][:half], beam[SIDE - 1 - v][:half]
        mean, rest = 0.5 * (near + far), 0.5 * (near - far)
        for x in range(half):
            term_even, term_odd = mean[x : x + 1, :] * both, rest[x : x + 1, :] * apart
            even[x] = term_even if v == 0 else even[x] + term_even
            odd[x] = term_odd if v == 0 else odd[x] + term_odd
    for x in range(SIDE):
        along_x = even[x] + odd[x] if x < half else even[SIDE - 1 - x] - odd[SIDE - 1 - x]
        total = None
        for v in range(SIDE):
            term = beam[v] * along_x[v : v + 1, :]
            total = term if v == 0 else total + term
        cube_ref[x * SIDE : (x + 1) * SIDE, columns] = total


def emitter_scratch(size, got, share):
    sources, rows = got.shape[:2]
    work = size * sources
    return [
        pltpu.VMEM((sources * rows + 8, ROWS), jnp.float32),
        pltpu.SemaphoreType.DMA,
        pltpu.VMEM((share * (work + 2) * 8, ROWS), jnp.float32),
        pltpu.SMEM((3, work // 2 + share + UNROLL), jnp.int32),
        pltpu.VMEM((sources, ROWS), jnp.int32),
        pltpu.SMEM((sources, ROWS), jnp.int32),
        pltpu.SemaphoreType.DMA,
    ]


def flat(got):
    return pltpu.with_memory_space_constraint(got.reshape(-1, ROWS), pltpu.VMEM)


def emitter_cost(size, got):
    work = size * got.shape[0]
    return pl.CostEstimate(
        flops=work * 2 * PIX * CB * ROWS, transcendentals=work * CB * ROWS, bytes_accessed=got.size * 4
    )


def deposit_first(size, per_dest, share, got):
    return pl.pallas_call(
        functools.partial(first_kernel, size, per_dest, share),
        out_shape=[jax.ShapeDtypeStruct((share, PIX, CB), jnp.float32)]
        + [jax.ShapeDtypeStruct((got.shape[0], ROWS), jnp.float32)] * 2,
        in_specs=[ANY],
        out_specs=[VMEM] * 3,
        scratch_shapes=emitter_scratch(size, got, share),
        cost_estimate=emitter_cost(size, got),
        name="deposit_first",
    )(flat(got))


def deposit_more(size, first, per_dest, share, chan, end, got, held):
    return pl.pallas_call(
        functools.partial(more_kernel, size, first, per_dest),
        out_shape=jax.ShapeDtypeStruct((share, PIX, CB), jnp.float32),
        in_specs=[VMEM, VMEM, ANY, VMEM],
        out_specs=VMEM,
        scratch_shapes=emitter_scratch(size, got, share),
        input_output_aliases={3: 0},
        name="deposit_more",
    )(chan, end, flat(got), held)


def deposit_last(size, first, per_dest, share, chan, end, got, held, widths):
    edge = jax.ShapeDtypeStruct((EDGE, PIX), jnp.float32)
    return pl.pallas_call(
        functools.partial(last_kernel, size, first, per_dest),
        out_shape=[jax.ShapeDtypeStruct((PIX, share * CB), jnp.float32), edge, edge],
        in_specs=[VMEM] * 3 + [ANY] * 2,
        out_specs=[VMEM] * 3,
        scratch_shapes=[
            pltpu.VMEM((share, PIX, CB), jnp.float32),
            pltpu.SemaphoreType.DMA,
        ]
        + emitter_scratch(size, got, share),
        cost_estimate=emitter_cost(size, got),
        name="deposit_last",
    )(chan, end, widths.reshape(1, -1), flat(got), held)


def split(values):
    high = values.astype(jnp.bfloat16)
    return high, (values - high.astype(jnp.float32)).astype(jnp.bfloat16)


def times(left, right, dims):
    (left_high, left_low), (right_high, right_low) = left, right

    def dot(a, b):
        return lax.dot_general(a, b, (dims, ((), ())), preferred_element_type=jnp.float32)

    return dot(left_high, right_high) + (dot(left_high, right_low) + dot(left_low, right_high))


def band_part(taps_ref, first, rows):
    shape = (rows, CB)
    apart = lax.broadcasted_iota(jnp.int32, shape, 0) - lax.broadcasted_iota(jnp.int32, shape, 1) + (first + HALF)
    band = jnp.zeros(shape, jnp.float32)
    for k in range(TAPS):
        band = jnp.where(apart == k, taps_ref[k], band)
    return split(band)


def taps_kernel(wide, taps_ref, cube_hbm, near_ref, far_ref, out_ref, cube_ref, out, high_ref, low_ref, sem, sems):
    fetched = pltpu.make_async_copy(cube_hbm, cube_ref, sem)
    fetched.start()
    slab, last = lax.axis_index("slab"), lax.axis_size("slab") - 1
    even = lax.rem(slab, 2) == 0
    for ref, part in zip((high_ref, low_ref), band_part(taps_ref, -CB, 3 * CB)):
        ref[...] = jnp.zeros_like(ref)
        for i in range(0, wide, CB):
            ref[i : i + 3 * CB, i : i + CB] = part
    end = cube_ref.shape[1]
    copies = []
    fetched.wait()
    for start in range(0, end, wide):
        low, high = max(start - CB, 0), min(start + wide + CB, end)
        rows, columns = slice(low - start + CB, high - start + CB), slice(start, start + wide)
        out[:, columns] = times(split(cube_ref[:, low:high]), (high_ref[rows], low_ref[rows]), ((1,), (0,)))
        if start == 0:
            edge = jnp.where(slab > 0, jnp.where(even, far_ref[...], near_ref[...]), 0.0)
            out[:, :CB] += times(split(edge), band_part(taps_ref, -EDGE, EDGE), ((0,), (0,)))
        if start + wide == end:
            edge = jnp.where(slab < last, jnp.where(even, near_ref[...], far_ref[...]), 0.0)
            out[:, end - CB :] += times(split(edge), band_part(taps_ref, CB, EDGE), ((0,), (0,)))
        copies.append(pltpu.make_async_copy(out.at[:, columns], out_ref.at[:, columns], sems.at[start // wide]))
        copies[-1].start()
    for copy in copies:
        copy.wait()


def sum_taps(taps, cube, near, far):
    wide = 2 * CB if cube.shape[1] % (2 * CB) == 0 else CB
    near, far = (pltpu.with_memory_space_constraint(x, pltpu.VMEM) for x in (near, far))
    return pl.pallas_call(
        functools.partial(taps_kernel, wide),
        out_shape=jax.ShapeDtypeStruct(cube.shape, jnp.float32),
        in_specs=[SMEM, ANY, VMEM, VMEM],
        out_specs=ANY,
        scratch_shapes=[pltpu.VMEM(cube.shape, jnp.float32)] * 2
        + [pltpu.VMEM((wide + 2 * CB, wide), jnp.bfloat16)] * 2
        + [pltpu.SemaphoreType.DMA, pltpu.SemaphoreType.DMA((cube.shape[1] // wide,))],
        name="taps",
    )(taps, cube, near, far)


def body(
    voxel_cell,
    offsets,
    line_center,
    line_width,
    luminosity,
    block_rows,
    block_chan,
    slot_table,
    beam_width,
    spectral_taps,
):
    slab_count = lax.axis_size("slab")
    dest_count = lax.axis_size("tile") * slab_count
    per_dest = slot_table.shape[1] // dest_count
    share = NCB // slab_count
    sizes = chunk_sizes(per_dest)

    def packed(wanted):
        return pack(
            sizes, wanted, dest_count, slab_count, share, slot_table, block_rows, block_chan,
            voxel_cell, offsets, line_center, line_width, luminosity,
        )

    sent = packed((0, 1))
    def exchange(piece):
        return lax.all_to_all(piece, ("tile", "slab"), split_axis=0, concat_axis=0, tiled=True)

    got_first = exchange(sent[0])
    got_first, last_piece = lax.optimization_barrier((got_first, sent[1]))
    got_last = exchange(last_piece)
    held, chan, end = deposit_first(sizes[0], per_dest, share, got_first)
    reach = sizes[0] + sizes[1]
    if len(sizes) > 2:
        longest = jnp.max(chan[:, ROWS - 1])
        held, got_last = lax.optimization_barrier((held, got_last))
        held = lax.cond(
            longest > float(reach * ROWS),
            lambda held: deposit_more(sizes[2], reach, per_dest, share, chan, end, exchange(packed((2,))[0]), held),
            lambda held: held,
            held,
        )
    cube, near, far = deposit_last(
        sizes[1], sizes[0], per_dest, share, chan, end, got_last, held, beam_width
    )
    near = lax.ppermute(near, "slab", [(i, i ^ 1) for i in range(slab_count)])
    far = lax.ppermute(far, "slab", [(i, (i + 1 if i % 2 else i - 1) % slab_count) for i in range(slab_count)])
    return sum_taps(spectral_taps, cube, near, far)[None]


def solution(mesh):
    placed = (
        P(("tile", "slab"), None),
        P(("tile", "slab"), None, None),
        P(("tile", "slab"), None),
        P(("tile", "slab"), None),
        P(("tile", "slab"), None),
        P(("tile", "slab")),
        P(("tile", "slab")),
        P(("tile", "slab"), None),
        P("slab"),
        P(),
    )
    return jax.shard_map(
        body, mesh=mesh, in_specs=placed, out_specs=P("tile", None, "slab"), check_vma=False
    )
```

```python
import functools
import math

import jax
import jax.numpy as jnp
from jax import lax
from jax.experimental import pallas as pl
from jax.experimental.pallas import tpu as pltpu
from jax.sharding import PartitionSpec as P

SIDE = 16
PIX = SIDE * SIDE
CB = 128
ROWS = 128
TAPS = 31
HALF = 15
EDGE = 16
NCB = 32
FIELDS = 6
UNROLL = 6
SKIP = 8
LOG2E = math.log2(math.e)
SMEM = pl.BlockSpec(memory_space=pltpu.SMEM)
VMEM = pl.BlockSpec(memory_space=pltpu.VMEM)
ANY = pl.BlockSpec(memory_space=pl.ANY)


def chunk_sizes(per_dest):
    early = late = max(per_dest * 9 // 24, 1)
    sizes = [early, late, per_dest - early - late]
    return [size for size in sizes if size > 0]


def padded_rows(rows):
    return -(-rows // 8) * 8


def pack_kernel(sizes, wanted, slab_count, share, slot_ref, count_ref, chan_ref, *refs):
    inputs, refs = refs[:5], refs[5:]
    sent, refs = refs[: len(wanted)], refs[len(wanted) :]
    staged, refs = refs[: len(wanted)], refs[len(wanted) :]
    props, stream, slots, counts, chans, plan, moves, sem = refs[:8]
    refs = refs[8:]
    (cell_ref, offset_ref, center_ref, width_ref, lum_ref), in_sem = refs[:5], refs[5]
    out_sems = refs[6:]
    outs = dict(zip(wanted, staged))
    fetches = [pltpu.make_async_copy(a, b, in_sem.at[i]) for i, (a, b) in enumerate(zip(inputs, refs[:5]))]
    for fetch_in in fetches:
        fetch_in.start()
    dest_count = slots.shape[0]
    per_dest = sum(sizes)
    block_total = cell_ref.shape[0]
    lane = lax.broadcasted_iota(jnp.int32, (dest_count, ROWS), 1)

    slot_row = slot_ref[...]
    blocks = lax.broadcasted_iota(jnp.int32, (block_total, slot_row.shape[1]), 0)
    chosen = jnp.where(blocks == slot_row, 1.0, 0.0).astype(jnp.bfloat16)
    table = jnp.concatenate([count_ref[...].reshape(1, -1), chan_ref[...].reshape(1, -1)], axis=0).astype(jnp.float32).astype(jnp.bfloat16)
    looked = jnp.dot(table, chosen, preferred_element_type=jnp.float32)
    slots[...] = jnp.zeros_like(slots)
    counts[...] = jnp.zeros_like(counts)
    chans[...] = jnp.zeros_like(chans)
    for dest in range(dest_count):
        columns = slice(dest * per_dest, (dest + 1) * per_dest)
        slots[dest : dest + 1, :per_dest] = slot_row[:, columns]
        counts[dest : dest + 1, :per_dest] = looked[0:1, columns]
        chans[dest : dest + 1, :per_dest] = looked[1:2, columns]
    count = counts[...]
    until = jnp.dot(count.astype(jnp.bfloat16), exclusive(ROWS), preferred_element_type=jnp.float32)
    end = until + count
    start = until.astype(jnp.int32)
    orders = jnp.zeros(lane.shape, jnp.int32)
    for values in ((start >> 7) * 8, start & (ROWS - 1), jnp.maximum(slots[...], 0) * 8):
        orders = jnp.where(lane < per_dest, values, pltpu.roll(orders, per_dest, 1))
    plan[...] = orders
    copy = pltpu.make_async_copy(plan, moves, sem)
    copy.start()

    if 0 in outs:
        rows = outs[0].shape[0] // dest_count
        dests = lax.broadcasted_iota(jnp.int32, lane.shape, 0)
        chan = chans[...] - (lax.rem(dests, slab_count) * share).astype(jnp.float32)
        longest = jnp.max(jnp.max(end, axis=0, keepdims=True), axis=1, keepdims=True)
        meta = sizes[0] * FIELDS
        outs[0][pl.ds(meta, dest_count, stride=rows), :] = jnp.where(lane == ROWS - 1, longest, chan)
        outs[0][pl.ds(meta + 1, dest_count, stride=rows), :] = end

    def gather_fields(tile, carry):
        first = pl.multiple_of(tile * 8, 8)
        here = pl.ds(first, 8)
        fields = (
            cell_ref[here, :].astype(jnp.float32),
            offset_ref[pl.ds(2 * first, 8, stride=2), :],
            offset_ref[pl.ds(2 * first + 1, 8, stride=2), :],
            center_ref[here, :],
            (-0.5 * LOG2E) / jnp.square(width_ref[here, :]),
            lum_ref[here, :].astype(jnp.bfloat16).astype(jnp.float32),
        )
        for field, values in enumerate(fields):
            props[pl.ds(8 * first + field, 8, stride=8), :] = values
        return carry

    for fetch_in in fetches:
        fetch_in.wait()
    lax.fori_loop(0, block_total // 8, gather_fields, 0, unroll=2)
    copy.wait()

    def send(dest):
        for out, whole, out_sem in zip(staged, sent, out_sems):
            rows = out.shape[0] // dest_count
            here = pl.ds(pl.multiple_of(dest * rows, 8), rows)
            pltpu.make_async_copy(out.at[here], whole.at[here], out_sem).start()

    lanes = lax.broadcasted_iota(jnp.int32, (8, ROWS), 1)

    def one_dest(dest, carry):
        pl.when(dest > 0)(lambda: send(dest - 1))
        for slot in range(per_dest):
            row, shift, target = (moves[dest, k * per_dest + slot] for k in range(3))
            row, target = pl.multiple_of(row, 8), pl.multiple_of(target, 8)
            turned = pltpu.roll(props[pl.ds(row, 8), :], shift, 1)
            pltpu.store(stream.at[pl.ds(target, 8), :], turned, mask=lanes >= shift)
            stream[pl.ds(target + 8, 8), :] = turned
        group = 0
        for part, size in enumerate(sizes):
            if part in outs:
                out = outs[part]
                base = pl.multiple_of(dest * (out.shape[0] // dest_count), 8)
                for place in range(size):
                    out[pl.ds(base + place * FIELDS, FIELDS), :] = stream[8 * (group + place) : 8 * (group + place) + FIELDS, :]
            group += size
        return carry

    lax.fori_loop(0, dest_count, one_dest, 0)
    send(dest_count - 1)
    for out, whole, out_sem in zip(staged, sent, out_sems):
        pltpu.make_async_copy(out, whole, out_sem).wait()


def pack(sizes, wanted, dest_count, slab_count, share, slot_list, counts, chans, cells, offsets, centers, widths, lums):
    rows = [padded_rows(size * FIELDS + (2 if part == 0 else 0)) for part, size in enumerate(sizes)]
    block_total = cells.shape[0]
    lists = (cells, offsets.reshape(block_total * 2, ROWS), centers, widths, lums)
    shapes = [(dest_count * rows[part], ROWS) for part in wanted]
    sent = pl.pallas_call(
        functools.partial(pack_kernel, sizes, wanted, slab_count, share),
        out_shape=[jax.ShapeDtypeStruct(shape, jnp.float32) for shape in shapes],
        in_specs=[VMEM] * 3 + [ANY] * 5,
        out_specs=[ANY] * len(wanted),
        scratch_shapes=[pltpu.VMEM(shape, jnp.float32) for shape in shapes]
        + [
            pltpu.VMEM((block_total * 8, ROWS), jnp.float32),
            pltpu.VMEM(((sum(sizes) + 2) * 8, ROWS), jnp.float32),
            pltpu.VMEM((dest_count, ROWS), jnp.int32),
            pltpu.VMEM((dest_count, ROWS), jnp.float32),
            pltpu.VMEM((dest_count, ROWS), jnp.float32),
            pltpu.VMEM((dest_count, ROWS), jnp.int32),
            pltpu.SMEM((dest_count, ROWS), jnp.int32),
            pltpu.SemaphoreType.DMA,
        ]
        + [pltpu.VMEM(values.shape, values.dtype) for values in lists]
        + [pltpu.SemaphoreType.DMA((5,))]
        + [pltpu.SemaphoreType.DMA] * len(wanted),
        name="pack",
    )(slot_list, counts, chans, *lists)
    return [piece.reshape(dest_count, rows[part], ROWS) for part, piece in zip(wanted, sent)]


def exclusive(size):
    before = lax.broadcasted_iota(jnp.int32, (size, size), 0)
    return (before < lax.broadcasted_iota(jnp.int32, (size, size), 1)).astype(jnp.bfloat16)


def plan_moves(size, first, per_dest, share, stride, rows, chan, end, plan):
    sources = chan.shape[0]
    lane = lax.broadcasted_iota(jnp.int32, chan.shape, 1)
    low, high = float(first * ROWS), float((first + size) * ROWS)
    start = jnp.where(lane == 0, 0.0, pltpu.roll(end, 1, 1))
    begin = jnp.clip(start, low, high) - low
    count = jnp.where(lane < per_dest, jnp.clip(end, low, high) - low - begin, 0.0)
    chan = jnp.where(count > 0.0, chan, 0.0)
    across = exclusive(ROWS)
    down = exclusive(sources)
    filled = jnp.zeros(chan.shape, jnp.float32)
    totals = jnp.zeros(chan.shape, jnp.float32)
    for c in range(share):
        own = jnp.where(chan == float(c), count, 0.0)
        moved = own.astype(jnp.bfloat16)
        here = jnp.dot(moved, across, preferred_element_type=jnp.float32)
        above = lax.dot_general(down, moved, (((0,), (0,)), ((), ())), preferred_element_type=jnp.float32)
        above = jnp.sum(above, axis=1, keepdims=True) + float(c * stride * ROWS)
        filled = filled + jnp.where(chan == float(c), here + above, 0.0)
        total = jnp.sum(jnp.sum(own, axis=0, keepdims=True), axis=1, keepdims=True)
        totals = totals + jnp.where(lane == c, total, 0.0)
    for start in range(0, per_dest, SKIP):
        inside = (lane >= start) & (lane < start + SKIP)
        total = jnp.sum(jnp.where(inside, count, 0.0), axis=1, keepdims=True)
        totals = totals + jnp.where(lane == share + start // SKIP, total, 0.0)
    filled = filled.astype(jnp.int32)
    begin = begin.astype(jnp.int32)
    base = lax.broadcasted_iota(jnp.int32, chan.shape, 0) * rows
    group = jnp.minimum(begin >> 7, size - 1)
    table = totals.astype(jnp.int32)
    for values in ((filled >> 7) * 8, (filled - begin) & (ROWS - 1), begin & (ROWS - 1), base + group * FIELDS):
        table = jnp.where(lane < per_dest, values, pltpu.roll(table, per_dest, 1))
    plan[...] = table


def add_emitters(size, first, per_dest, chan, end, got, acc, streams, todo, plan, moves, sem, ready=()):
    source_count = chan.shape[0]
    share = acc.shape[0]
    stride = streams.shape[0] // (8 * share)
    lane = lax.broadcasted_iota(jnp.int32, (FIELDS, ROWS), 1)
    plan_moves(size, first, per_dest, share, stride, (got.shape[0] - 8) // source_count, chan, end, plan)
    copy = pltpu.make_async_copy(plan, moves, sem)
    copy.start()
    copy.wait()
    for other in ready:
        other.wait()

    def move(source, places):
        for place in places:
            row, begin, turn, target = (moves[source, k * per_dest + place] for k in range(4))
            target = pl.multiple_of(target, 8)
            here = got[pl.ds(row, FIELDS), :]
            there = got[pl.ds(row + FIELDS, FIELDS), :]
            filled = (jnp.full(lane.shape, begin, jnp.int32) + turn) & (ROWS - 1)
            whole = pltpu.roll(jnp.where(lane >= begin, here, there), turn, 1)
            pltpu.store(streams.at[pl.ds(target, FIELDS), :], whole, mask=lane >= filled)
            streams[pl.ds(target + 8, FIELDS), :] = whole

    def append(source, carry):
        if first == 0:
            move(source, range(per_dest))
        for start in range(0, 0 if first == 0 else per_dest, SKIP):
            places = range(start, min(start + SKIP, per_dest))
            live = moves[source, 4 * per_dest + share + start // SKIP]
            pl.when(live > 0)(functools.partial(move, source, places))
        return carry

    lax.fori_loop(0, source_count, append, 0)

    def list_chan(chan, count):
        total = moves[0, 4 * per_dest + chan]

        def list_pair(pair, at):
            todo[0, at] = chan
            todo[1, at] = chan * stride + 2 * pair
            todo[2, at] = total - 2 * ROWS * pair
            return at + 1

        return lax.fori_loop(0, (total + 2 * ROWS - 1) >> 8, list_pair, count)

    pair_count = lax.fori_loop(0, share, list_chan, 0)
    for extra in range(UNROLL - 1):
        todo[0, pair_count + extra] = 0
        todo[1, pair_count + extra] = 0
        todo[2, pair_count + extra] = 0

    place16 = lax.broadcasted_iota(jnp.int32, (SIDE, ROWS), 0).astype(jnp.float32)
    place8 = lax.broadcasted_iota(jnp.int32, (8, ROWS), 0).astype(jnp.float32) + 0.5

    def hat(cell, frac):
        apart = place16 - cell
        return jnp.where(apart == 0.0, 1.0 - frac, jnp.where(apart == 1.0, frac, 0.0))

    def factors(group, left):
        props = jnp.where(lane < left, streams[pl.ds(pl.multiple_of(group * 8, 8), FIELDS), :], 0.0)
        cell, frac_x, frac_y, center, decay, bright = (props[f : f + 1, :] for f in range(FIELDS))
        cell_x = jnp.floor(cell * (1.0 / SIDE))
        weight_x = hat(cell_x, frac_x)
        weight_y = hat(cell - SIDE * cell_x, frac_y)
        spread = jnp.concatenate(
            [(weight_x[x : x + 1, :] * weight_y).astype(jnp.bfloat16) for x in range(SIDE)], axis=0
        )
        apart = place8 - center
        profile = [jnp.exp2(jnp.square(apart + 8.0 * i) * decay) for i in range(CB // 8)]
        total = profile[0]
        for part in profile[1:]:
            total = total + part
        scale = bright / jnp.sum(total, axis=0, keepdims=True)
        line = jnp.concatenate(profile, axis=0) * scale
        return spread, line.astype(jnp.bfloat16)

    def some_pairs(turn, carry):
        for step in range(UNROLL):
            at = turn * UNROLL + step
            chan, group, left = todo[0, at], todo[1, at], todo[2, at]
            spread_0, line_0 = factors(group, left)
            spread_1, line_1 = factors(group + 1, left - ROWS)
            acc[chan] += lax.dot_general(
                jnp.concatenate([spread_0, spread_1], axis=1),
                jnp.concatenate([line_0, line_1], axis=1),
                (((1,), (1,)), ((), ())),
                preferred_element_type=jnp.float32,
            )
        return carry

    lax.fori_loop(0, (pair_count + UNROLL - 1) // UNROLL, some_pairs, 0)


def fetch(got_ref, got, sem):
    copy = pltpu.make_async_copy(got_ref, got.at[pl.ds(0, got_ref.shape[0])], sem)
    copy.start()
    return copy


def first_kernel(size, per_dest, share, got_ref, acc, chan_ref, end_ref, got, got_sem, *scratch):
    copy = fetch(got_ref, got, got_sem)
    acc[...] = jnp.zeros_like(acc)
    sources = scratch[-2].shape[0]
    rows = got_ref.shape[0] // sources
    copy.wait()
    chan = got[pl.ds(size * FIELDS, sources, stride=rows), :]
    end = got[pl.ds(size * FIELDS + 1, sources, stride=rows), :]
    chan_ref[...] = chan
    end_ref[...] = end
    add_emitters(size, 0, per_dest, chan, end, got, acc, *scratch)


def more_kernel(size, first, per_dest, chan_ref, end_ref, got_ref, held_ref, acc, got, got_sem, *scratch):
    copy = fetch(got_ref, got, got_sem)
    acc[...] = held_ref[...]
    copy.wait()
    add_emitters(size, first, per_dest, chan_ref[...], end_ref[...], got, acc, *scratch)


def last_kernel(size, first, per_dest, chan_ref, end_ref, width_ref, got_ref, held_ref, cube, near_ref, far_ref,
                acc, held_sem, got, got_sem, *scratch):
    held = pltpu.make_async_copy(held_ref, acc, held_sem)
    held.start()
    copy = fetch(got_ref, got, got_sem)
    add_emitters(size, first, per_dest, chan_ref[...], end_ref[...], got, acc, *scratch, ready=(copy, held))
    share = acc.shape[0]

    def one_chan(chan, carry):
        columns = pl.ds(pl.multiple_of(chan * CB, CB), CB)
        smooth(acc.at[chan], width_ref[:, columns], cube, columns)
        return carry

    lax.fori_loop(0, share, one_chan, 0)
    even = lax.rem(lax.axis_index("slab"), 2) == 0
    head = cube[:, :CB].T[:EDGE]
    tail = cube[:, (share - 1) * CB :].T[CB - EDGE :]
    near_ref[...] = jnp.where(even, tail, head)
    far_ref[...] = jnp.where(even, head, tail)


def smooth(plane_ref, widths, cube_ref, columns):
    decay = (-0.5 * LOG2E) / jnp.square(widths)
    places = lax.broadcasted_iota(jnp.int32, (SIDE, CB), 0).astype(jnp.float32)
    beam = [jnp.exp2(jnp.square(places - float(v)) * decay) for v in range(SIDE)]
    norm = beam[0]
    for v in range(1, SIDE):
        norm = norm + beam[v]
    inverse = 1.0 / norm
    beam = [b * inverse for b in beam]
    half = SIDE // 2
    even, odd = [None] * half, [None] * half
    for v in range(half):
        low = plane_ref[v * SIDE : (v + 1) * SIDE, :]
        high = plane_ref[(SIDE - 1 - v) * SIDE : (SIDE - v) * SIDE, :]
        both, apart = low + high, low - high
        near, far = beam[v][:half], beam[SIDE - 1 - v][:half]
        mean, rest = 0.5 * (near + far), 0.5 * (near - far)
        for x in range(half):
            term_even, term_odd = mean[x : x + 1, :] * both, rest[x : x + 1, :] * apart
            even[x] = term_even if v == 0 else even[x] + term_even
            odd[x] = term_odd if v == 0 else odd[x] + term_odd
    for x in range(SIDE):
        along_x = even[x] + odd[x] if x < half else even[SIDE - 1 - x] - odd[SIDE - 1 - x]
        total = None
        for v in range(SIDE):
            term = beam[v] * along_x[v : v + 1, :]
            total = term if v == 0 else total + term
        cube_ref[x * SIDE : (x + 1) * SIDE, columns] = total


def emitter_scratch(size, got, share):
    sources, rows = got.shape[:2]
    work = size * sources
    return [
        pltpu.VMEM((sources * rows + 8, ROWS), jnp.float32),
        pltpu.SemaphoreType.DMA,
        pltpu.VMEM((share * (work + 2) * 8, ROWS), jnp.float32),
        pltpu.SMEM((3, work // 2 + share + UNROLL), jnp.int32),
        pltpu.VMEM((sources, ROWS), jnp.int32),
        pltpu.SMEM((sources, ROWS), jnp.int32),
        pltpu.SemaphoreType.DMA,
    ]


def flat(got):
    return pltpu.with_memory_space_constraint(got.reshape(-1, ROWS), pltpu.VMEM)


def emitter_cost(size, got):
    work = size * got.shape[0]
    return pl.CostEstimate(
        flops=work * 2 * PIX * CB * ROWS, transcendentals=work * CB * ROWS, bytes_accessed=got.size * 4
    )


def deposit_first(size, per_dest, share, got):
    return pl.pallas_call(
        functools.partial(first_kernel, size, per_dest, share),
        out_shape=[jax.ShapeDtypeStruct((share, PIX, CB), jnp.float32)]
        + [jax.ShapeDtypeStruct((got.shape[0], ROWS), jnp.float32)] * 2,
        in_specs=[ANY],
        out_specs=[VMEM] * 3,
        scratch_shapes=emitter_scratch(size, got, share),
        cost_estimate=emitter_cost(size, got),
        name="deposit_first",
    )(flat(got))


def deposit_more(size, first, per_dest, share, chan, end, got, held):
    return pl.pallas_call(
        functools.partial(more_kernel, size, first, per_dest),
        out_shape=jax.ShapeDtypeStruct((share, PIX, CB), jnp.float32),
        in_specs=[VMEM, VMEM, ANY, VMEM],
        out_specs=VMEM,
        scratch_shapes=emitter_scratch(size, got, share),
        input_output_aliases={3: 0},
        name="deposit_more",
    )(chan, end, flat(got), held)


def deposit_last(size, first, per_dest, share, chan, end, got, held, widths):
    edge = jax.ShapeDtypeStruct((EDGE, PIX), jnp.float32)
    return pl.pallas_call(
        functools.partial(last_kernel, size, first, per_dest),
        out_shape=[pltpu.VMEM((PIX, share * CB), jnp.float32), edge, edge],
        in_specs=[VMEM] * 3 + [ANY] * 2,
        out_specs=[VMEM] * 3,
        scratch_shapes=[
            pltpu.VMEM((share, PIX, CB), jnp.float32),
            pltpu.SemaphoreType.DMA,
        ]
        + emitter_scratch(size, got, share),
        cost_estimate=emitter_cost(size, got),
        name="deposit_last",
    )(chan, end, widths.reshape(1, -1), flat(got), held)


def split(values):
    high = values.astype(jnp.bfloat16)
    return high, (values - high.astype(jnp.float32)).astype(jnp.bfloat16)


def times(left, right, dims):
    (left_high, left_low), (right_high, right_low) = left, right

    def dot(a, b):
        return lax.dot_general(a, b, (dims, ((), ())), preferred_element_type=jnp.float32)

    return dot(left_high, right_high) + (dot(left_high, right_low) + dot(left_low, right_high))


def band_part(taps_ref, first, rows):
    shape = (rows, CB)
    apart = lax.broadcasted_iota(jnp.int32, shape, 0) - lax.broadcasted_iota(jnp.int32, shape, 1) + (first + HALF)
    band = jnp.zeros(shape, jnp.float32)
    for k in range(TAPS):
        band = jnp.where(apart == k, taps_ref[k], band)
    return split(band)


def taps_kernel(wide, taps_ref, cube_ref, near_ref, far_ref, out_ref, out, high_ref, low_ref, sems):
    slab, last = lax.axis_index("slab"), lax.axis_size("slab") - 1
    even = lax.rem(slab, 2) == 0
    for ref, part in zip((high_ref, low_ref), band_part(taps_ref, -CB, 3 * CB)):
        ref[...] = jnp.zeros_like(ref)
        for i in range(0, wide, CB):
            ref[i : i + 3 * CB, i : i + CB] = part
    end = cube_ref.shape[1]
    copies = []
    for start in range(0, end, wide):
        low, high = max(start - CB, 0), min(start + wide + CB, end)
        rows, columns = slice(low - start + CB, high - start + CB), slice(start, start + wide)
        out[:, columns] = times(split(cube_ref[:, low:high]), (high_ref[rows], low_ref[rows]), ((1,), (0,)))
        if start == 0:
            edge = jnp.where(slab > 0, jnp.where(even, far_ref[...], near_ref[...]), 0.0)
            out[:, :CB] += times(split(edge), band_part(taps_ref, -EDGE, EDGE), ((0,), (0,)))
        if start + wide == end:
            edge = jnp.where(slab < last, jnp.where(even, near_ref[...], far_ref[...]), 0.0)
            out[:, end - CB :] += times(split(edge), band_part(taps_ref, CB, EDGE), ((0,), (0,)))
        copies.append(pltpu.make_async_copy(out.at[:, columns], out_ref.at[:, columns], sems.at[start // wide]))
        copies[-1].start()
    for copy in copies:
        copy.wait()


def sum_taps(taps, cube, near, far):
    wide = 2 * CB if cube.shape[1] % (2 * CB) == 0 else CB
    cube, near, far = (pltpu.with_memory_space_constraint(x, pltpu.VMEM) for x in (cube, near, far))
    return pl.pallas_call(
        functools.partial(taps_kernel, wide),
        out_shape=jax.ShapeDtypeStruct(cube.shape, jnp.float32),
        in_specs=[SMEM, VMEM, VMEM, VMEM],
        out_specs=ANY,
        scratch_shapes=[pltpu.VMEM(cube.shape, jnp.float32)]
        + [pltpu.VMEM((wide + 2 * CB, wide), jnp.bfloat16)] * 2
        + [pltpu.SemaphoreType.DMA((cube.shape[1] // wide,))],
        name="taps",
    )(taps, cube, near, far)


def body(
    voxel_cell,
    offsets,
    line_center,
    line_width,
    luminosity,
    block_rows,
    block_chan,
    slot_table,
    beam_width,
    spectral_taps,
):
    slab_count = lax.axis_size("slab")
    dest_count = lax.axis_size("tile") * slab_count
    per_dest = slot_table.shape[1] // dest_count
    share = NCB // slab_count
    sizes = chunk_sizes(per_dest)

    def packed(wanted):
        return pack(
            sizes, wanted, dest_count, slab_count, share, slot_table, block_rows, block_chan,
            voxel_cell, offsets, line_center, line_width, luminosity,
        )

    sent = packed((0, 1))
    def exchange(piece):
        return lax.all_to_all(piece, ("tile", "slab"), split_axis=0, concat_axis=0, tiled=True)

    got_first = exchange(sent[0])
    got_first, last_piece = lax.optimization_barrier((got_first, sent[1]))
    got_last = exchange(last_piece)
    held, chan, end = deposit_first(sizes[0], per_dest, share, got_first)
    reach = sizes[0] + sizes[1]
    if len(sizes) > 2:
        longest = jnp.max(chan[:, ROWS - 1])
        held, got_last = lax.optimization_barrier((held, got_last))
        held = lax.cond(
            longest > float(reach * ROWS),
            lambda held: deposit_more(sizes[2], reach, per_dest, share, chan, end, exchange(packed((2,))[0]), held),
            lambda held: held,
            held,
        )
    cube, near, far = deposit_last(
        sizes[1], sizes[0], per_dest, share, chan, end, got_last, held, beam_width
    )
    near = lax.ppermute(near, "slab", [(i, i ^ 1) for i in range(slab_count)])
    far = lax.ppermute(far, "slab", [(i, (i + 1 if i % 2 else i - 1) % slab_count) for i in range(slab_count)])
    return sum_taps(spectral_taps, cube, near, far)[None]


def solution(mesh):
    placed = (
        P(("tile", "slab"), None),
        P(("tile", "slab"), None, None),
        P(("tile", "slab"), None),
        P(("tile", "slab"), None),
        P(("tile", "slab"), None),
        P(("tile", "slab")),
        P(("tile", "slab")),
        P(("tile", "slab"), None),
        P("slab"),
        P(),
    )
    return jax.shard_map(
        body, mesh=mesh, in_specs=placed, out_specs=P("tile", None, "slab"), check_vma=False
    )
```

```python
import functools
import math

import jax
import jax.numpy as jnp
from jax import lax
from jax.experimental import pallas as pl
from jax.experimental.pallas import tpu as pltpu
from jax.sharding import PartitionSpec as P

SIDE = 16
PIX = SIDE * SIDE
CB = 128
ROWS = 128
TAPS = 31
HALF = 15
EDGE = 16
NCB = 32
FIELDS = 6
UNROLL = 6
SKIP = 8
AHEAD = 4
LOG2E = math.log2(math.e)
SMEM = pl.BlockSpec(memory_space=pltpu.SMEM)
VMEM = pl.BlockSpec(memory_space=pltpu.VMEM)
ANY = pl.BlockSpec(memory_space=pl.ANY)


def chunk_sizes(per_dest):
    early = late = max(per_dest * 9 // 24, 1)
    sizes = [early, late, per_dest - early - late]
    return [size for size in sizes if size > 0]


def padded_rows(rows):
    return -(-rows // 8) * 8


def pack_kernel(sizes, wanted, slab_count, share, slot_ref, count_ref, chan_ref, *refs):
    inputs, refs = refs[:5], refs[5:]
    sent, refs = refs[: len(wanted)], refs[len(wanted) :]
    staged, refs = refs[: len(wanted)], refs[len(wanted) :]
    props, *streams, slots, counts, chans, plan, moves, sem = refs[: 7 + AHEAD]
    refs = refs[7 + AHEAD :]
    (cell_ref, offset_ref, center_ref, width_ref, lum_ref), in_sem = refs[:5], refs[5]
    out_sems = refs[6:]
    outs = dict(zip(wanted, staged))
    fetches = [pltpu.make_async_copy(a, b, in_sem.at[i]) for i, (a, b) in enumerate(zip(inputs, refs[:5]))]
    for fetch_in in fetches:
        fetch_in.start()
    dest_count = slots.shape[0]
    per_dest = sum(sizes)
    block_total = cell_ref.shape[0]
    lane = lax.broadcasted_iota(jnp.int32, (dest_count, ROWS), 1)

    slot_row = slot_ref[...]
    blocks = lax.broadcasted_iota(jnp.int32, (block_total, slot_row.shape[1]), 0)
    chosen = jnp.where(blocks == slot_row, 1.0, 0.0).astype(jnp.bfloat16)
    table = jnp.concatenate([count_ref[...].reshape(1, -1), chan_ref[...].reshape(1, -1)], axis=0).astype(jnp.float32).astype(jnp.bfloat16)
    looked = jnp.dot(table, chosen, preferred_element_type=jnp.float32)
    slots[...] = jnp.zeros_like(slots)
    counts[...] = jnp.zeros_like(counts)
    chans[...] = jnp.zeros_like(chans)
    for dest in range(dest_count):
        columns = slice(dest * per_dest, (dest + 1) * per_dest)
        slots[dest : dest + 1, :per_dest] = slot_row[:, columns]
        counts[dest : dest + 1, :per_dest] = looked[0:1, columns]
        chans[dest : dest + 1, :per_dest] = looked[1:2, columns]
    count = counts[...]
    until = jnp.dot(count.astype(jnp.bfloat16), exclusive(ROWS), preferred_element_type=jnp.float32)
    end = until + count
    start = until.astype(jnp.int32)
    orders = jnp.zeros(lane.shape, jnp.int32)
    for values in ((start >> 7) * 8, start & (ROWS - 1), jnp.maximum(slots[...], 0) * 8):
        orders = jnp.where(lane < per_dest, values, pltpu.roll(orders, per_dest, 1))
    plan[...] = orders
    copy = pltpu.make_async_copy(plan, moves, sem)
    copy.start()

    if 0 in outs:
        rows = outs[0].shape[0] // dest_count
        dests = lax.broadcasted_iota(jnp.int32, lane.shape, 0)
        chan = chans[...] - (lax.rem(dests, slab_count) * share).astype(jnp.float32)
        longest = jnp.max(jnp.max(end, axis=0, keepdims=True), axis=1, keepdims=True)
        meta = sizes[0] * FIELDS
        outs[0][pl.ds(meta, dest_count, stride=rows), :] = jnp.where(lane == ROWS - 1, longest, chan)
        outs[0][pl.ds(meta + 1, dest_count, stride=rows), :] = end

    def gather_fields(tile, carry):
        first = pl.multiple_of(tile * 8, 8)
        here = pl.ds(first, 8)
        fields = (
            cell_ref[here, :].astype(jnp.float32),
            offset_ref[pl.ds(2 * first, 8, stride=2), :],
            offset_ref[pl.ds(2 * first + 1, 8, stride=2), :],
            center_ref[here, :],
            (-0.5 * LOG2E) / jnp.square(width_ref[here, :]),
            lum_ref[here, :].astype(jnp.bfloat16).astype(jnp.float32),
        )
        for field, values in enumerate(fields):
            props[pl.ds(8 * first + field, 8, stride=8), :] = values
        return carry

    for fetch_in in fetches:
        fetch_in.wait()
    lax.fori_loop(0, block_total // 8, gather_fields, 0, unroll=2)
    copy.wait()

    def send(dest):
        for out, whole, out_sem in zip(staged, sent, out_sems):
            rows = out.shape[0] // dest_count
            here = pl.ds(pl.multiple_of(dest * rows, 8), rows)
            pltpu.make_async_copy(out.at[here], whole.at[here], out_sem).start()

    lanes = lax.broadcasted_iota(jnp.int32, (8, ROWS), 1)

    def some_dests(turn, carry):
        first = turn * len(streams)
        for back in range(len(streams)):
            pl.when(turn > 0)(functools.partial(send, first - 1 - back))
        for slot in range(per_dest):
            for ahead, stream in enumerate(streams):
                row, shift, target = (moves[first + ahead, k * per_dest + slot] for k in range(3))
                row, target = pl.multiple_of(row, 8), pl.multiple_of(target, 8)
                turned = pltpu.roll(props[pl.ds(row, 8), :], shift, 1)
                pltpu.store(stream.at[pl.ds(target, 8), :], turned, mask=lanes >= shift)
                stream[pl.ds(target + 8, 8), :] = turned
        for ahead, stream in enumerate(streams):
            group = 0
            for part, size in enumerate(sizes):
                if part in outs:
                    out = outs[part]
                    base = pl.multiple_of((first + ahead) * (out.shape[0] // dest_count), 8)
                    for place in range(size):
                        here = 8 * (group + place)
                        out[pl.ds(base + place * FIELDS, FIELDS), :] = stream[here : here + FIELDS, :]
                group += size
        return carry

    lax.fori_loop(0, dest_count // len(streams), some_dests, 0)
    for back in range(1, len(streams)):
        send(dest_count - 1 - back)
    send(dest_count - 1)
    for out, whole, out_sem in zip(staged, sent, out_sems):
        pltpu.make_async_copy(out, whole, out_sem).wait()


def pack(sizes, wanted, dest_count, slab_count, share, slot_list, counts, chans, cells, offsets, centers, widths, lums):
    rows = [padded_rows(size * FIELDS + (2 if part == 0 else 0)) for part, size in enumerate(sizes)]
    block_total = cells.shape[0]
    lists = (cells, offsets.reshape(block_total * 2, ROWS), centers, widths, lums)
    shapes = [(dest_count * rows[part], ROWS) for part in wanted]
    sent = pl.pallas_call(
        functools.partial(pack_kernel, sizes, wanted, slab_count, share),
        out_shape=[jax.ShapeDtypeStruct(shape, jnp.float32) for shape in shapes],
        in_specs=[VMEM] * 3 + [ANY] * 5,
        out_specs=[ANY] * len(wanted),
        scratch_shapes=[pltpu.VMEM(shape, jnp.float32) for shape in shapes]
        + [
            pltpu.VMEM((block_total * 8, ROWS), jnp.float32),
            *[pltpu.VMEM(((sum(sizes) + 2) * 8, ROWS), jnp.float32)] * AHEAD,
            pltpu.VMEM((dest_count, ROWS), jnp.int32),
            pltpu.VMEM((dest_count, ROWS), jnp.float32),
            pltpu.VMEM((dest_count, ROWS), jnp.float32),
            pltpu.VMEM((dest_count, ROWS), jnp.int32),
            pltpu.SMEM((dest_count, ROWS), jnp.int32),
            pltpu.SemaphoreType.DMA,
        ]
        + [pltpu.VMEM(values.shape, values.dtype) for values in lists]
        + [pltpu.SemaphoreType.DMA((5,))]
        + [pltpu.SemaphoreType.DMA] * len(wanted),
        name="pack",
    )(slot_list, counts, chans, *lists)
    return [piece.reshape(dest_count, rows[part], ROWS) for part, piece in zip(wanted, sent)]


def exclusive(size):
    before = lax.broadcasted_iota(jnp.int32, (size, size), 0)
    return (before < lax.broadcasted_iota(jnp.int32, (size, size), 1)).astype(jnp.bfloat16)


def plan_moves(size, first, per_dest, share, stride, rows, chan, end, plan):
    sources = chan.shape[0]
    lane = lax.broadcasted_iota(jnp.int32, chan.shape, 1)
    low, high = float(first * ROWS), float((first + size) * ROWS)
    start = jnp.where(lane == 0, 0.0, pltpu.roll(end, 1, 1))
    begin = jnp.clip(start, low, high) - low
    count = jnp.where(lane < per_dest, jnp.clip(end, low, high) - low - begin, 0.0)
    chan = jnp.where(count > 0.0, chan, 0.0)
    across = exclusive(ROWS)
    down = exclusive(sources)
    filled = jnp.zeros(chan.shape, jnp.float32)
    totals = jnp.zeros(chan.shape, jnp.float32)
    for c in range(share):
        own = jnp.where(chan == float(c), count, 0.0)
        moved = own.astype(jnp.bfloat16)
        here = jnp.dot(moved, across, preferred_element_type=jnp.float32)
        above = lax.dot_general(down, moved, (((0,), (0,)), ((), ())), preferred_element_type=jnp.float32)
        above = jnp.sum(above, axis=1, keepdims=True) + float(c * stride * ROWS)
        filled = filled + jnp.where(chan == float(c), here + above, 0.0)
        total = jnp.sum(jnp.sum(own, axis=0, keepdims=True), axis=1, keepdims=True)
        totals = totals + jnp.where(lane == c, total, 0.0)
    for start in range(0, per_dest, SKIP):
        inside = (lane >= start) & (lane < start + SKIP)
        total = jnp.sum(jnp.where(inside, count, 0.0), axis=1, keepdims=True)
        totals = totals + jnp.where(lane == share + start // SKIP, total, 0.0)
    filled = filled.astype(jnp.int32)
    begin = begin.astype(jnp.int32)
    base = lax.broadcasted_iota(jnp.int32, chan.shape, 0) * rows
    group = jnp.minimum(begin >> 7, size - 1)
    table = totals.astype(jnp.int32)
    for values in ((filled >> 7) * 8, (filled - begin) & (ROWS - 1), begin & (ROWS - 1), base + group * FIELDS):
        table = jnp.where(lane < per_dest, values, pltpu.roll(table, per_dest, 1))
    plan[...] = table


def add_emitters(size, first, per_dest, chan, end, got, acc, streams, todo, plan, moves, sem, ready=()):
    source_count = chan.shape[0]
    share = acc.shape[0]
    stride = streams.shape[0] // (8 * share)
    lane = lax.broadcasted_iota(jnp.int32, (FIELDS, ROWS), 1)
    plan_moves(size, first, per_dest, share, stride, (got.shape[0] - 8) // source_count, chan, end, plan)
    copy = pltpu.make_async_copy(plan, moves, sem)
    copy.start()
    copy.wait()
    for other in ready:
        other.wait()

    def move(source, places):
        for place in places:
            row, begin, turn, target = (moves[source, k * per_dest + place] for k in range(4))
            target = pl.multiple_of(target, 8)
            here = got[pl.ds(row, FIELDS), :]
            there = got[pl.ds(row + FIELDS, FIELDS), :]
            filled = (jnp.full(lane.shape, begin, jnp.int32) + turn) & (ROWS - 1)
            whole = pltpu.roll(jnp.where(lane >= begin, here, there), turn, 1)
            pltpu.store(streams.at[pl.ds(target, FIELDS), :], whole, mask=lane >= filled)
            streams[pl.ds(target + 8, FIELDS), :] = whole

    def append(source, carry):
        if first == 0:
            move(source, range(per_dest))
        for start in range(0, 0 if first == 0 else per_dest, SKIP):
            places = range(start, min(start + SKIP, per_dest))
            live = moves[source, 4 * per_dest + share + start // SKIP]
            pl.when(live > 0)(functools.partial(move, source, places))
        return carry

    lax.fori_loop(0, source_count, append, 0)

    def list_chan(chan, count):
        total = moves[0, 4 * per_dest + chan]

        def list_pair(pair, at):
            todo[0, at] = chan
            todo[1, at] = chan * stride + 2 * pair
            todo[2, at] = total - 2 * ROWS * pair
            return at + 1

        return lax.fori_loop(0, (total + 2 * ROWS - 1) >> 8, list_pair, count)

    pair_count = lax.fori_loop(0, share, list_chan, 0)
    for extra in range(UNROLL - 1):
        todo[0, pair_count + extra] = 0
        todo[1, pair_count + extra] = 0
        todo[2, pair_count + extra] = 0

    place16 = lax.broadcasted_iota(jnp.int32, (SIDE, ROWS), 0).astype(jnp.float32)
    place8 = lax.broadcasted_iota(jnp.int32, (8, ROWS), 0).astype(jnp.float32) + 0.5

    def hat(cell, frac):
        apart = place16 - cell
        return jnp.where(apart == 0.0, 1.0 - frac, jnp.where(apart == 1.0, frac, 0.0))

    def factors(group, left):
        props = jnp.where(lane < left, streams[pl.ds(pl.multiple_of(group * 8, 8), FIELDS), :], 0.0)
        cell, frac_x, frac_y, center, decay, bright = (props[f : f + 1, :] for f in range(FIELDS))
        cell_x = jnp.floor(cell * (1.0 / SIDE))
        weight_x = hat(cell_x, frac_x)
        weight_y = hat(cell - SIDE * cell_x, frac_y)
        spread = jnp.concatenate(
            [(weight_x[x : x + 1, :] * weight_y).astype(jnp.bfloat16) for x in range(SIDE)], axis=0
        )
        apart = place8 - center
        profile = [jnp.exp2(jnp.square(apart + 8.0 * i) * decay) for i in range(CB // 8)]
        total = profile[0]
        for part in profile[1:]:
            total = total + part
        scale = bright / jnp.sum(total, axis=0, keepdims=True)
        line = jnp.concatenate(profile, axis=0) * scale
        return spread, line.astype(jnp.bfloat16)

    def some_pairs(turn, carry):
        for step in range(UNROLL):
            at = turn * UNROLL + step
            chan, group, left = todo[0, at], todo[1, at], todo[2, at]
            spread_0, line_0 = factors(group, left)
            spread_1, line_1 = factors(group + 1, left - ROWS)
            acc[chan] += lax.dot_general(
                jnp.concatenate([spread_0, spread_1], axis=1),
                jnp.concatenate([line_0, line_1], axis=1),
                (((1,), (1,)), ((), ())),
                preferred_element_type=jnp.float32,
            )
        return carry

    lax.fori_loop(0, (pair_count + UNROLL - 1) // UNROLL, some_pairs, 0)


def fetch(got_ref, got, sem):
    copy = pltpu.make_async_copy(got_ref, got.at[pl.ds(0, got_ref.shape[0])], sem)
    copy.start()
    return copy


def first_kernel(size, per_dest, share, got_ref, acc, chan_ref, end_ref, got, got_sem, *scratch):
    copy = fetch(got_ref, got, got_sem)
    acc[...] = jnp.zeros_like(acc)
    sources = scratch[-2].shape[0]
    rows = got_ref.shape[0] // sources
    copy.wait()
    chan = got[pl.ds(size * FIELDS, sources, stride=rows), :]
    end = got[pl.ds(size * FIELDS + 1, sources, stride=rows), :]
    chan_ref[...] = chan
    end_ref[...] = end
    add_emitters(size, 0, per_dest, chan, end, got, acc, *scratch)


def more_kernel(size, first, per_dest, chan_ref, end_ref, got_ref, held_ref, acc, got, got_sem, *scratch):
    copy = fetch(got_ref, got, got_sem)
    acc[...] = held_ref[...]
    copy.wait()
    add_emitters(size, first, per_dest, chan_ref[...], end_ref[...], got, acc, *scratch)


def last_kernel(size, first, per_dest, chan_ref, end_ref, width_ref, got_ref, held_ref, cube, near_ref, far_ref,
                acc, held_sem, got, got_sem, *scratch):
    held = pltpu.make_async_copy(held_ref, acc, held_sem)
    held.start()
    copy = fetch(got_ref, got, got_sem)
    add_emitters(size, first, per_dest, chan_ref[...], end_ref[...], got, acc, *scratch, ready=(copy, held))
    share = acc.shape[0]

    def one_chan(chan, carry):
        columns = pl.ds(pl.multiple_of(chan * CB, CB), CB)
        smooth(acc.at[chan], width_ref[:, columns], cube, columns)
        return carry

    lax.fori_loop(0, share, one_chan, 0)
    even = lax.rem(lax.axis_index("slab"), 2) == 0
    head = cube[:, :CB].T[:EDGE]
    tail = cube[:, (share - 1) * CB :].T[CB - EDGE :]
    near_ref[...] = jnp.where(even, tail, head)
    far_ref[...] = jnp.where(even, head, tail)


def smooth(plane_ref, widths, cube_ref, columns):
    decay = (-0.5 * LOG2E) / jnp.square(widths)
    places = lax.broadcasted_iota(jnp.int32, (SIDE, CB), 0).astype(jnp.float32)
    beam = [jnp.exp2(jnp.square(places - float(v)) * decay) for v in range(SIDE)]
    norm = beam[0]
    for v in range(1, SIDE):
        norm = norm + beam[v]
    inverse = 1.0 / norm
    beam = [b * inverse for b in beam]
    half = SIDE // 2
    even, odd = [None] * half, [None] * half
    for v in range(half):
        low = plane_ref[v * SIDE : (v + 1) * SIDE, :]
        high = plane_ref[(SIDE - 1 - v) * SIDE : (SIDE - v) * SIDE, :]
        both, apart = low + high, low - high
        near, far = beam[v][:half], beam[SIDE - 1 - v][:half]
        mean, rest = 0.5 * (near + far), 0.5 * (near - far)
        for x in range(half):
            term_even, term_odd = mean[x : x + 1, :] * both, rest[x : x + 1, :] * apart
            even[x] = term_even if v == 0 else even[x] + term_even
            odd[x] = term_odd if v == 0 else odd[x] + term_odd
    for x in range(SIDE):
        along_x = even[x] + odd[x] if x < half else even[SIDE - 1 - x] - odd[SIDE - 1 - x]
        total = None
        for v in range(SIDE):
            term = beam[v] * along_x[v : v + 1, :]
            total = term if v == 0 else total + term
        cube_ref[x * SIDE : (x + 1) * SIDE, columns] = total


def emitter_scratch(size, got, share):
    sources, rows = got.shape[:2]
    work = size * sources
    return [
        pltpu.VMEM((sources * rows + 8, ROWS), jnp.float32),
        pltpu.SemaphoreType.DMA,
        pltpu.VMEM((share * (work + 2) * 8, ROWS), jnp.float32),
        pltpu.SMEM((3, work // 2 + share + UNROLL), jnp.int32),
        pltpu.VMEM((sources, ROWS), jnp.int32),
        pltpu.SMEM((sources, ROWS), jnp.int32),
        pltpu.SemaphoreType.DMA,
    ]


def flat(got):
    return pltpu.with_memory_space_constraint(got.reshape(-1, ROWS), pltpu.VMEM)


def emitter_cost(size, got):
    work = size * got.shape[0]
    return pl.CostEstimate(
        flops=work * 2 * PIX * CB * ROWS, transcendentals=work * CB * ROWS, bytes_accessed=got.size * 4
    )


def deposit_first(size, per_dest, share, got):
    return pl.pallas_call(
        functools.partial(first_kernel, size, per_dest, share),
        out_shape=[jax.ShapeDtypeStruct((share, PIX, CB), jnp.float32)]
        + [jax.ShapeDtypeStruct((got.shape[0], ROWS), jnp.float32)] * 2,
        in_specs=[ANY],
        out_specs=[VMEM] * 3,
        scratch_shapes=emitter_scratch(size, got, share),
        cost_estimate=emitter_cost(size, got),
        name="deposit_first",
    )(flat(got))


def deposit_more(size, first, per_dest, share, chan, end, got, held):
    return pl.pallas_call(
        functools.partial(more_kernel, size, first, per_dest),
        out_shape=jax.ShapeDtypeStruct((share, PIX, CB), jnp.float32),
        in_specs=[VMEM, VMEM, ANY, VMEM],
        out_specs=VMEM,
        scratch_shapes=emitter_scratch(size, got, share),
        input_output_aliases={3: 0},
        name="deposit_more",
    )(chan, end, flat(got), held)


def deposit_last(size, first, per_dest, share, chan, end, got, held, widths):
    edge = jax.ShapeDtypeStruct((EDGE, PIX), jnp.float32)
    return pl.pallas_call(
        functools.partial(last_kernel, size, first, per_dest),
        out_shape=[pltpu.VMEM((PIX, share * CB), jnp.float32), edge, edge],
        in_specs=[VMEM] * 3 + [ANY] * 2,
        out_specs=[VMEM] * 3,
        scratch_shapes=[
            pltpu.VMEM((share, PIX, CB), jnp.float32),
            pltpu.SemaphoreType.DMA,
        ]
        + emitter_scratch(size, got, share),
        cost_estimate=emitter_cost(size, got),
        name="deposit_last",
    )(chan, end, widths.reshape(1, -1), flat(got), held)


def split(values):
    high = values.astype(jnp.bfloat16)
    return high, (values - high.astype(jnp.float32)).astype(jnp.bfloat16)


def times(left, right, dims):
    (left_high, left_low), (right_high, right_low) = left, right

    def dot(a, b):
        return lax.dot_general(a, b, (dims, ((), ())), preferred_element_type=jnp.float32)

    return dot(left_high, right_high) + (dot(left_high, right_low) + dot(left_low, right_high))


def band_part(taps_ref, first, rows):
    shape = (rows, CB)
    apart = lax.broadcasted_iota(jnp.int32, shape, 0) - lax.broadcasted_iota(jnp.int32, shape, 1) + (first + HALF)
    band = jnp.zeros(shape, jnp.float32)
    for k in range(TAPS):
        band = jnp.where(apart == k, taps_ref[k], band)
    return split(band)


def taps_kernel(wide, taps_ref, cube_ref, near_ref, far_ref, out_ref, out, high_ref, low_ref, sems):
    slab, last = lax.axis_index("slab"), lax.axis_size("slab") - 1
    even = lax.rem(slab, 2) == 0
    for ref, part in zip((high_ref, low_ref), band_part(taps_ref, -CB, 3 * CB)):
        ref[...] = jnp.zeros_like(ref)
        for i in range(0, wide, CB):
            ref[i : i + 3 * CB, i : i + CB] = part
    end = cube_ref.shape[1]
    copies = []
    for start in range(0, end, wide):
        low, high = max(start - CB, 0), min(start + wide + CB, end)
        rows, columns = slice(low - start + CB, high - start + CB), slice(start, start + wide)
        out[:, columns] = times(split(cube_ref[:, low:high]), (high_ref[rows], low_ref[rows]), ((1,), (0,)))
        if start == 0:
            edge = jnp.where(slab > 0, jnp.where(even, far_ref[...], near_ref[...]), 0.0)
            out[:, :CB] += times(split(edge), band_part(taps_ref, -EDGE, EDGE), ((0,), (0,)))
        if start + wide == end:
            edge = jnp.where(slab < last, jnp.where(even, near_ref[...], far_ref[...]), 0.0)
            out[:, end - CB :] += times(split(edge), band_part(taps_ref, CB, EDGE), ((0,), (0,)))
        copies.append(pltpu.make_async_copy(out.at[:, columns], out_ref.at[:, columns], sems.at[start // wide]))
        copies[-1].start()
    for copy in copies:
        copy.wait()


def sum_taps(taps, cube, near, far):
    wide = 2 * CB if cube.shape[1] % (2 * CB) == 0 else CB
    cube, near, far = (pltpu.with_memory_space_constraint(x, pltpu.VMEM) for x in (cube, near, far))
    return pl.pallas_call(
        functools.partial(taps_kernel, wide),
        out_shape=jax.ShapeDtypeStruct(cube.shape, jnp.float32),
        in_specs=[SMEM, VMEM, VMEM, VMEM],
        out_specs=ANY,
        scratch_shapes=[pltpu.VMEM(cube.shape, jnp.float32)]
        + [pltpu.VMEM((wide + 2 * CB, wide), jnp.bfloat16)] * 2
        + [pltpu.SemaphoreType.DMA((cube.shape[1] // wide,))],
        name="taps",
    )(taps, cube, near, far)


def body(
    voxel_cell,
    offsets,
    line_center,
    line_width,
    luminosity,
    block_rows,
    block_chan,
    slot_table,
    beam_width,
    spectral_taps,
):
    slab_count = lax.axis_size("slab")
    dest_count = lax.axis_size("tile") * slab_count
    per_dest = slot_table.shape[1] // dest_count
    share = NCB // slab_count
    sizes = chunk_sizes(per_dest)

    def packed(wanted):
        return pack(
            sizes, wanted, dest_count, slab_count, share, slot_table, block_rows, block_chan,
            voxel_cell, offsets, line_center, line_width, luminosity,
        )

    sent = packed((0, 1))
    def exchange(piece):
        return lax.all_to_all(piece, ("tile", "slab"), split_axis=0, concat_axis=0, tiled=True)

    got_first = exchange(sent[0])
    got_first, last_piece = lax.optimization_barrier((got_first, sent[1]))
    got_last = exchange(last_piece)
    held, chan, end = deposit_first(sizes[0], per_dest, share, got_first)
    reach = sizes[0] + sizes[1]
    if len(sizes) > 2:
        longest = jnp.max(chan[:, ROWS - 1])
        held, got_last = lax.optimization_barrier((held, got_last))
        held = lax.cond(
            longest > float(reach * ROWS),
            lambda held: deposit_more(sizes[2], reach, per_dest, share, chan, end, exchange(packed((2,))[0]), held),
            lambda held: held,
            held,
        )
    cube, near, far = deposit_last(
        sizes[1], sizes[0], per_dest, share, chan, end, got_last, held, beam_width
    )
    near = lax.ppermute(near, "slab", [(i, i ^ 1) for i in range(slab_count)])
    far = lax.ppermute(far, "slab", [(i, (i + 1 if i % 2 else i - 1) % slab_count) for i in range(slab_count)])
    return sum_taps(spectral_taps, cube, near, far)[None]


def solution(mesh):
    placed = (
        P(("tile", "slab"), None),
        P(("tile", "slab"), None, None),
        P(("tile", "slab"), None),
        P(("tile", "slab"), None),
        P(("tile", "slab"), None),
        P(("tile", "slab")),
        P(("tile", "slab")),
        P(("tile", "slab"), None),
        P("slab"),
        P(),
    )
    return jax.shard_map(
        body, mesh=mesh, in_specs=placed, out_specs=P("tile", None, "slab"), check_vma=False
    )
```

```python
import functools
import math

import jax
import jax.numpy as jnp
from jax import lax
from jax.experimental import pallas as pl
from jax.experimental.pallas import tpu as pltpu
from jax.sharding import PartitionSpec as P

SIDE = 16
PIX = SIDE * SIDE
CB = 128
ROWS = 128
TAPS = 31
HALF = 15
EDGE = 16
NCB = 32
FIELDS = 6
UNROLL = 8
SKIP = 8
AHEAD = 4
LOG2E = math.log2(math.e)
SMEM = pl.BlockSpec(memory_space=pltpu.SMEM)
VMEM = pl.BlockSpec(memory_space=pltpu.VMEM)
ANY = pl.BlockSpec(memory_space=pl.ANY)


def chunk_sizes(per_dest):
    early = late = max(per_dest * 9 // 24, 1)
    sizes = [early, late, per_dest - early - late]
    return [size for size in sizes if size > 0]


def padded_rows(rows):
    return -(-rows // 8) * 8


def pack_kernel(sizes, wanted, slab_count, share, slot_ref, count_ref, chan_ref, *refs):
    inputs, refs = refs[:5], refs[5:]
    sent, refs = refs[: len(wanted)], refs[len(wanted) :]
    staged, refs = refs[: len(wanted)], refs[len(wanted) :]
    props, *streams, slots, counts, chans, plan, moves, sem = refs[: 7 + AHEAD]
    refs = refs[7 + AHEAD :]
    (cell_ref, offset_ref, center_ref, width_ref, lum_ref), in_sem = refs[:5], refs[5]
    out_sems = refs[6:]
    outs = dict(zip(wanted, staged))
    fetches = [pltpu.make_async_copy(a, b, in_sem.at[i]) for i, (a, b) in enumerate(zip(inputs, refs[:5]))]
    for fetch_in in fetches:
        fetch_in.start()
    dest_count = slots.shape[0]
    per_dest = sum(sizes)
    block_total = cell_ref.shape[0]
    lane = lax.broadcasted_iota(jnp.int32, (dest_count, ROWS), 1)

    slot_row = slot_ref[...]
    blocks = lax.broadcasted_iota(jnp.int32, (block_total, slot_row.shape[1]), 0)
    chosen = jnp.where(blocks == slot_row, 1.0, 0.0).astype(jnp.bfloat16)
    table = jnp.concatenate([count_ref[...].reshape(1, -1), chan_ref[...].reshape(1, -1)], axis=0).astype(jnp.float32).astype(jnp.bfloat16)
    looked = jnp.dot(table, chosen, preferred_element_type=jnp.float32)
    slots[...] = jnp.zeros_like(slots)
    counts[...] = jnp.zeros_like(counts)
    chans[...] = jnp.zeros_like(chans)
    for dest in range(dest_count):
        columns = slice(dest * per_dest, (dest + 1) * per_dest)
        slots[dest : dest + 1, :per_dest] = slot_row[:, columns]
        counts[dest : dest + 1, :per_dest] = looked[0:1, columns]
        chans[dest : dest + 1, :per_dest] = looked[1:2, columns]
    count = counts[...]
    until = jnp.dot(count.astype(jnp.bfloat16), exclusive(ROWS), preferred_element_type=jnp.float32)
    end = until + count
    start = until.astype(jnp.int32)
    orders = jnp.zeros(lane.shape, jnp.int32)
    for values in ((start >> 7) * 8, start & (ROWS - 1), jnp.maximum(slots[...], 0) * 8):
        orders = jnp.where(lane < per_dest, values, pltpu.roll(orders, per_dest, 1))
    plan[...] = orders
    copy = pltpu.make_async_copy(plan, moves, sem)
    copy.start()

    if 0 in outs:
        rows = outs[0].shape[0] // dest_count
        dests = lax.broadcasted_iota(jnp.int32, lane.shape, 0)
        chan = chans[...] - (lax.rem(dests, slab_count) * share).astype(jnp.float32)
        longest = jnp.max(jnp.max(end, axis=0, keepdims=True), axis=1, keepdims=True)
        meta = sizes[0] * FIELDS
        outs[0][pl.ds(meta, dest_count, stride=rows), :] = jnp.where(lane == ROWS - 1, longest, chan)
        outs[0][pl.ds(meta + 1, dest_count, stride=rows), :] = end

    def gather_fields(tile, carry):
        first = pl.multiple_of(tile * 8, 8)
        here = pl.ds(first, 8)
        fields = (
            cell_ref[here, :].astype(jnp.float32),
            offset_ref[pl.ds(2 * first, 8, stride=2), :],
            offset_ref[pl.ds(2 * first + 1, 8, stride=2), :],
            center_ref[here, :],
            (-0.5 * LOG2E) / jnp.square(width_ref[here, :]),
            lum_ref[here, :].astype(jnp.bfloat16).astype(jnp.float32),
        )
        for field, values in enumerate(fields):
            props[pl.ds(8 * first + field, 8, stride=8), :] = values
        return carry

    for fetch_in in fetches:
        fetch_in.wait()
    lax.fori_loop(0, block_total // 8, gather_fields, 0, unroll=2)
    copy.wait()

    def send(dest):
        for out, whole, out_sem in zip(staged, sent, out_sems):
            rows = out.shape[0] // dest_count
            here = pl.ds(pl.multiple_of(dest * rows, 8), rows)
            pltpu.make_async_copy(out.at[here], whole.at[here], out_sem).start()

    lanes = lax.broadcasted_iota(jnp.int32, (8, ROWS), 1)

    def some_dests(turn, carry):
        first = turn * len(streams)
        for back in range(len(streams)):
            pl.when(turn > 0)(functools.partial(send, first - 1 - back))
        for slot in range(per_dest):
            for ahead, stream in enumerate(streams):
                row, shift, target = (moves[first + ahead, k * per_dest + slot] for k in range(3))
                row, target = pl.multiple_of(row, 8), pl.multiple_of(target, 8)
                turned = pltpu.roll(props[pl.ds(row, 8), :], shift, 1)
                pltpu.store(stream.at[pl.ds(target, 8), :], turned, mask=lanes >= shift)
                stream[pl.ds(target + 8, 8), :] = turned
        for ahead, stream in enumerate(streams):
            group = 0
            for part, size in enumerate(sizes):
                if part in outs:
                    out = outs[part]
                    base = pl.multiple_of((first + ahead) * (out.shape[0] // dest_count), 8)
                    for place in range(size):
                        here = 8 * (group + place)
                        out[pl.ds(base + place * FIELDS, FIELDS), :] = stream[here : here + FIELDS, :]
                group += size
        return carry

    lax.fori_loop(0, dest_count // len(streams), some_dests, 0)
    for back in range(1, len(streams)):
        send(dest_count - 1 - back)
    send(dest_count - 1)
    for out, whole, out_sem in zip(staged, sent, out_sems):
        pltpu.make_async_copy(out, whole, out_sem).wait()


def pack(sizes, wanted, dest_count, slab_count, share, slot_list, counts, chans, cells, offsets, centers, widths, lums):
    rows = [padded_rows(size * FIELDS + (2 if part == 0 else 0)) for part, size in enumerate(sizes)]
    block_total = cells.shape[0]
    lists = (cells, offsets.reshape(block_total * 2, ROWS), centers, widths, lums)
    shapes = [(dest_count * rows[part], ROWS) for part in wanted]
    sent = pl.pallas_call(
        functools.partial(pack_kernel, sizes, wanted, slab_count, share),
        out_shape=[jax.ShapeDtypeStruct(shape, jnp.float32) for shape in shapes],
        in_specs=[VMEM] * 3 + [ANY] * 5,
        out_specs=[ANY] * len(wanted),
        scratch_shapes=[pltpu.VMEM(shape, jnp.float32) for shape in shapes]
        + [
            pltpu.VMEM((block_total * 8, ROWS), jnp.float32),
            *[pltpu.VMEM(((sum(sizes) + 2) * 8, ROWS), jnp.float32)] * AHEAD,
            pltpu.VMEM((dest_count, ROWS), jnp.int32),
            pltpu.VMEM((dest_count, ROWS), jnp.float32),
            pltpu.VMEM((dest_count, ROWS), jnp.float32),
            pltpu.VMEM((dest_count, ROWS), jnp.int32),
            pltpu.SMEM((dest_count, ROWS), jnp.int32),
            pltpu.SemaphoreType.DMA,
        ]
        + [pltpu.VMEM(values.shape, values.dtype) for values in lists]
        + [pltpu.SemaphoreType.DMA((5,))]
        + [pltpu.SemaphoreType.DMA] * len(wanted),
        compiler_params=pltpu.CompilerParams(),
        name="pack",
    )(slot_list, counts, chans, *lists)
    return [piece.reshape(dest_count, rows[part], ROWS) for part, piece in zip(wanted, sent)]


def exclusive(size):
    before = lax.broadcasted_iota(jnp.int32, (size, size), 0)
    return (before < lax.broadcasted_iota(jnp.int32, (size, size), 1)).astype(jnp.bfloat16)


def plan_moves(size, first, per_dest, share, stride, rows, chan, end, plan):
    sources = chan.shape[0]
    lane = lax.broadcasted_iota(jnp.int32, chan.shape, 1)
    low, high = float(first * ROWS), float((first + size) * ROWS)
    start = jnp.where(lane == 0, 0.0, pltpu.roll(end, 1, 1))
    begin = jnp.clip(start, low, high) - low
    count = jnp.where(lane < per_dest, jnp.clip(end, low, high) - low - begin, 0.0)
    chan = jnp.where(count > 0.0, chan, 0.0)
    across = exclusive(ROWS)
    down = exclusive(sources)
    filled = jnp.zeros(chan.shape, jnp.float32)
    totals = jnp.zeros(chan.shape, jnp.float32)
    for c in range(share):
        own = jnp.where(chan == float(c), count, 0.0)
        moved = own.astype(jnp.bfloat16)
        here = jnp.dot(moved, across, preferred_element_type=jnp.float32)
        above = lax.dot_general(down, moved, (((0,), (0,)), ((), ())), preferred_element_type=jnp.float32)
        above = jnp.sum(above, axis=1, keepdims=True) + float(c * stride * ROWS)
        filled = filled + jnp.where(chan == float(c), here + above, 0.0)
        total = jnp.sum(jnp.sum(own, axis=0, keepdims=True), axis=1, keepdims=True)
        totals = totals + jnp.where(lane == c, total, 0.0)
    for start in range(0, per_dest, SKIP):
        inside = (lane >= start) & (lane < start + SKIP)
        total = jnp.sum(jnp.where(inside, count, 0.0), axis=1, keepdims=True)
        totals = totals + jnp.where(lane == share + start // SKIP, total, 0.0)
    filled = filled.astype(jnp.int32)
    begin = begin.astype(jnp.int32)
    base = lax.broadcasted_iota(jnp.int32, chan.shape, 0) * rows
    group = jnp.minimum(begin >> 7, size - 1)
    table = totals.astype(jnp.int32)
    for values in ((filled >> 7) * 8, (filled - begin) & (ROWS - 1), begin & (ROWS - 1), base + group * FIELDS):
        table = jnp.where(lane < per_dest, values, pltpu.roll(table, per_dest, 1))
    plan[...] = table


def add_emitters(size, first, per_dest, chan, end, got, acc, streams, todo, plan, moves, sem, ready=()):
    source_count = chan.shape[0]
    share = acc.shape[0]
    stride = streams.shape[0] // (8 * share)
    lane = lax.broadcasted_iota(jnp.int32, (FIELDS, ROWS), 1)
    plan_moves(size, first, per_dest, share, stride, (got.shape[0] - 8) // source_count, chan, end, plan)
    copy = pltpu.make_async_copy(plan, moves, sem)
    copy.start()
    copy.wait()
    for other in ready:
        other.wait()

    def move(source, places):
        for place in places:
            row, begin, turn, target = (moves[source, k * per_dest + place] for k in range(4))
            target = pl.multiple_of(target, 8)
            here = got[pl.ds(row, FIELDS), :]
            there = got[pl.ds(row + FIELDS, FIELDS), :]
            filled = (jnp.full(lane.shape, begin, jnp.int32) + turn) & (ROWS - 1)
            whole = pltpu.roll(jnp.where(lane >= begin, here, there), turn, 1)
            pltpu.store(streams.at[pl.ds(target, FIELDS), :], whole, mask=lane >= filled)
            streams[pl.ds(target + 8, FIELDS), :] = whole

    def append(source, carry):
        if first == 0:
            move(source, range(per_dest))
        for start in range(0, 0 if first == 0 else per_dest, SKIP):
            places = range(start, min(start + SKIP, per_dest))
            live = moves[source, 4 * per_dest + share + start // SKIP]
            pl.when(live > 0)(functools.partial(move, source, places))
        return carry

    lax.fori_loop(0, source_count, append, 0)

    def list_chan(chan, count):
        total = moves[0, 4 * per_dest + chan]

        def list_pair(pair, at):
            todo[0, at] = chan
            todo[1, at] = chan * stride + 2 * pair
            todo[2, at] = total - 2 * ROWS * pair
            return at + 1

        return lax.fori_loop(0, (total + 2 * ROWS - 1) >> 8, list_pair, count)

    pair_count = lax.fori_loop(0, share, list_chan, 0)
    for extra in range(UNROLL - 1):
        todo[0, pair_count + extra] = 0
        todo[1, pair_count + extra] = 0
        todo[2, pair_count + extra] = 0

    place16 = lax.broadcasted_iota(jnp.int32, (SIDE, ROWS), 0).astype(jnp.float32)
    place8 = lax.broadcasted_iota(jnp.int32, (8, ROWS), 0).astype(jnp.float32) + 0.5

    def hat(cell, frac):
        apart = place16 - cell
        return jnp.where(apart == 0.0, 1.0 - frac, jnp.where(apart == 1.0, frac, 0.0))

    def factors(group, left):
        props = jnp.where(lane < left, streams[pl.ds(pl.multiple_of(group * 8, 8), FIELDS), :], 0.0)
        cell, frac_x, frac_y, center, decay, bright = (props[f : f + 1, :] for f in range(FIELDS))
        cell_x = jnp.floor(cell * (1.0 / SIDE))
        weight_x = hat(cell_x, frac_x)
        weight_y = hat(cell - SIDE * cell_x, frac_y)
        spread = jnp.concatenate(
            [(weight_x[x : x + 1, :] * weight_y).astype(jnp.bfloat16) for x in range(SIDE)], axis=0
        )
        apart = place8 - center
        profile = [jnp.exp2(jnp.square(apart + 8.0 * i) * decay) for i in range(CB // 8)]
        total = profile[0]
        for part in profile[1:]:
            total = total + part
        scale = bright / jnp.sum(total, axis=0, keepdims=True)
        line = jnp.concatenate(profile, axis=0) * scale
        return spread, line.astype(jnp.bfloat16)

    def some_pairs(turn, carry):
        for step in range(UNROLL):
            at = turn * UNROLL + step
            chan, group, left = todo[0, at], todo[1, at], todo[2, at]
            spread_0, line_0 = factors(group, left)
            spread_1, line_1 = factors(group + 1, left - ROWS)
            acc[chan] += lax.dot_general(
                jnp.concatenate([spread_0, spread_1], axis=1),
                jnp.concatenate([line_0, line_1], axis=1),
                (((1,), (1,)), ((), ())),
                preferred_element_type=jnp.float32,
            )
        return carry

    lax.fori_loop(0, (pair_count + UNROLL - 1) // UNROLL, some_pairs, 0)


def fetch(got_ref, got, sem):
    copy = pltpu.make_async_copy(got_ref, got.at[pl.ds(0, got_ref.shape[0])], sem)
    copy.start()
    return copy


def first_kernel(size, per_dest, share, got_ref, acc, chan_ref, end_ref, got, got_sem, *scratch):
    copy = fetch(got_ref, got, got_sem)
    acc[...] = jnp.zeros_like(acc)
    sources = scratch[-2].shape[0]
    rows = got_ref.shape[0] // sources
    copy.wait()
    chan = got[pl.ds(size * FIELDS, sources, stride=rows), :]
    end = got[pl.ds(size * FIELDS + 1, sources, stride=rows), :]
    chan_ref[...] = chan
    end_ref[...] = end
    add_emitters(size, 0, per_dest, chan, end, got, acc, *scratch)


def more_kernel(size, first, per_dest, chan_ref, end_ref, got_ref, held_ref, acc, got, got_sem, *scratch):
    copy = fetch(got_ref, got, got_sem)
    acc[...] = held_ref[...]
    copy.wait()
    add_emitters(size, first, per_dest, chan_ref[...], end_ref[...], got, acc, *scratch)


def last_kernel(size, first, per_dest, chan_ref, end_ref, width_ref, got_ref, held_ref, cube, near_ref, far_ref,
                acc, held_sem, got, got_sem, *scratch):
    held = pltpu.make_async_copy(held_ref, acc, held_sem)
    held.start()
    copy = fetch(got_ref, got, got_sem)
    add_emitters(size, first, per_dest, chan_ref[...], end_ref[...], got, acc, *scratch, ready=(copy, held))
    share = acc.shape[0]

    def one_chan(chan, carry):
        columns = pl.ds(pl.multiple_of(chan * CB, CB), CB)
        smooth(acc.at[chan], width_ref[:, columns], cube, columns)
        return carry

    lax.fori_loop(0, share, one_chan, 0)
    even = lax.rem(lax.axis_index("slab"), 2) == 0
    head = cube[:, :CB].T[:EDGE]
    tail = cube[:, (share - 1) * CB :].T[CB - EDGE :]
    near_ref[...] = jnp.where(even, tail, head)
    far_ref[...] = jnp.where(even, head, tail)


def smooth(plane_ref, widths, cube_ref, columns):
    decay = (-0.5 * LOG2E) / jnp.square(widths)
    places = lax.broadcasted_iota(jnp.int32, (SIDE, CB), 0).astype(jnp.float32)
    beam = [jnp.exp2(jnp.square(places - float(v)) * decay) for v in range(SIDE)]
    norm = beam[0]
    for v in range(1, SIDE):
        norm = norm + beam[v]
    inverse = 1.0 / norm
    beam = [b * inverse for b in beam]
    half = SIDE // 2
    even, odd = [None] * half, [None] * half
    for v in range(half):
        low = plane_ref[v * SIDE : (v + 1) * SIDE, :]
        high = plane_ref[(SIDE - 1 - v) * SIDE : (SIDE - v) * SIDE, :]
        both, apart = low + high, low - high
        near, far = beam[v][:half], beam[SIDE - 1 - v][:half]
        mean, rest = 0.5 * (near + far), 0.5 * (near - far)
        for x in range(half):
            term_even, term_odd = mean[x : x + 1, :] * both, rest[x : x + 1, :] * apart
            even[x] = term_even if v == 0 else even[x] + term_even
            odd[x] = term_odd if v == 0 else odd[x] + term_odd
    for x in range(SIDE):
        along_x = even[x] + odd[x] if x < half else even[SIDE - 1 - x] - odd[SIDE - 1 - x]
        total = None
        for v in range(SIDE):
            term = beam[v] * along_x[v : v + 1, :]
            total = term if v == 0 else total + term
        cube_ref[x * SIDE : (x + 1) * SIDE, columns] = total


def emitter_scratch(size, got, share):
    sources, rows = got.shape[:2]
    work = size * sources
    return [
        pltpu.VMEM((sources * rows + 8, ROWS), jnp.float32),
        pltpu.SemaphoreType.DMA,
        pltpu.VMEM((share * (work + 2) * 8, ROWS), jnp.float32),
        pltpu.SMEM((3, work // 2 + share + UNROLL), jnp.int32),
        pltpu.VMEM((sources, ROWS), jnp.int32),
        pltpu.SMEM((sources, ROWS), jnp.int32),
        pltpu.SemaphoreType.DMA,
    ]


def flat(got):
    return pltpu.with_memory_space_constraint(got.reshape(-1, ROWS), pltpu.VMEM)


def emitter_cost(size, got):
    work = size * got.shape[0]
    return pl.CostEstimate(
        flops=work * 2 * PIX * CB * ROWS, transcendentals=work * CB * ROWS, bytes_accessed=got.size * 4
    )


def deposit_first(size, per_dest, share, got):
    return pl.pallas_call(
        functools.partial(first_kernel, size, per_dest, share),
        out_shape=[jax.ShapeDtypeStruct((share, PIX, CB), jnp.float32)]
        + [jax.ShapeDtypeStruct((got.shape[0], ROWS), jnp.float32)] * 2,
        in_specs=[ANY],
        out_specs=[VMEM] * 3,
        scratch_shapes=emitter_scratch(size, got, share),
        cost_estimate=emitter_cost(size, got),
        name="deposit_first",
    )(flat(got))


def deposit_more(size, first, per_dest, share, chan, end, got, held):
    return pl.pallas_call(
        functools.partial(more_kernel, size, first, per_dest),
        out_shape=jax.ShapeDtypeStruct((share, PIX, CB), jnp.float32),
        in_specs=[VMEM, VMEM, ANY, VMEM],
        out_specs=VMEM,
        scratch_shapes=emitter_scratch(size, got, share),
        input_output_aliases={3: 0},
        name="deposit_more",
    )(chan, end, flat(got), held)


def deposit_last(size, first, per_dest, share, chan, end, got, held, widths):
    edge = jax.ShapeDtypeStruct((EDGE, PIX), jnp.float32)
    return pl.pallas_call(
        functools.partial(last_kernel, size, first, per_dest),
        out_shape=[pltpu.VMEM((PIX, share * CB), jnp.float32), edge, edge],
        in_specs=[VMEM] * 3 + [ANY] * 2,
        out_specs=[VMEM] * 3,
        scratch_shapes=[
            pltpu.VMEM((share, PIX, CB), jnp.float32),
            pltpu.SemaphoreType.DMA,
        ]
        + emitter_scratch(size, got, share),
        cost_estimate=emitter_cost(size, got),
        name="deposit_last",
    )(chan, end, widths.reshape(1, -1), flat(got), held)


def split(values):
    high = values.astype(jnp.bfloat16)
    return high, (values - high.astype(jnp.float32)).astype(jnp.bfloat16)


def times(left, right, dims):
    (left_high, left_low), (right_high, right_low) = left, right

    def dot(a, b):
        return lax.dot_general(a, b, (dims, ((), ())), preferred_element_type=jnp.float32)

    return dot(left_high, right_high) + (dot(left_high, right_low) + dot(left_low, right_high))


def band_part(taps_ref, first, rows):
    shape = (rows, CB)
    apart = lax.broadcasted_iota(jnp.int32, shape, 0) - lax.broadcasted_iota(jnp.int32, shape, 1) + (first + HALF)
    band = jnp.zeros(shape, jnp.float32)
    for k in range(TAPS):
        band = jnp.where(apart == k, taps_ref[k], band)
    return split(band)


def taps_kernel(wide, taps_ref, cube_ref, near_ref, far_ref, out_ref, out, high_ref, low_ref, sems):
    slab, last = lax.axis_index("slab"), lax.axis_size("slab") - 1
    even = lax.rem(slab, 2) == 0
    for ref, part in zip((high_ref, low_ref), band_part(taps_ref, -CB, 3 * CB)):
        ref[...] = jnp.zeros_like(ref)
        for i in range(0, wide, CB):
            ref[i : i + 3 * CB, i : i + CB] = part
    end = cube_ref.shape[1]
    copies = []
    for start in range(0, end, wide):
        low, high = max(start - CB, 0), min(start + wide + CB, end)
        rows, columns = slice(low - start + CB, high - start + CB), slice(start, start + wide)
        out[:, columns] = times(split(cube_ref[:, low:high]), (high_ref[rows], low_ref[rows]), ((1,), (0,)))
        if start == 0:
            edge = jnp.where(slab > 0, jnp.where(even, far_ref[...], near_ref[...]), 0.0)
            out[:, :CB] += times(split(edge), band_part(taps_ref, -EDGE, EDGE), ((0,), (0,)))
        if start + wide == end:
            edge = jnp.where(slab < last, jnp.where(even, near_ref[...], far_ref[...]), 0.0)
            out[:, end - CB :] += times(split(edge), band_part(taps_ref, CB, EDGE), ((0,), (0,)))
        copies.append(pltpu.make_async_copy(out.at[:, columns], out_ref.at[:, columns], sems.at[start // wide]))
        copies[-1].start()
    for copy in copies:
        copy.wait()


def sum_taps(taps, cube, near, far):
    wide = 2 * CB if cube.shape[1] % (2 * CB) == 0 else CB
    cube, near, far = (pltpu.with_memory_space_constraint(x, pltpu.VMEM) for x in (cube, near, far))
    return pl.pallas_call(
        functools.partial(taps_kernel, wide),
        out_shape=jax.ShapeDtypeStruct(cube.shape, jnp.float32),
        in_specs=[SMEM, VMEM, VMEM, VMEM],
        out_specs=ANY,
        scratch_shapes=[pltpu.VMEM(cube.shape, jnp.float32)]
        + [pltpu.VMEM((wide + 2 * CB, wide), jnp.bfloat16)] * 2
        + [pltpu.SemaphoreType.DMA((cube.shape[1] // wide,))],
        name="taps",
    )(taps, cube, near, far)


def body(
    voxel_cell,
    offsets,
    line_center,
    line_width,
    luminosity,
    block_rows,
    block_chan,
    slot_table,
    beam_width,
    spectral_taps,
):
    slab_count = lax.axis_size("slab")
    dest_count = lax.axis_size("tile") * slab_count
    per_dest = slot_table.shape[1] // dest_count
    share = NCB // slab_count
    sizes = chunk_sizes(per_dest)

    def packed(wanted):
        return pack(
            sizes, wanted, dest_count, slab_count, share, slot_table, block_rows, block_chan,
            voxel_cell, offsets, line_center, line_width, luminosity,
        )

    sent = packed((0, 1))
    def exchange(piece):
        return lax.all_to_all(piece, ("tile", "slab"), split_axis=0, concat_axis=0, tiled=True)

    got_first = exchange(sent[0])
    got_first, last_piece = lax.optimization_barrier((got_first, sent[1]))
    got_last = exchange(last_piece)
    held, chan, end = deposit_first(sizes[0], per_dest, share, got_first)
    reach = sizes[0] + sizes[1]
    if len(sizes) > 2:
        longest = jnp.max(chan[:, ROWS - 1])
        held, got_last = lax.optimization_barrier((held, got_last))
        held = lax.cond(
            longest > float(reach * ROWS),
            lambda held: deposit_more(sizes[2], reach, per_dest, share, chan, end, exchange(packed((2,))[0]), held),
            lambda held: held,
            held,
        )
    cube, near, far = deposit_last(
        sizes[1], sizes[0], per_dest, share, chan, end, got_last, held, beam_width
    )
    near = lax.ppermute(near, "slab", [(i, i ^ 1) for i in range(slab_count)])
    far = lax.ppermute(far, "slab", [(i, (i + 1 if i % 2 else i - 1) % slab_count) for i in range(slab_count)])
    return sum_taps(spectral_taps, cube, near, far)[None]


def solution(mesh):
    placed = (
        P(("tile", "slab"), None),
        P(("tile", "slab"), None, None),
        P(("tile", "slab"), None),
        P(("tile", "slab"), None),
        P(("tile", "slab"), None),
        P(("tile", "slab")),
        P(("tile", "slab")),
        P(("tile", "slab"), None),
        P("slab"),
        P(),
    )
    return jax.shard_map(
        body, mesh=mesh, in_specs=placed, out_specs=P("tile", None, "slab"), check_vma=False
    )
```

```python
import functools
import math

import jax
import jax.numpy as jnp
from jax import lax
from jax.experimental import pallas as pl
from jax.experimental.pallas import tpu as pltpu
from jax.sharding import PartitionSpec as P

SIDE = 16
PIX = SIDE * SIDE
CB = 128
ROWS = 128
TAPS = 31
HALF = 15
EDGE = 16
NCB = 32
FIELDS = 6
UNROLL = 8
SKIP = 8
AHEAD = 8
LOG2E = math.log2(math.e)
SMEM = pl.BlockSpec(memory_space=pltpu.SMEM)
VMEM = pl.BlockSpec(memory_space=pltpu.VMEM)
ANY = pl.BlockSpec(memory_space=pl.ANY)


def chunk_sizes(per_dest):
    early = late = max(per_dest * 9 // 24, 1)
    sizes = [early, late, per_dest - early - late]
    return [size for size in sizes if size > 0]


def padded_rows(rows):
    return -(-rows // 8) * 8


def pack_kernel(sizes, wanted, slab_count, share, slot_ref, count_ref, chan_ref, *refs):
    inputs, refs = refs[:5], refs[5:]
    sent, refs = refs[: len(wanted)], refs[len(wanted) :]
    staged, refs = refs[: len(wanted)], refs[len(wanted) :]
    props, *streams, slots, counts, chans, plan, moves, sem = refs[: 7 + AHEAD]
    refs = refs[7 + AHEAD :]
    (cell_ref, offset_ref, center_ref, width_ref, lum_ref), in_sem = refs[:5], refs[5]
    out_sems = refs[6:]
    outs = dict(zip(wanted, staged))
    fetches = [pltpu.make_async_copy(a, b, in_sem.at[i]) for i, (a, b) in enumerate(zip(inputs, refs[:5]))]
    for fetch_in in fetches:
        fetch_in.start()
    dest_count = slots.shape[0]
    per_dest = sum(sizes)
    block_total = cell_ref.shape[0]
    lane = lax.broadcasted_iota(jnp.int32, (dest_count, ROWS), 1)

    slot_row = slot_ref[...]
    blocks = lax.broadcasted_iota(jnp.int32, (block_total, slot_row.shape[1]), 0)
    chosen = jnp.where(blocks == slot_row, 1.0, 0.0).astype(jnp.bfloat16)
    table = jnp.concatenate([count_ref[...].reshape(1, -1), chan_ref[...].reshape(1, -1)], axis=0).astype(jnp.float32).astype(jnp.bfloat16)
    looked = jnp.dot(table, chosen, preferred_element_type=jnp.float32)
    slots[...] = jnp.zeros_like(slots)
    counts[...] = jnp.zeros_like(counts)
    chans[...] = jnp.zeros_like(chans)
    for dest in range(dest_count):
        columns = slice(dest * per_dest, (dest + 1) * per_dest)
        slots[dest : dest + 1, :per_dest] = slot_row[:, columns]
        counts[dest : dest + 1, :per_dest] = looked[0:1, columns]
        chans[dest : dest + 1, :per_dest] = looked[1:2, columns]
    count = counts[...]
    until = jnp.dot(count.astype(jnp.bfloat16), exclusive(ROWS), preferred_element_type=jnp.float32)
    end = until + count
    start = until.astype(jnp.int32)
    orders = jnp.zeros(lane.shape, jnp.int32)
    for values in ((start >> 7) * 8, start & (ROWS - 1), jnp.maximum(slots[...], 0) * 8):
        orders = jnp.where(lane < per_dest, values, pltpu.roll(orders, per_dest, 1))
    plan[...] = orders
    copy = pltpu.make_async_copy(plan, moves, sem)
    copy.start()

    if 0 in outs:
        rows = outs[0].shape[0] // dest_count
        dests = lax.broadcasted_iota(jnp.int32, lane.shape, 0)
        chan = chans[...] - (lax.rem(dests, slab_count) * share).astype(jnp.float32)
        longest = jnp.max(jnp.max(end, axis=0, keepdims=True), axis=1, keepdims=True)
        meta = sizes[0] * FIELDS
        outs[0][pl.ds(meta, dest_count, stride=rows), :] = jnp.where(lane == ROWS - 1, longest, chan)
        outs[0][pl.ds(meta + 1, dest_count, stride=rows), :] = end

    def gather_fields(tile, carry):
        first = pl.multiple_of(tile * 8, 8)
        here = pl.ds(first, 8)
        fields = (
            cell_ref[here, :].astype(jnp.float32),
            offset_ref[pl.ds(2 * first, 8, stride=2), :],
            offset_ref[pl.ds(2 * first + 1, 8, stride=2), :],
            center_ref[here, :],
            (-0.5 * LOG2E) / jnp.square(width_ref[here, :]),
            lum_ref[here, :].astype(jnp.bfloat16).astype(jnp.float32),
        )
        for field, values in enumerate(fields):
            props[pl.ds(8 * first + field, 8, stride=8), :] = values
        return carry

    for fetch_in in fetches:
        fetch_in.wait()
    lax.fori_loop(0, block_total // 8, gather_fields, 0, unroll=2)
    copy.wait()

    def send(dest):
        for out, whole, out_sem in zip(staged, sent, out_sems):
            rows = out.shape[0] // dest_count
            here = pl.ds(pl.multiple_of(dest * rows, 8), rows)
            pltpu.make_async_copy(out.at[here], whole.at[here], out_sem).start()

    lanes = lax.broadcasted_iota(jnp.int32, (8, ROWS), 1)

    def some_dests(turn, carry):
        first = turn * len(streams)
        for back in range(len(streams)):
            pl.when(turn > 0)(functools.partial(send, first - 1 - back))
        for slot in range(per_dest):
            for ahead, stream in enumerate(streams):
                row, shift, target = (moves[first + ahead, k * per_dest + slot] for k in range(3))
                row, target = pl.multiple_of(row, 8), pl.multiple_of(target, 8)
                turned = pltpu.roll(props[pl.ds(row, 8), :], shift, 1)
                pltpu.store(stream.at[pl.ds(target, 8), :], turned, mask=lanes >= shift)
                stream[pl.ds(target + 8, 8), :] = turned
        for ahead, stream in enumerate(streams):
            group = 0
            for part, size in enumerate(sizes):
                if part in outs:
                    out = outs[part]
                    base = pl.multiple_of((first + ahead) * (out.shape[0] // dest_count), 8)
                    for place in range(size):
                        here = 8 * (group + place)
                        out[pl.ds(base + place * FIELDS, FIELDS), :] = stream[here : here + FIELDS, :]
                group += size
        return carry

    lax.fori_loop(0, dest_count // len(streams), some_dests, 0)
    for back in range(1, len(streams)):
        send(dest_count - 1 - back)
    send(dest_count - 1)
    for out, whole, out_sem in zip(staged, sent, out_sems):
        pltpu.make_async_copy(out, whole, out_sem).wait()


def pack(sizes, wanted, dest_count, slab_count, share, slot_list, counts, chans, cells, offsets, centers, widths, lums):
    rows = [padded_rows(size * FIELDS + (2 if part == 0 else 0)) for part, size in enumerate(sizes)]
    block_total = cells.shape[0]
    lists = (cells, offsets.reshape(block_total * 2, ROWS), centers, widths, lums)
    shapes = [(dest_count * rows[part], ROWS) for part in wanted]
    sent = pl.pallas_call(
        functools.partial(pack_kernel, sizes, wanted, slab_count, share),
        out_shape=[jax.ShapeDtypeStruct(shape, jnp.float32) for shape in shapes],
        in_specs=[VMEM] * 3 + [ANY] * 5,
        out_specs=[ANY] * len(wanted),
        scratch_shapes=[pltpu.VMEM(shape, jnp.float32) for shape in shapes]
        + [
            pltpu.VMEM((block_total * 8, ROWS), jnp.float32),
            *[pltpu.VMEM(((sum(sizes) + 2) * 8, ROWS), jnp.float32)] * AHEAD,
            pltpu.VMEM((dest_count, ROWS), jnp.int32),
            pltpu.VMEM((dest_count, ROWS), jnp.float32),
            pltpu.VMEM((dest_count, ROWS), jnp.float32),
            pltpu.VMEM((dest_count, ROWS), jnp.int32),
            pltpu.SMEM((dest_count, ROWS), jnp.int32),
            pltpu.SemaphoreType.DMA,
        ]
        + [pltpu.VMEM(values.shape, values.dtype) for values in lists]
        + [pltpu.SemaphoreType.DMA((5,))]
        + [pltpu.SemaphoreType.DMA] * len(wanted),
        name="pack",
    )(slot_list, counts, chans, *lists)
    return [piece.reshape(dest_count, rows[part], ROWS) for part, piece in zip(wanted, sent)]


def exclusive(size):
    before = lax.broadcasted_iota(jnp.int32, (size, size), 0)
    return (before < lax.broadcasted_iota(jnp.int32, (size, size), 1)).astype(jnp.bfloat16)


def plan_moves(size, first, per_dest, share, stride, rows, chan, end, plan):
    sources = chan.shape[0]
    lane = lax.broadcasted_iota(jnp.int32, chan.shape, 1)
    low, high = float(first * ROWS), float((first + size) * ROWS)
    start = jnp.where(lane == 0, 0.0, pltpu.roll(end, 1, 1))
    begin = jnp.clip(start, low, high) - low
    count = jnp.where(lane < per_dest, jnp.clip(end, low, high) - low - begin, 0.0)
    chan = jnp.where(count > 0.0, chan, 0.0)
    across = exclusive(ROWS)
    down = exclusive(sources)
    filled = jnp.zeros(chan.shape, jnp.float32)
    totals = jnp.zeros(chan.shape, jnp.float32)
    for c in range(share):
        own = jnp.where(chan == float(c), count, 0.0)
        moved = own.astype(jnp.bfloat16)
        here = jnp.dot(moved, across, preferred_element_type=jnp.float32)
        above = lax.dot_general(down, moved, (((0,), (0,)), ((), ())), preferred_element_type=jnp.float32)
        above = jnp.sum(above, axis=1, keepdims=True) + float(c * stride * ROWS)
        filled = filled + jnp.where(chan == float(c), here + above, 0.0)
        total = jnp.sum(jnp.sum(own, axis=0, keepdims=True), axis=1, keepdims=True)
        totals = totals + jnp.where(lane == c, total, 0.0)
    for start in range(0, per_dest, SKIP):
        inside = (lane >= start) & (lane < start + SKIP)
        total = jnp.sum(jnp.where(inside, count, 0.0), axis=1, keepdims=True)
        totals = totals + jnp.where(lane == share + start // SKIP, total, 0.0)
    filled = filled.astype(jnp.int32)
    begin = begin.astype(jnp.int32)
    base = lax.broadcasted_iota(jnp.int32, chan.shape, 0) * rows
    group = jnp.minimum(begin >> 7, size - 1)
    table = totals.astype(jnp.int32)
    for values in ((filled >> 7) * 8, (filled - begin) & (ROWS - 1), begin & (ROWS - 1), base + group * FIELDS):
        table = jnp.where(lane < per_dest, values, pltpu.roll(table, per_dest, 1))
    plan[...] = table


def add_emitters(size, first, per_dest, chan, end, got, acc, streams, todo, plan, moves, sem, ready=()):
    source_count = chan.shape[0]
    share = acc.shape[0]
    stride = streams.shape[0] // (8 * share)
    lane = lax.broadcasted_iota(jnp.int32, (FIELDS, ROWS), 1)
    plan_moves(size, first, per_dest, share, stride, (got.shape[0] - 8) // source_count, chan, end, plan)
    copy = pltpu.make_async_copy(plan, moves, sem)
    copy.start()
    copy.wait()
    for other in ready:
        other.wait()

    def move(source, places):
        for place in places:
            row, begin, turn, target = (moves[source, k * per_dest + place] for k in range(4))
            target = pl.multiple_of(target, 8)
            here = got[pl.ds(row, FIELDS), :]
            there = got[pl.ds(row + FIELDS, FIELDS), :]
            filled = (jnp.full(lane.shape, begin, jnp.int32) + turn) & (ROWS - 1)
            whole = pltpu.roll(jnp.where(lane >= begin, here, there), turn, 1)
            pltpu.store(streams.at[pl.ds(target, FIELDS), :], whole, mask=lane >= filled)
            streams[pl.ds(target + 8, FIELDS), :] = whole

    def append(source, carry):
        if first == 0:
            move(source, range(per_dest))
        for start in range(0, 0 if first == 0 else per_dest, SKIP):
            places = range(start, min(start + SKIP, per_dest))
            live = moves[source, 4 * per_dest + share + start // SKIP]
            pl.when(live > 0)(functools.partial(move, source, places))
        return carry

    lax.fori_loop(0, source_count, append, 0)

    def list_chan(chan, count):
        total = moves[0, 4 * per_dest + chan]

        def list_pair(pair, at):
            todo[0, at] = chan
            todo[1, at] = chan * stride + 2 * pair
            todo[2, at] = total - 2 * ROWS * pair
            return at + 1

        return lax.fori_loop(0, (total + 2 * ROWS - 1) >> 8, list_pair, count)

    pair_count = lax.fori_loop(0, share, list_chan, 0)
    for extra in range(UNROLL - 1):
        todo[0, pair_count + extra] = 0
        todo[1, pair_count + extra] = 0
        todo[2, pair_count + extra] = 0

    place16 = lax.broadcasted_iota(jnp.int32, (SIDE, ROWS), 0).astype(jnp.float32)
    place8 = lax.broadcasted_iota(jnp.int32, (8, ROWS), 0).astype(jnp.float32) + 0.5

    def hat(cell, frac):
        apart = place16 - cell
        return jnp.where(apart == 0.0, 1.0 - frac, jnp.where(apart == 1.0, frac, 0.0))

    def factors(group, left):
        props = jnp.where(lane < left, streams[pl.ds(pl.multiple_of(group * 8, 8), FIELDS), :], 0.0)
        cell, frac_x, frac_y, center, decay, bright = (props[f : f + 1, :] for f in range(FIELDS))
        cell_x = jnp.floor(cell * (1.0 / SIDE))
        weight_x = hat(cell_x, frac_x)
        weight_y = hat(cell - SIDE * cell_x, frac_y)
        spread = jnp.concatenate(
            [(weight_x[x : x + 1, :] * weight_y).astype(jnp.bfloat16) for x in range(SIDE)], axis=0
        )
        apart = place8 - center
        profile = [jnp.exp2(jnp.square(apart + 8.0 * i) * decay) for i in range(CB // 8)]
        total = profile[0]
        for part in profile[1:]:
            total = total + part
        scale = bright / jnp.sum(total, axis=0, keepdims=True)
        line = jnp.concatenate(profile, axis=0) * scale
        return spread, line.astype(jnp.bfloat16)

    def some_pairs(turn, carry):
        for step in range(UNROLL):
            at = turn * UNROLL + step
            chan, group, left = todo[0, at], todo[1, at], todo[2, at]
            spread_0, line_0 = factors(group, left)
            spread_1, line_1 = factors(group + 1, left - ROWS)
            acc[chan] += lax.dot_general(
                jnp.concatenate([spread_0, spread_1], axis=1),
                jnp.concatenate([line_0, line_1], axis=1),
                (((1,), (1,)), ((), ())),
                preferred_element_type=jnp.float32,
            )
        return carry

    lax.fori_loop(0, (pair_count + UNROLL - 1) // UNROLL, some_pairs, 0)


def fetch(got_ref, got, sem):
    copy = pltpu.make_async_copy(got_ref, got.at[pl.ds(0, got_ref.shape[0])], sem)
    copy.start()
    return copy


def first_kernel(size, per_dest, share, got_ref, acc, chan_ref, end_ref, got, got_sem, *scratch):
    copy = fetch(got_ref, got, got_sem)
    acc[...] = jnp.zeros_like(acc)
    sources = scratch[-2].shape[0]
    rows = got_ref.shape[0] // sources
    copy.wait()
    chan = got[pl.ds(size * FIELDS, sources, stride=rows), :]
    end = got[pl.ds(size * FIELDS + 1, sources, stride=rows), :]
    chan_ref[...] = chan
    end_ref[...] = end
    add_emitters(size, 0, per_dest, chan, end, got, acc, *scratch)


def more_kernel(size, first, per_dest, chan_ref, end_ref, got_ref, held_ref, acc, got, got_sem, *scratch):
    copy = fetch(got_ref, got, got_sem)
    acc[...] = held_ref[...]
    copy.wait()
    add_emitters(size, first, per_dest, chan_ref[...], end_ref[...], got, acc, *scratch)


def last_kernel(size, first, per_dest, chan_ref, end_ref, width_ref, got_ref, held_ref, cube, near_ref, far_ref,
                acc, held_sem, got, got_sem, *scratch):
    held = pltpu.make_async_copy(held_ref, acc, held_sem)
    held.start()
    copy = fetch(got_ref, got, got_sem)
    add_emitters(size, first, per_dest, chan_ref[...], end_ref[...], got, acc, *scratch, ready=(copy, held))
    share = acc.shape[0]

    def one_chan(chan, carry):
        columns = pl.ds(pl.multiple_of(chan * CB, CB), CB)
        smooth(acc.at[chan], width_ref[:, columns], cube, columns)
        return carry

    lax.fori_loop(0, share, one_chan, 0)
    even = lax.rem(lax.axis_index("slab"), 2) == 0
    head = cube[:, :CB].T[:EDGE]
    tail = cube[:, (share - 1) * CB :].T[CB - EDGE :]
    near_ref[...] = jnp.where(even, tail, head)
    far_ref[...] = jnp.where(even, head, tail)


def smooth(plane_ref, widths, cube_ref, columns):
    decay = (-0.5 * LOG2E) / jnp.square(widths)
    places = lax.broadcasted_iota(jnp.int32, (SIDE, CB), 0).astype(jnp.float32)
    beam = [jnp.exp2(jnp.square(places - float(v)) * decay) for v in range(SIDE)]
    norm = beam[0]
    for v in range(1, SIDE):
        norm = norm + beam[v]
    inverse = 1.0 / norm
    beam = [b * inverse for b in beam]
    half = SIDE // 2
    even, odd = [None] * half, [None] * half
    for v in range(half):
        low = plane_ref[v * SIDE : (v + 1) * SIDE, :]
        high = plane_ref[(SIDE - 1 - v) * SIDE : (SIDE - v) * SIDE, :]
        both, apart = low + high, low - high
        near, far = beam[v][:half], beam[SIDE - 1 - v][:half]
        mean, rest = 0.5 * (near + far), 0.5 * (near - far)
        for x in range(half):
            term_even, term_odd = mean[x : x + 1, :] * both, rest[x : x + 1, :] * apart
            even[x] = term_even if v == 0 else even[x] + term_even
            odd[x] = term_odd if v == 0 else odd[x] + term_odd
    for x in range(SIDE):
        along_x = even[x] + odd[x] if x < half else even[SIDE - 1 - x] - odd[SIDE - 1 - x]
        total = None
        for v in range(SIDE):
            term = beam[v] * along_x[v : v + 1, :]
            total = term if v == 0 else total + term
        cube_ref[x * SIDE : (x + 1) * SIDE, columns] = total


def emitter_scratch(size, got, share):
    sources, rows = got.shape[:2]
    work = size * sources
    return [
        pltpu.VMEM((sources * rows + 8, ROWS), jnp.float32),
        pltpu.SemaphoreType.DMA,
        pltpu.VMEM((share * (work + 2) * 8, ROWS), jnp.float32),
        pltpu.SMEM((3, work // 2 + share + UNROLL), jnp.int32),
        pltpu.VMEM((sources, ROWS), jnp.int32),
        pltpu.SMEM((sources, ROWS), jnp.int32),
        pltpu.SemaphoreType.DMA,
    ]


def flat(got):
    return pltpu.with_memory_space_constraint(got.reshape(-1, ROWS), pltpu.VMEM)


def emitter_cost(size, got):
    work = size * got.shape[0]
    return pl.CostEstimate(
        flops=work * 2 * PIX * CB * ROWS, transcendentals=work * CB * ROWS, bytes_accessed=got.size * 4
    )


def deposit_first(size, per_dest, share, got):
    return pl.pallas_call(
        functools.partial(first_kernel, size, per_dest, share),
        out_shape=[jax.ShapeDtypeStruct((share, PIX, CB), jnp.float32)]
        + [jax.ShapeDtypeStruct((got.shape[0], ROWS), jnp.float32)] * 2,
        in_specs=[ANY],
        out_specs=[VMEM] * 3,
        scratch_shapes=emitter_scratch(size, got, share),
        cost_estimate=emitter_cost(size, got),
        name="deposit_first",
    )(flat(got))


def deposit_more(size, first, per_dest, share, chan, end, got, held):
    return pl.pallas_call(
        functools.partial(more_kernel, size, first, per_dest),
        out_shape=jax.ShapeDtypeStruct((share, PIX, CB), jnp.float32),
        in_specs=[VMEM, VMEM, ANY, VMEM],
        out_specs=VMEM,
        scratch_shapes=emitter_scratch(size, got, share),
        input_output_aliases={3: 0},
        name="deposit_more",
    )(chan, end, flat(got), held)


def deposit_last(size, first, per_dest, share, chan, end, got, held, widths):
    edge = jax.ShapeDtypeStruct((EDGE, PIX), jnp.float32)
    return pl.pallas_call(
        functools.partial(last_kernel, size, first, per_dest),
        out_shape=[pltpu.VMEM((PIX, share * CB), jnp.float32), edge, edge],
        in_specs=[VMEM] * 3 + [ANY] * 2,
        out_specs=[VMEM] * 3,
        scratch_shapes=[
            pltpu.VMEM((share, PIX, CB), jnp.float32),
            pltpu.SemaphoreType.DMA,
        ]
        + emitter_scratch(size, got, share),
        cost_estimate=emitter_cost(size, got),
        name="deposit_last",
    )(chan, end, widths.reshape(1, -1), flat(got), held)


def split(values):
    high = values.astype(jnp.bfloat16)
    return high, (values - high.astype(jnp.float32)).astype(jnp.bfloat16)


def times(left, right, dims):
    (left_high, left_low), (right_high, right_low) = left, right

    def dot(a, b):
        return lax.dot_general(a, b, (dims, ((), ())), preferred_element_type=jnp.float32)

    return dot(left_high, right_high) + (dot(left_high, right_low) + dot(left_low, right_high))


def band_part(taps_ref, first, rows):
    shape = (rows, CB)
    apart = lax.broadcasted_iota(jnp.int32, shape, 0) - lax.broadcasted_iota(jnp.int32, shape, 1) + (first + HALF)
    band = jnp.zeros(shape, jnp.float32)
    for k in range(TAPS):
        band = jnp.where(apart == k, taps_ref[k], band)
    return split(band)


def taps_kernel(wide, taps_ref, cube_ref, near_ref, far_ref, out_ref, out, high_ref, low_ref, sems):
    slab, last = lax.axis_index("slab"), lax.axis_size("slab") - 1
    even = lax.rem(slab, 2) == 0
    for ref, part in zip((high_ref, low_ref), band_part(taps_ref, -CB, 3 * CB)):
        ref[...] = jnp.zeros_like(ref)
        for i in range(0, wide, CB):
            ref[i : i + 3 * CB, i : i + CB] = part
    end = cube_ref.shape[1]
    copies = []
    for start in range(0, end, wide):
        low, high = max(start - CB, 0), min(start + wide + CB, end)
        rows, columns = slice(low - start + CB, high - start + CB), slice(start, start + wide)
        out[:, columns] = times(split(cube_ref[:, low:high]), (high_ref[rows], low_ref[rows]), ((1,), (0,)))
        if start == 0:
            edge = jnp.where(slab > 0, jnp.where(even, far_ref[...], near_ref[...]), 0.0)
            out[:, :CB] += times(split(edge), band_part(taps_ref, -EDGE, EDGE), ((0,), (0,)))
        if start + wide == end:
            edge = jnp.where(slab < last, jnp.where(even, near_ref[...], far_ref[...]), 0.0)
            out[:, end - CB :] += times(split(edge), band_part(taps_ref, CB, EDGE), ((0,), (0,)))
        copies.append(pltpu.make_async_copy(out.at[:, columns], out_ref.at[:, columns], sems.at[start // wide]))
        copies[-1].start()
    for copy in copies:
        copy.wait()


def sum_taps(taps, cube, near, far):
    wide = 2 * CB if cube.shape[1] % (2 * CB) == 0 else CB
    cube, near, far = (pltpu.with_memory_space_constraint(x, pltpu.VMEM) for x in (cube, near, far))
    return pl.pallas_call(
        functools.partial(taps_kernel, wide),
        out_shape=jax.ShapeDtypeStruct(cube.shape, jnp.float32),
        in_specs=[SMEM, VMEM, VMEM, VMEM],
        out_specs=ANY,
        scratch_shapes=[pltpu.VMEM(cube.shape, jnp.float32)]
        + [pltpu.VMEM((wide + 2 * CB, wide), jnp.bfloat16)] * 2
        + [pltpu.SemaphoreType.DMA((cube.shape[1] // wide,))],
        name="taps",
    )(taps, cube, near, far)


def body(
    voxel_cell,
    offsets,
    line_center,
    line_width,
    luminosity,
    block_rows,
    block_chan,
    slot_table,
    beam_width,
    spectral_taps,
):
    slab_count = lax.axis_size("slab")
    dest_count = lax.axis_size("tile") * slab_count
    per_dest = slot_table.shape[1] // dest_count
    share = NCB // slab_count
    sizes = chunk_sizes(per_dest)

    def packed(wanted):
        return pack(
            sizes, wanted, dest_count, slab_count, share, slot_table, block_rows, block_chan,
            voxel_cell, offsets, line_center, line_width, luminosity,
        )

    sent = packed((0, 1))
    def exchange(piece):
        return lax.all_to_all(piece, ("tile", "slab"), split_axis=0, concat_axis=0, tiled=True)

    got_first = exchange(sent[0])
    got_first, last_piece = lax.optimization_barrier((got_first, sent[1]))
    got_last = exchange(last_piece)
    held, chan, end = deposit_first(sizes[0], per_dest, share, got_first)
    reach = sizes[0] + sizes[1]
    if len(sizes) > 2:
        longest = jnp.max(chan[:, ROWS - 1])
        held, got_last = lax.optimization_barrier((held, got_last))
        held = lax.cond(
            longest > float(reach * ROWS),
            lambda held: deposit_more(sizes[2], reach, per_dest, share, chan, end, exchange(packed((2,))[0]), held),
            lambda held: held,
            held,
        )
    cube, near, far = deposit_last(
        sizes[1], sizes[0], per_dest, share, chan, end, got_last, held, beam_width
    )
    near = lax.ppermute(near, "slab", [(i, i ^ 1) for i in range(slab_count)])
    far = lax.ppermute(far, "slab", [(i, (i + 1 if i % 2 else i - 1) % slab_count) for i in range(slab_count)])
    return sum_taps(spectral_taps, cube, near, far)[None]


def solution(mesh):
    placed = (
        P(("tile", "slab"), None),
        P(("tile", "slab"), None, None),
        P(("tile", "slab"), None),
        P(("tile", "slab"), None),
        P(("tile", "slab"), None),
        P(("tile", "slab")),
        P(("tile", "slab")),
        P(("tile", "slab"), None),
        P("slab"),
        P(),
    )
    return jax.shard_map(
        body, mesh=mesh, in_specs=placed, out_specs=P("tile", None, "slab"), check_vma=False
    )
```
